256 devices in a mesh: band: 16 (over z, y_lo), col: 16 (over x, y_hi, core).
Axes of the slice: x: 4, y: 4 (y_hi: 2, y_lo: 2; y = y_hi * 2 + y_lo), z: 8, core: 2. Of those that a mesh axis runs over, the one named last changes fastest.
Arguments:
- valence_wave: bfloat16 [16, 96, 9216], P('band', 'col'), may hold values from -6 to 6
- conduction_wave: bfloat16 [16, 96, 9216], P('band', 'col'), may hold values from -6 to 6
- valence_index: int32 [16], replicated, may hold values from 0 to 4095
- occupied_energy: float32 [4096], replicated, may hold values from -6 to -0.5
- conduction_energy: float32 [16], replicated, may hold values from 0.5 to 8
- frequency: float32 [4], replicated, may hold values from 0.5 to 16
- gvec_cell: int32 [32768], P('col'), may hold values from 0 to 55295, as said below
- block_cell: int32 [16], P('col'), may hold values from 0 to 55295, as said below
Outputs:
- chi: float32 [32768, 128], P(('col', 'band'))
The draws below stay inside these ranges and needn't reach their ends.
Inputs may be any that keep to these rules, and one draw needn't show every extreme that they name: `gvec_cell`: for rows j of owner k (k * 2048 <= j < (k + 1) * 2048) the entry is (kx 6 + ky - k * 6) * 96 + kz for the G vector's grid point (kx, ky, kz), whose ky lies in [k * 6, (k + 1) * 6); no point appears twice among the rows and block columns of one owner. `block_cell`: block column m has owner k = m // 1 and is encoded as for gvec_cell; its points differ from every row point of the same owner.
All inputs are finite; a program needn't handle non-finite values.
Results may differ from the reference program's by a relative error of at most 0.018.
Values may be sent and summed in bfloat16 or wider, within the bound.
No kernel may reach another device: no remote copies, remote signals or barrier semaphores. Data moves between devices by JAX's collectives and lax.ppermute only.
A program may use at most 128 MiB of HBM per device.

```python
import math
import jax
import jax.numpy as jnp
from jax import lax

GX = 96
GY = 96
GZ = 96
G_DEV = 2048
NV = 16
NW = 4
NOCC = 4096
GB = 16
NG = 32768
NC = 16
PENCIL = 55296
GB_DEV = 1


def cell_lists(key):
    owners = NG // G_DEV
    keys = jax.random.split(jax.random.fold_in(key, 7), owners)
    return jax.vmap(lambda single: jax.random.permutation(single, PENCIL))(keys)


def draw_gvec_cell(key, part):
    lists = cell_lists(key)
    return lists[:, :G_DEV].reshape(-1).astype(jnp.int32)


def draw_block_cell(key, part):
    lists = cell_lists(key)
    return lists[:, G_DEV:G_DEV + GB_DEV].reshape(-1).astype(jnp.int32)


def set_ends(values, stream_key, low, high):
    longest = values.shape.index(max(values.shape))
    spots = []
    for shift in (0, 1):
        where = [jax.random.randint(jax.random.fold_in(stream_key, axis), (), 0, length) for axis, length in enumerate(values.shape)]
        where[longest] = (where[longest] + shift) % values.shape[longest]
        spots.append(tuple(where))
    return values.at[spots[0]].set(low).at[spots[1]].set(high)


def shard_levels(rng, extent, cuts, smallest, largest):
    factor_of, own = 1.0, jax.random.fold_in(rng, 6)
    for dim, parts in cuts:
        steps = jnp.exp(jax.random.uniform(jax.random.fold_in(own, dim), (parts,), jnp.float32, smallest / len(cuts), largest / len(cuts)))
        factor_of = factor_of * jnp.repeat(steps, extent[dim] // parts).reshape([-1 if axis == dim else 1 for axis in range(len(extent))])
    return factor_of


def bell_draw(stream_key, shape, scale, bound, cuts=(), kind=jnp.bfloat16):
    entries = jax.random.normal(stream_key, shape, jnp.float32) * scale
    if len(cuts) > 0:
        entries = shard_levels(stream_key, shape, cuts, -0.22, 0.18) * entries
    return jnp.clip(entries, min=-bound, max=bound).astype(kind)


def setup_inputs(seed: int = 0) -> dict:
    streams_of = jax.random.split(jax.random.key(seed), 9)
    return {
        "valence_wave": bell_draw(streams_of[0], (NV, GX, GY * GZ), 1.0, 6.0, ((0, 16), (1, 16))),
        "conduction_wave": bell_draw(streams_of[1], (NC, GX, GY * GZ), 1.0, 6.0, ((0, 16), (1, 16))),
        "valence_index": set_ends(jax.random.randint(streams_of[2], (NV,), 0, NOCC), jax.random.fold_in(streams_of[2], 1), 0, NOCC - 1).astype(jnp.int32),
        "occupied_energy": jnp.clip(jax.random.uniform(streams_of[3], (NOCC,), jnp.float32, -6.0, -0.5), -6.0, -0.5),
        "conduction_energy": jnp.clip(jax.random.uniform(streams_of[4], (NC,), jnp.float32, 0.5, 8.0), 0.5, 8.0),
        "frequency": jnp.clip(jnp.exp(jax.random.uniform(streams_of[5], (NW,), jnp.float32, math.log(0.5), math.log(16.0))), 0.5, 16.0),
        "gvec_cell": draw_gvec_cell(jax.random.fold_in(streams_of[8], 71), 0),
        "block_cell": draw_block_cell(jax.random.fold_in(streams_of[8], 71), 0),
    }


HIGHEST = lax.Precision.HIGHEST

def dft_tables(length, factor, out_type):
    indices = jnp.arange(length, dtype=jnp.int32)
    phases = indices[:, None] * indices[None, :] % length
    angles = phases.astype(jnp.float32) * (2.0 * math.pi / length)
    return ((jnp.cos(angles) * factor).astype(out_type), (-jnp.sin(angles) * factor).astype(out_type))

def weighted_columns(block, weights):
    columns = block.astype(jnp.float32)
    stacked = jnp.stack([columns, jnp.stack([-columns[1], columns[0]])])
    scaled = stacked[None] * weights[:, None, None, :, None]
    scaled = scaled.transpose(2, 3, 0, 1, 4).astype(jnp.bfloat16)
    return scaled.reshape(2, block.shape[1], -1)

def reference(valence_wave, conduction_wave, valence_index, occupied_energy, conduction_energy, frequency, gvec_cell, block_cell):
    col_count = NG // G_DEV
    slab_y = GY // col_count

    def grid_points(cells, per_owner):
        owner = jnp.arange(cells.shape[0], dtype=jnp.int32) // per_owner
        point_x = cells // (slab_y * GZ)
        point_y = owner * slab_y + cells // GZ % slab_y
        point_z = cells % GZ
        return (point_x, point_y, point_z)
    row_points = grid_points(gvec_cell, G_DEV)
    block_points = grid_points(block_cell, GB // col_count)
    x_cosine, x_sine = dft_tables(GX, 1.0 / math.sqrt(GX), jnp.bfloat16)
    cosine_full = x_cosine.astype(jnp.float32)
    sine_full = x_sine.astype(jnp.float32)
    valence_float = valence_wave.astype(jnp.float32).reshape(NV, GX, GY, GZ)

    def one_band(wave):
        products = valence_float * wave.astype(jnp.float32).reshape(GX, GY, GZ)[None]
        plane = jnp.fft.fft2(products, axes=(2, 3)) / math.sqrt(GY * GZ)
        plane_real = lax.optimization_barrier(jnp.real(plane).astype(jnp.bfloat16)).astype(jnp.float32)
        plane_imag = lax.optimization_barrier(jnp.imag(plane).astype(jnp.bfloat16)).astype(jnp.float32)
        real_part = jnp.einsum('kx,vxyz->vkyz', cosine_full, plane_real, precision=HIGHEST) - jnp.einsum('kx,vxyz->vkyz', sine_full, plane_imag, precision=HIGHEST)
        imag_part = jnp.einsum('kx,vxyz->vkyz', sine_full, plane_real, precision=HIGHEST) + jnp.einsum('kx,vxyz->vkyz', cosine_full, plane_imag, precision=HIGHEST)
        density_real = real_part.astype(jnp.bfloat16)
        density_imag = imag_part.astype(jnp.bfloat16)
        rows = jnp.stack([density_real[:, row_points[0], row_points[1], row_points[2]], density_imag[:, row_points[0], row_points[1], row_points[2]]])
        block = jnp.stack([density_real[:, block_points[0], block_points[1], block_points[2]], density_imag[:, block_points[0], block_points[1], block_points[2]]])
        return (rows, block)
    rows, blocks = lax.map(one_band, conduction_wave)
    row_density = jnp.transpose(rows, (1, 0, 2, 3)).reshape(2, NC * NV, NG)
    block_density = jnp.transpose(blocks, (1, 0, 2, 3)).reshape(2, NC * NV, GB)
    valence_energy = occupied_energy[valence_index]
    gap = (conduction_energy[:, None] - valence_energy[None, :]).reshape(-1)
    freq_column = frequency[:, None]
    weights = -4.0 * gap[None, :] / (gap[None, :] * gap[None, :] + freq_column * freq_column) * (1.0 / math.sqrt(NV * NC))
    right_side = weighted_columns(block_density, weights).reshape(2 * NC * NV, -1)
    left_side = jnp.transpose(row_density, (2, 0, 1)).reshape(NG, 2 * NC * NV)
    return jnp.dot(left_side, right_side, preferred_element_type=jnp.float32)
```

```python
import functools
import math

import jax
import jax.numpy as jnp
import ml_dtypes
import numpy as np
from jax import lax
from jax.experimental import pallas as pl
from jax.experimental.pallas import tpu as pltpu
from jax.sharding import Mesh
from jax.sharding import PartitionSpec as P

BF16 = jnp.bfloat16
F32 = jnp.float32

N = 96
SLABS = 16
X6 = 6
Y6 = 6
Y16 = 16
K7 = 7
FLAT = K7 * N
WIDE = 768
ITEMS = 4
CHUNKS = 2
C_OF_CHUNK = ((0, 1), (3, 2))
G_DEV = 2048
NBLOCK = 16
TILE = 512

BAND = ("z1", "z0", "yl")
VGROUP = ("z0", "yl")
COL = ("x", "yh", "co")


def unit(phase, period):
    angle = 2.0 * np.pi * (np.asarray(phase) % period) / period
    return np.cos(angle), -np.sin(angle)


def bf16(table):
    return np.asarray(table, np.float32).astype(ml_dtypes.bfloat16)


@functools.cache
def lane_table():
    y6, z = np.divmod(np.arange(Y6 * N), N)
    k7, kz = np.divmod(np.arange(FLAT), N)
    phase = 16 * y6[:, None] * k7[None, :] + z[:, None] * kz[None, :]
    cosine, sine = unit(phase, N)
    table = np.zeros((Y6 * N, 2 * WIDE))
    table[:, :FLAT] = cosine
    table[:, WIDE : WIDE + FLAT] = sine
    return bf16(table)


@functools.cache
def twiddle_table():
    k7 = np.arange(FLAT) // N
    cosine, sine = unit(np.arange(Y16)[:, None] * k7[None, :], N)
    table = np.zeros((2, Y16, WIDE), np.float32)
    table[0, :, :FLAT] = cosine / N
    table[1, :, :FLAT] = sine / N
    return table


@functools.cache
def row_table():
    table = np.zeros((SLABS, ITEMS, 2, X6, 2, ITEMS, X6, Y16))
    cosine, sine = unit(np.arange(SLABS)[:, None] * np.arange(Y16)[None, :], SLABS)
    for item in range(ITEMS):
        for x in range(X6):
            table[:, item, 0, x, 0, item, x] = cosine
            table[:, item, 0, x, 1, item, x] = -sine
            table[:, item, 1, x, 0, item, x] = sine
            table[:, item, 1, x, 1, item, x] = cosine
    return bf16(table.reshape(SLABS * ITEMS * 2 * X6, 2 * ITEMS * X6 * Y16))


@functools.cache
def x_table():
    table = np.zeros((2, ITEMS, N, SLABS, ITEMS, 2, X6))
    cosine, sine = unit(np.arange(N)[:, None] * np.arange(N)[None, :], N)
    cosine = (cosine * 0.5 / math.sqrt(N)).reshape(N, SLABS, X6)
    sine = (sine * 0.5 / math.sqrt(N)).reshape(N, SLABS, X6)
    for item in range(ITEMS):
        table[0, item, :, :, item, 0] = cosine
        table[0, item, :, :, item, 1] = -sine
        table[1, item, :, :, item, 0] = sine
        table[1, item, :, :, item, 1] = cosine
    return bf16(table.reshape(2 * ITEMS * N, SLABS * ITEMS * 2 * X6))


@functools.cache
def pair_table():
    valence, conduction, imaginary = [], [], []
    for band in range(16):
        z1, group = divmod(band, 4)
        for slots in C_OF_CHUNK:
            for kind in range(4):
                for item in range(ITEMS):
                    slot_v = 2 * (item // 2) + kind // 2
                    slot_c = slots[item % 2]
                    valence.append(z1 * 4 + (group ^ slot_v))
                    conduction.append((z1 - slot_c) % 4 * 4 + group)
                    imaginary.append(kind % 2)
    return np.array(valence), np.array(conduction), np.array(imaginary)


def plane_kernel(v_ref, c_ref, lane_ref, twiddle_ref, row_ref, out_ref, low_ref):
    rows = X6 * Y16
    twiddle_c = twiddle_ref[0][None]
    twiddle_s = twiddle_ref[1][None]
    for item in range(ITEMS):
        wave_c = c_ref[item % 2]
        pairs = jnp.concatenate(
            [v_ref[2 * (item // 2)] * wave_c, v_ref[2 * (item // 2) + 1] * wave_c], axis=0
        )
        moved = jnp.dot(pairs, lane_ref[...], preferred_element_type=F32)
        real = moved[:rows, :WIDE] - moved[rows:, WIDE:]
        imag = moved[:rows, WIDE:] + moved[rows:, :WIDE]
        real = real.reshape(X6, Y16, WIDE)
        imag = imag.reshape(X6, Y16, WIDE)
        turned_r = real * twiddle_c - imag * twiddle_s
        turned_i = real * twiddle_s + imag * twiddle_c
        low_ref[item * rows : (item + 1) * rows, :] = turned_r.reshape(rows, WIDE).astype(BF16)
        low_ref[(ITEMS + item) * rows : (ITEMS + item + 1) * rows, :] = turned_i.reshape(
            rows, WIDE
        ).astype(BF16)
    per_slab = ITEMS * 2 * X6
    for part in range(4):
        count = SLABS // 4
        planes = jnp.dot(
            row_ref[part * count * per_slab : (part + 1) * count * per_slab, :],
            low_ref[...],
            preferred_element_type=F32,
        )
        out_ref[part * count : (part + 1) * count] = planes.astype(BF16).reshape(
            count, per_slab, WIDE
        )


def planes_of(v, c, tables):
    per_slab = ITEMS * 2 * X6
    return pl.pallas_call(
        plane_kernel,
        out_shape=jax.ShapeDtypeStruct((SLABS, per_slab, WIDE), BF16),
        scratch_shapes=[pltpu.VMEM((2 * ITEMS * X6 * Y16, WIDE), BF16)],
        compiler_params=pltpu.CompilerParams(vmem_limit_bytes=40 << 20),
        cost_estimate=pl.CostEstimate(
            flops=2_700_000_000, bytes_accessed=6_000_000, transcendentals=0
        ),
        name="planes",
    )(v, c, *tables)


def pick_kernel(t_ref, x_ref, flat_ref, kx_ref, out_ref, density_ref):
    rows = SLABS * ITEMS * 2 * X6
    density_ref[...] = jnp.dot(
        x_ref[...], t_ref[...].reshape(rows, WIDE), preferred_element_type=F32
    ).astype(BF16)

    def body(step, carry):
        lanes = pl.ds(pl.multiple_of(step * TILE, TILE), TILE)
        spot = lax.broadcasted_iota(jnp.int32, (WIDE, TILE), 0)
        chosen = jnp.where(spot == flat_ref[:, lanes], 1.0, 0.0).astype(BF16)
        values = jnp.dot(density_ref[...], chosen, preferred_element_type=F32)
        kx = lax.broadcasted_iota(jnp.int32, (N, TILE), 0) == kx_ref[:, lanes]
        values = jnp.where(kx[None], values.reshape(2 * ITEMS, N, TILE), 0.0)
        out_ref[:, lanes] = values.sum(axis=1)
        return carry

    lax.fori_loop(0, 2 * G_DEV // TILE, body, 0)


def points_of(planes, table, flat, kx):
    return pl.pallas_call(
        pick_kernel,
        out_shape=jax.ShapeDtypeStruct((2 * ITEMS, 2 * G_DEV), F32),
        scratch_shapes=[pltpu.VMEM((2 * ITEMS * N, WIDE), BF16)],
        compiler_params=pltpu.CompilerParams(vmem_limit_bytes=40 << 20),
        cost_estimate=pl.CostEstimate(
            flops=5_700_000_000, bytes_accessed=3_000_000, transcendentals=0
        ),
        name="points",
    )(planes, table, flat, kx)


def split_kernel(own0_ref, own1_ref, far_ref, out_ref):
    for chunk, own_ref in enumerate((own0_ref, own1_ref)):
        own_r = own_ref[:ITEMS, :G_DEV]
        own_i = own_ref[ITEMS:, :G_DEV]
        far_r = far_ref[chunk, :ITEMS, :].astype(F32)
        far_i = far_ref[chunk, ITEMS:, :].astype(F32)
        pairs = jnp.concatenate(
            [own_r + far_r, own_i - far_i, own_i + far_i, far_r - own_r], axis=0
        ).astype(BF16)
        for band in range(16):
            out_ref[band, chunk * 16 : (chunk + 1) * 16, :] = pairs[
                :, band * 128 : (band + 1) * 128
            ]


def split_pairs(own0, own1, far):
    return pl.pallas_call(
        split_kernel,
        out_shape=jax.ShapeDtypeStruct((16, 32, 128), BF16),
        cost_estimate=pl.CostEstimate(
            flops=1_000_000, bytes_accessed=500_000, transcendentals=0
        ),
        name="split",
    )(own0, own1, far)


def block_kernel(v_ref, c_ref, lane_ref, row_ref, out_ref):
    for chunk, slots in enumerate(C_OF_CHUNK):
        for half in range(2):
            for item in range(ITEMS):
                pair = v_ref[2 * (item // 2) + half] * c_ref[chunk, item % 2]
                sums = jnp.dot(pair, lane_ref[...], preferred_element_type=F32) * row_ref[...]
                index = (chunk * 2 + half) * ITEMS + item
                out_ref[index : index + 1, :] = sums.sum(axis=0, keepdims=True)


def block_sums(v, c, lanes, rows):
    return pl.pallas_call(
        block_kernel,
        out_shape=jax.ShapeDtypeStruct((16, 128), F32),
        cost_estimate=pl.CostEstimate(
            flops=250_000_000, bytes_accessed=1_500_000, transcendentals=0
        ),
        name="block",
    )(v, c, lanes, rows)


def sum_kernel(left_ref, right_ref, out_ref):
    out_ref[...] = lax.dot_general(
        left_ref[...],
        right_ref[...],
        (((0,), (0,)), ((), ())),
        preferred_element_type=F32,
    )


def copy_for_each(x, axis, devices):
    return lax.all_to_all(
        jnp.broadcast_to(x[None], (devices, *x.shape)), axis, 0, 0, tiled=True
    )


def wave_rows(wave):
    return wave.reshape(X6, Y6, Y16, N).transpose(0, 2, 1, 3).reshape(X6 * Y16, Y6 * N)


def turn(phase):
    angle = (phase % N).astype(F32) * (2.0 * math.pi / N)
    return jnp.cos(angle), -jnp.sin(angle)


def per_device(
    valence_wave,
    conduction_wave,
    valence_index,
    occupied_energy,
    conduction_energy,
    frequency,
    gvec_cell,
    block_cell,
):
    col = lax.axis_index(COL)
    wave_v = wave_rows(valence_wave)
    wave_c = wave_rows(conduction_wave)
    all_v = [wave_v]
    for mask in (1, 2, 3):
        all_v.append(lax.ppermute(wave_v, VGROUP, [(i, i ^ mask) for i in range(4)]))
    all_c = [wave_c] + [None] * 3
    for shift in (1, 3, 2):
        all_c[shift] = lax.ppermute(wave_c, "z1", [(i, (i + shift) % 4) for i in range(4)])
    v = jnp.stack(all_v)
    c = [jnp.stack([all_c[slot] for slot in slots]) for slots in C_OF_CHUNK]

    mirror_of = [(k, SLABS - 1 - k) for k in range(SLABS)]
    far_cell = lax.ppermute(gvec_cell, COL, mirror_of)
    far_x, far_y, far_z = far_cell // 576, far_cell // N % 6, far_cell % N
    flat = jnp.concatenate([gvec_cell % 576, (6 - far_y) * N + (N - far_z) % N])[None]
    kx = jnp.concatenate([gvec_cell // 576, (N - far_x) % N])[None]

    cells = copy_for_each(block_cell, COL, SLABS).reshape(NBLOCK)
    block_x = cells // 576
    block_y = jnp.arange(NBLOCK, dtype=jnp.int32) * 6 + cells // N % 6
    block_z = cells % N

    tables = (lane_table(), twiddle_table(), row_table())
    sent = [lax.all_to_all(planes_of(v, part, tables), COL, 0, 0, tiled=True) for part in c]

    lane = jnp.arange(Y6 * N, dtype=jnp.int32)
    lane_c, lane_s = turn(
        (lane // N * 16)[:, None] * block_y[None] + (lane % N)[:, None] * block_z[None]
    )
    row = jnp.arange(X6 * Y16, dtype=jnp.int32)
    row_c, row_s = turn(
        (row // Y16 + X6 * col)[:, None] * block_x[None] + (row % Y16)[:, None] * block_y[None]
    )
    scale = 1.0 / (N * math.sqrt(N))
    zeros = jnp.zeros((Y6 * N, 64), F32)
    lanes = jnp.concatenate([lane_c, lane_s, lane_c, lane_s, zeros], axis=1).astype(BF16)
    rows = jnp.concatenate([row_c, -row_s, row_s, row_c, zeros[: X6 * Y16]], axis=1) * scale
    partial = block_sums(v, jnp.stack(c), lanes, rows)
    here = copy_for_each(partial, COL, SLABS).reshape(SLABS, 16, 128).sum(axis=0)
    here = jnp.concatenate(
        [here[:, :16] + here[:, 16:32], here[:, 32:48] + here[:, 48:64]], axis=1
    )
    block = copy_for_each(here.astype(BF16), BAND, 16).reshape(16, CHUNKS, 2, ITEMS, 2, NBLOCK)

    pair_v, pair_c, pair_part = pair_table()
    occupied = jnp.arange(occupied_energy.shape[0], dtype=jnp.int32)
    valence_energy = jnp.sum(
        jnp.where(valence_index[:, None] == occupied[None, :], occupied_energy[None, :], 0.0),
        axis=1,
    )
    count_v, count_c = valence_index.shape[0], conduction_energy.shape[0]
    energy_v = jnp.sum(
        jnp.where(pair_v[:, None] == np.arange(count_v)[None], valence_energy[None], 0.0), axis=1
    )
    energy_c = jnp.sum(
        jnp.where(pair_c[:, None] == np.arange(count_c)[None], conduction_energy[None], 0.0),
        axis=1,
    )
    gap = (energy_c - energy_v)[:, None]
    weight = (
        -4.0 * gap / (gap * gap + frequency[None] * frequency[None])
        * (1.0 / math.sqrt(count_v * count_c))
    )
    block = block.astype(F32)
    real, imag = block[..., 0, :], block[..., 1, :]
    columns = jnp.stack(
        [jnp.stack([real, -imag], axis=-2), jnp.stack([imag, real], axis=-2)], axis=3
    )
    columns = columns.reshape(512, 1, 2, NBLOCK)
    right = (columns * weight[:, :, None, None]).astype(BF16).reshape(512, -1)

    found = [points_of(planes, x_table(), flat, kx) for planes in sent]
    mirrored = jnp.stack([part[:, G_DEV:].astype(BF16) for part in found])
    far = lax.ppermute(mirrored, COL, mirror_of)
    pairs = split_pairs(found[0], found[1], far)
    left = lax.all_to_all(pairs, BAND, 0, 0, tiled=True).reshape(512, 128)
    return pl.pallas_call(
        sum_kernel,
        out_shape=jax.ShapeDtypeStruct((128, right.shape[1]), F32),
        name="pair_sum",
    )(left, right)


def solution(mesh):
    fine = Mesh(
        mesh.devices.reshape(4, 2, 2, 4, 2, 2), ("z1", "z0", "yl", "x", "yh", "co")
    )
    return jax.shard_map(
        per_device,
        mesh=fine,
        in_specs=(
            P(BAND, COL, None),
            P(BAND, COL, None),
            P(),
            P(),
            P(),
            P(),
            P(COL),
            P(COL),
        ),
        out_specs=P(COL + BAND, None),
        check_vma=False,
    )
```

```python
import functools
import math

import jax
import jax.numpy as jnp
import ml_dtypes
import numpy as np
from jax import lax
from jax.experimental import pallas as pl
from jax.experimental.pallas import tpu as pltpu
from jax.sharding import Mesh
from jax.sharding import PartitionSpec as P

BF16 = jnp.bfloat16
F32 = jnp.float32

N = 96
SLABS = 16
X6 = 6
Y6 = 6
Y16 = 16
K7 = 7
FLAT = K7 * N
WIDE = 768
ITEMS = 4
CHUNKS = 2
SPARE = 640
G_DEV = 2048
NBLOCK = 16
TILE = 512

BAND = ("z1", "z0", "yl")
VGROUP = ("z0", "yl")
COL = ("x", "yh", "co")


def unit(phase, period):
    angle = 2.0 * np.pi * (np.asarray(phase) % period) / period
    return np.cos(angle), -np.sin(angle)


def bf16(table):
    return np.asarray(table, np.float32).astype(ml_dtypes.bfloat16)


@functools.cache
def lane_table():
    y6, z = np.divmod(np.arange(Y6 * N), N)
    k7, kz = np.divmod(np.arange(FLAT), N)
    phase = 16 * y6[:, None] * k7[None, :] + z[:, None] * kz[None, :]
    cosine, sine = unit(phase, N)
    table = np.zeros((Y6 * N, 2 * WIDE))
    table[:, :FLAT] = cosine
    table[:, WIDE : WIDE + FLAT] = sine
    return bf16(table)


@functools.cache
def twiddle_table():
    k7 = np.arange(FLAT) // N
    cosine, sine = unit(np.arange(Y16)[:, None] * k7[None, :], N)
    table = np.zeros((2, Y16, WIDE), np.float32)
    table[0, :, :FLAT] = cosine / N
    table[1, :, :FLAT] = sine / N
    return table


@functools.cache
def row_table():
    table = np.zeros((SLABS, ITEMS, 2, X6, 2, ITEMS, X6, Y16))
    cosine, sine = unit(np.arange(SLABS)[:, None] * np.arange(Y16)[None, :], SLABS)
    for item in range(ITEMS):
        for x in range(X6):
            table[:, item, 0, x, 0, item, x] = cosine
            table[:, item, 0, x, 1, item, x] = -sine
            table[:, item, 1, x, 0, item, x] = sine
            table[:, item, 1, x, 1, item, x] = cosine
    return bf16(table.reshape(SLABS * ITEMS * 2 * X6, 2 * ITEMS * X6 * Y16))


@functools.cache
def x_table():
    table = np.zeros((2, ITEMS, N, SLABS, ITEMS, 2, X6))
    cosine, sine = unit(np.arange(N)[:, None] * np.arange(N)[None, :], N)
    cosine = (cosine * 0.5 / math.sqrt(N)).reshape(N, SLABS, X6)
    sine = (sine * 0.5 / math.sqrt(N)).reshape(N, SLABS, X6)
    for item in range(ITEMS):
        table[0, item, :, :, item, 0] = cosine
        table[0, item, :, :, item, 1] = -sine
        table[1, item, :, :, item, 0] = sine
        table[1, item, :, :, item, 1] = cosine
    return bf16(table.reshape(2 * ITEMS * N, SLABS * ITEMS * 2 * X6))


@functools.cache
def pair_table():
    valence, conduction = [], []
    for band in range(16):
        z1, group = divmod(band, 4)
        for chunk in range(CHUNKS):
            for half in range(2):
                for item in range(ITEMS):
                    slot_v = 2 * (item // 2) + half
                    slot_c = 2 * chunk + item % 2
                    valence.append(z1 * 4 + (group ^ slot_v))
                    conduction.append((z1 ^ slot_c) * 4 + group)
    return np.array(valence), np.array(conduction)


@functools.cache
def column_tables():
    tables = np.zeros((2, 128, 4, 2, NBLOCK))
    m = np.arange(NBLOCK)
    tables[0, 32 + m, :, 0, m] = 1.0
    tables[0, 64 + m, :, 1, m] = -1.0
    tables[1, 64 + m, :, 0, m] = 1.0
    tables[1, 32 + m, :, 1, m] = 1.0
    return bf16(tables.reshape(2, 128, 128))


def plane_kernel(v0, v1, v2, v3, c_ref, lane_ref, twiddle_ref, row_ref, *refs):
    *block_ref, out_ref, low_ref = refs
    waves = (v0, v1, v2, v3)
    rows = X6 * Y16
    twiddle_c = twiddle_ref[0][None]
    twiddle_s = twiddle_ref[1][None]
    for item in range(ITEMS):
        wave_c = c_ref[item % 2]
        pairs = jnp.concatenate(
            [waves[2 * (item // 2)][...] * wave_c, waves[2 * (item // 2) + 1][...] * wave_c],
            axis=0,
        )
        moved = jnp.dot(pairs, lane_ref[...], preferred_element_type=F32)
        real = moved[:rows, :WIDE] - moved[rows:, WIDE:]
        imag = moved[:rows, WIDE:] + moved[rows:, :WIDE]
        real = real.reshape(X6, Y16, WIDE)
        imag = imag.reshape(X6, Y16, WIDE)
        turned_r = real * twiddle_c - imag * twiddle_s
        turned_i = real * twiddle_s + imag * twiddle_c
        low_ref[item * rows : (item + 1) * rows, :] = turned_r.reshape(rows, WIDE).astype(BF16)
        low_ref[(ITEMS + item) * rows : (ITEMS + item + 1) * rows, :] = turned_i.reshape(
            rows, WIDE
        ).astype(BF16)
    per_slab = ITEMS * 2 * X6
    count = SLABS // 4
    for part in range(4):
        planes = jnp.dot(
            row_ref[part * count * per_slab : (part + 1) * count * per_slab, :],
            low_ref[...],
            preferred_element_type=F32,
        ).reshape(count, per_slab, WIDE)
        slabs = slice(part * count, (part + 1) * count)
        out_ref[slabs] = planes.astype(BF16)
        if block_ref:
            spare = planes[:, :32, SPARE:] + block_ref[0][...][None]
            out_ref[slabs, :32, SPARE:] = spare.astype(BF16)


def planes_of(v, c, tables, *block):
    per_slab = ITEMS * 2 * X6
    return pl.pallas_call(
        plane_kernel,
        out_shape=jax.ShapeDtypeStruct((SLABS, per_slab, WIDE), BF16),
        scratch_shapes=[pltpu.VMEM((2 * ITEMS * X6 * Y16, WIDE), BF16)],
        compiler_params=pltpu.CompilerParams(vmem_limit_bytes=40 << 20),
        cost_estimate=pl.CostEstimate(
            flops=2_700_000_000, bytes_accessed=6_000_000, transcendentals=0
        ),
        name="planes",
    )(*v, c, *tables, *block)


def pick(density_ref, flat_ref, kx_ref, store):
    def body(step, carry):
        lanes = pl.ds(pl.multiple_of(step * TILE, TILE), TILE)
        spot = lax.broadcasted_iota(jnp.int32, (WIDE, TILE), 0)
        chosen = jnp.where(spot == flat_ref[:, lanes], 1.0, 0.0).astype(BF16)
        values = jnp.dot(density_ref[...], chosen, preferred_element_type=F32)
        kx = lax.broadcasted_iota(jnp.int32, (N, TILE), 0) == kx_ref[:, lanes]
        values = jnp.where(kx[None], values.reshape(2 * ITEMS, N, TILE), 0.0)
        store(lanes, values.sum(axis=1))
        return carry

    lax.fori_loop(0, G_DEV // TILE, body, 0)


def transform_x(t_ref, x_ref, density_ref):
    density_ref[...] = jnp.dot(
        x_ref[...],
        t_ref[...].reshape(SLABS * ITEMS * 2 * X6, WIDE),
        preferred_element_type=F32,
    ).astype(BF16)


def first_kernel(t_ref, x_ref, own_ref, own_kx_ref, far_ref, far_kx_ref, own_out, far_out, low):
    transform_x(t_ref, x_ref, low)

    def store_far(lanes, values):
        far_out[:, lanes] = values.astype(BF16)

    def store_own(lanes, values):
        own_out[:, lanes] = values

    pick(low, far_ref, far_kx_ref, store_far)
    pick(low, own_ref, own_kx_ref, store_own)


def second_far_kernel(t_ref, x_ref, far_ref, far_kx_ref, first_ref, far_out, low, block_out):
    transform_x(t_ref, x_ref, low)
    far_out[0] = first_ref[...]

    def store_far(lanes, values):
        far_out[1, :, lanes] = values.astype(BF16)

    pick(low, far_ref, far_kx_ref, store_far)
    spare = t_ref[:, :32, SPARE:].astype(F32).sum(axis=0)
    spare = spare[:16] + spare[16:]
    spare = spare + pltpu.roll(spare, 128 - NBLOCK, 1)
    block_out[...] = spare


def second_own_kernel(low, own_ref, own_kx_ref, own_out):
    def store_own(lanes, values):
        own_out[:, lanes] = values

    pick(low, own_ref, own_kx_ref, store_own)


OWN = jax.ShapeDtypeStruct((2 * ITEMS, G_DEV), F32)
LOW = (2 * ITEMS * N, WIDE)


def first_points(planes, table, own, far):
    return pl.pallas_call(
        first_kernel,
        out_shape=(OWN, jax.ShapeDtypeStruct((2 * ITEMS, G_DEV), BF16)),
        scratch_shapes=[pltpu.VMEM(LOW, BF16)],
        compiler_params=pltpu.CompilerParams(vmem_limit_bytes=40 << 20),
        cost_estimate=pl.CostEstimate(
            flops=5_700_000_000, bytes_accessed=3_000_000, transcendentals=0
        ),
        name="first_points",
    )(planes, table, *own, *far)


def second_far_points(planes, table, far, first):
    return pl.pallas_call(
        second_far_kernel,
        out_shape=(
            jax.ShapeDtypeStruct((CHUNKS, 2 * ITEMS, G_DEV), BF16),
            jax.ShapeDtypeStruct(LOW, BF16),
            jax.ShapeDtypeStruct((16, 128), F32),
        ),
        compiler_params=pltpu.CompilerParams(vmem_limit_bytes=40 << 20),
        cost_estimate=pl.CostEstimate(
            flops=3_300_000_000, bytes_accessed=4_000_000, transcendentals=0
        ),
        name="second_far_points",
    )(planes, table, *far, first)


def second_own_points(low, own):
    return pl.pallas_call(
        second_own_kernel,
        out_shape=OWN,
        compiler_params=pltpu.CompilerParams(vmem_limit_bytes=40 << 20),
        cost_estimate=pl.CostEstimate(
            flops=2_400_000_000, bytes_accessed=1_300_000, transcendentals=0
        ),
        name="second_own_points",
    )(low, *own)


def split_kernel(own0_ref, own1_ref, far_ref, block_ref, out_ref):
    real, imag = [], []
    for chunk, own_ref in enumerate((own0_ref, own1_ref)):
        own_r = own_ref[:ITEMS, :]
        own_i = own_ref[ITEMS:, :]
        far_r = far_ref[chunk, :ITEMS, :].astype(F32)
        far_i = far_ref[chunk, ITEMS:, :].astype(F32)
        real += [own_r + far_r, own_i + far_i]
        imag += [own_i - far_i, far_r - own_r]
    pairs = jnp.concatenate(real + imag, axis=0).astype(BF16)
    block = block_ref[...].astype(BF16)
    for band in range(16):
        out_ref[band, :32, :] = pairs[:, band * 128 : (band + 1) * 128]
        out_ref[band, 32:, :] = block


def split_pairs(own0, own1, far, block):
    return pl.pallas_call(
        split_kernel,
        out_shape=jax.ShapeDtypeStruct((16, 48, 128), BF16),
        cost_estimate=pl.CostEstimate(
            flops=1_000_000, bytes_accessed=500_000, transcendentals=0
        ),
        name="split",
    )(own0, own1, far, block)


def block_kernel(v0, v1, v2, v3, c0_ref, c1_ref, lane_ref, row_ref, out_ref):
    waves = (v0, v1, v2, v3)
    for chunk, c_ref in enumerate((c0_ref, c1_ref)):
        for half in range(2):
            for item in range(ITEMS):
                pair = waves[2 * (item // 2) + half][...] * c_ref[item % 2]
                sums = jnp.dot(pair, lane_ref[...], preferred_element_type=F32) * row_ref[...]
                total = sums.sum(axis=0, keepdims=True)
                high = total.astype(BF16).astype(F32)
                index = (chunk * 2 + half) * ITEMS + item
                out_ref[index : index + 1, :] = high
                out_ref[16 + index : 17 + index, :] = total - high


def block_sums(v, c, lanes, rows):
    return pl.pallas_call(
        block_kernel,
        out_shape=jax.ShapeDtypeStruct((32, 128), F32),
        cost_estimate=pl.CostEstimate(
            flops=250_000_000, bytes_accessed=1_500_000, transcendentals=0
        ),
        name="block",
    )(*v, *c, lanes, rows)


def sum_kernel(pairs_ref, weight_ref, column_ref, out_ref):
    pairs = 16 * 16
    block = pairs_ref[:, 32:, :].reshape(pairs, 128)
    total = None
    for part in range(2):
        left = pairs_ref[:, 16 * part : 16 * (part + 1), :].reshape(pairs, 128)
        columns = jnp.dot(block, column_ref[part], preferred_element_type=F32)
        right = (columns * weight_ref[...]).astype(BF16)
        term = lax.dot_general(
            left, right, (((0,), (0,)), ((), ())), preferred_element_type=F32
        )
        total = term if total is None else total + term
    out_ref[...] = total


def wave_rows(wave):
    return wave.reshape(X6, Y6, Y16, N).transpose(0, 2, 1, 3).reshape(X6 * Y16, Y6 * N)


def turn(phase):
    angle = (phase % N).astype(F32) * (2.0 * math.pi / N)
    return jnp.cos(angle), -jnp.sin(angle)


def per_device(
    valence_wave,
    conduction_wave,
    valence_index,
    occupied_energy,
    conduction_energy,
    frequency,
    gvec_cell,
    block_cell,
):
    col = lax.axis_index(COL)
    wave_v = wave_rows(valence_wave)
    wave_c = wave_rows(conduction_wave)
    v = [wave_v]
    for mask in (1, 2, 3):
        v.append(lax.ppermute(wave_v, VGROUP, [(i, i ^ mask) for i in range(4)]))
    c = [jnp.stack([wave_c, lax.ppermute(wave_c, "z1", [(i, i ^ 1) for i in range(4)])])]
    c.append(lax.ppermute(c[0], "z1", [(i, i ^ 2) for i in range(4)]))

    tables = (lane_table(), twiddle_table(), row_table())
    sent0 = lax.all_to_all(planes_of(v, c[0], tables), COL, 0, 0, tiled=True)

    mirror_of = [(k, SLABS - 1 - k) for k in range(SLABS)]
    far_cell = lax.ppermute(gvec_cell, COL, mirror_of)
    far_x, far_y, far_z = far_cell // 576, far_cell // N % 6, far_cell % N
    own = ((gvec_cell % 576)[None], (gvec_cell // 576)[None])
    far = (((6 - far_y) * N + (N - far_z) % N)[None], ((N - far_x) % N)[None])

    spots = jnp.arange(NBLOCK, dtype=jnp.int32)
    cells = jnp.where(spots == col, block_cell[0], 0)
    for mask in (1, 2, 4, 8):
        cells = cells + lax.ppermute(cells, COL, [(k, k ^ mask) for k in range(SLABS)])
    block_x = cells // 576
    block_y = spots * 6 + cells // N % 6
    block_z = cells % N
    lane = jnp.arange(Y6 * N, dtype=jnp.int32)
    lane_c, lane_s = turn(
        (lane // N * 16)[:, None] * block_y[None] + (lane % N)[:, None] * block_z[None]
    )
    row = jnp.arange(X6 * Y16, dtype=jnp.int32)
    row_c, row_s = turn(
        (row // Y16 + X6 * col)[:, None] * block_x[None] + (row % Y16)[:, None] * block_y[None]
    )
    scale = 1.0 / (N * math.sqrt(N))
    zeros = jnp.zeros((Y6 * N, 32), F32)
    lanes = jnp.concatenate([zeros, lane_c, lane_s, lane_c, lane_s, zeros], axis=1).astype(BF16)
    zeros = zeros[: X6 * Y16]
    rows = jnp.concatenate([zeros, row_c, -row_s, row_s, row_c, zeros], axis=1) * scale
    block = block_sums(v, c, lanes, rows)
    sent1 = lax.all_to_all(planes_of(v, c[1], tables, block), COL, 0, 0, tiled=True)

    pair_v, pair_c = pair_table()
    occupied = jnp.arange(occupied_energy.shape[0], dtype=jnp.int32)
    valence_energy = jnp.sum(
        jnp.where(valence_index[:, None] == occupied[None, :], occupied_energy[None, :], 0.0),
        axis=1,
    )
    count_v, count_c = valence_index.shape[0], conduction_energy.shape[0]
    energy_v = jnp.sum(
        jnp.where(pair_v[:, None] == np.arange(count_v)[None], valence_energy[None], 0.0), axis=1
    )
    energy_c = jnp.sum(
        jnp.where(pair_c[:, None] == np.arange(count_c)[None], conduction_energy[None], 0.0),
        axis=1,
    )
    gap = (energy_c - energy_v)[:, None]
    omega = jnp.repeat(frequency, 2 * NBLOCK)[None]
    weight = -4.0 * gap / (gap * gap + omega * omega) * (1.0 / math.sqrt(count_v * count_c))

    own0, far0 = first_points(sent0, x_table(), own, far)
    mirrored, low, columns = second_far_points(sent1, x_table(), far, far0)
    mirrored = lax.ppermute(mirrored, COL, mirror_of)
    own1 = second_own_points(low, own)
    pairs = split_pairs(own0, own1, mirrored, columns)
    pairs = lax.all_to_all(pairs, BAND, 0, 0, tiled=True)
    return pl.pallas_call(
        sum_kernel,
        out_shape=jax.ShapeDtypeStruct((128, 128), F32),
        name="pair_sum",
    )(pairs, weight, column_tables())


def solution(mesh):
    fine = Mesh(
        mesh.devices.reshape(4, 2, 2, 4, 2, 2), ("z1", "z0", "yl", "x", "yh", "co")
    )
    return jax.shard_map(
        per_device,
        mesh=fine,
        in_specs=(
            P(BAND, COL, None),
            P(BAND, COL, None),
            P(),
            P(),
            P(),
            P(),
            P(COL),
            P(COL),
        ),
        out_specs=P(COL + BAND, None),
        check_vma=False,
    )
```

```python
import functools
import math

import jax
import jax.numpy as jnp
import ml_dtypes
import numpy as np
from jax import lax
from jax.experimental import pallas as pl
from jax.experimental.pallas import tpu as pltpu
from jax.sharding import Mesh
from jax.sharding import PartitionSpec as P

BF16 = jnp.bfloat16
F32 = jnp.float32

N = 96
SLABS = 16
X6 = 6
Y6 = 6
Y16 = 16
K7 = 7
FLAT = K7 * N
WIDE = 768
ITEMS = 4
CHUNKS = 2
SPARE = 640
G_DEV = 2048
NBLOCK = 16
TILE = 512

BAND = ("z1", "z0", "yl")
VGROUP = ("z0", "yl")
COL = ("x", "yh", "co")


def unit(phase, period):
    angle = 2.0 * np.pi * (np.asarray(phase) % period) / period
    return np.cos(angle), -np.sin(angle)


def bf16(table):
    return np.asarray(table, np.float32).astype(ml_dtypes.bfloat16)


@functools.cache
def lane_table():
    y6, z = np.divmod(np.arange(Y6 * N), N)
    k7, kz = np.divmod(np.arange(FLAT), N)
    phase = 16 * y6[:, None] * k7[None, :] + z[:, None] * kz[None, :]
    cosine, sine = unit(phase, N)
    table = np.zeros((Y6 * N, 2 * WIDE))
    table[:, :FLAT] = cosine
    table[:, WIDE : WIDE + FLAT] = sine
    return bf16(table)


@functools.cache
def twiddle_table():
    k7 = np.arange(FLAT) // N
    cosine, sine = unit(np.arange(Y16)[:, None] * k7[None, :], N)
    table = np.zeros((2, Y16, WIDE), np.float32)
    table[0, :, :FLAT] = cosine / N
    table[1, :, :FLAT] = sine / N
    return table


@functools.cache
def row_table():
    table = np.zeros((SLABS, ITEMS, 2, X6, 2, ITEMS, X6, Y16))
    cosine, sine = unit(np.arange(SLABS)[:, None] * np.arange(Y16)[None, :], SLABS)
    for item in range(ITEMS):
        for x in range(X6):
            table[:, item, 0, x, 0, item, x] = cosine
            table[:, item, 0, x, 1, item, x] = -sine
            table[:, item, 1, x, 0, item, x] = sine
            table[:, item, 1, x, 1, item, x] = cosine
    return bf16(table.reshape(SLABS * ITEMS * 2 * X6, 2 * ITEMS * X6 * Y16))


@functools.cache
def x_table():
    table = np.zeros((2, ITEMS, N, SLABS, ITEMS, 2, X6))
    cosine, sine = unit(np.arange(N)[:, None] * np.arange(N)[None, :], N)
    cosine = (cosine * 0.5 / math.sqrt(N)).reshape(N, SLABS, X6)
    sine = (sine * 0.5 / math.sqrt(N)).reshape(N, SLABS, X6)
    for item in range(ITEMS):
        table[0, item, :, :, item, 0] = cosine
        table[0, item, :, :, item, 1] = -sine
        table[1, item, :, :, item, 0] = sine
        table[1, item, :, :, item, 1] = cosine
    return bf16(table.reshape(2 * ITEMS * N, SLABS * ITEMS * 2 * X6))


@functools.cache
def pair_table():
    valence, conduction = [], []
    for band in range(16):
        z1, group = divmod(band, 4)
        for chunk in range(CHUNKS):
            for half in range(2):
                for item in range(ITEMS):
                    slot_v = 2 * (item // 2) + half
                    slot_c = (0, 1, 3, 2)[2 * chunk + item % 2]
                    valence.append(z1 * 4 + (group ^ slot_v))
                    conduction.append((z1 - slot_c) % 4 * 4 + group)
    return np.array(valence), np.array(conduction)


@functools.cache
def column_tables():
    tables = np.zeros((2, 128, 4, 2, NBLOCK))
    m = np.arange(NBLOCK)
    tables[0, 32 + m, :, 0, m] = 1.0
    tables[0, 64 + m, :, 1, m] = -1.0
    tables[1, 64 + m, :, 0, m] = 1.0
    tables[1, 32 + m, :, 1, m] = 1.0
    return bf16(tables.reshape(2, 128, 128))


VMEM = pl.BlockSpec(memory_space=pltpu.VMEM)
HBM = pl.BlockSpec(memory_space=pltpu.HBM)
LANE_CUTS = 3


def in_hbm(x):
    return pltpu.with_memory_space_constraint(jnp.asarray(x), pltpu.HBM)


X_CUTS = 3


def cut_copies(source, target, sems, cuts, dim):
    size = source.shape[dim] // cuts
    moves = []
    for i in range(cuts):
        window = pl.ds(i * size, size)
        spot = (window,) if dim == 0 else (slice(None), window)
        moves.append(pltpu.make_async_copy(source.at[spot], target.at[spot], sems.at[i]))
        moves[-1].start()
    return moves


def plane_kernel(v0, v1, v2, v3, c0, c1, lane_hbm, row_hbm, twiddle_ref, *refs, through):
    *refs, low_ref, lane_ref, row_ref, slab_ref, lane_sems, row_sem, slab_sems, keep_sems = refs
    lane_moves = cut_copies(lane_hbm, lane_ref, lane_sems, LANE_CUTS, 1)
    row_move = pltpu.make_async_copy(row_hbm, row_ref, row_sem)
    row_move.start()
    if through:
        block_ref = None
        out_ref = refs[through]
        kept = [
            pltpu.make_async_copy(refs[i], refs[through + 1 + i], keep_sems.at[i])
            for i in range(through)
        ]
    else:
        block_ref, out_ref = refs
        kept = []
    for move in kept:
        move.start()
    waves = (v0, v1, v2, v3)
    waves_c = (c0, c1)
    rows = X6 * Y16
    twiddle_c = twiddle_ref[0][None]
    twiddle_s = twiddle_ref[1][None]
    width = 2 * WIDE // LANE_CUTS
    for item in range(ITEMS):
        wave_c = waves_c[item % 2][...]
        pairs = jnp.concatenate(
            [waves[2 * (item // 2)][...] * wave_c, waves[2 * (item // 2) + 1][...] * wave_c],
            axis=0,
        )
        parts = []
        for i in range(LANE_CUTS):
            if item == 0:
                lane_moves[i].wait()
            parts.append(
                jnp.dot(
                    pairs,
                    lane_ref[:, i * width : (i + 1) * width],
                    preferred_element_type=F32,
                )
            )
        moved = jnp.concatenate(parts, axis=1)
        real = moved[:rows, :WIDE] - moved[rows:, WIDE:]
        imag = moved[:rows, WIDE:] + moved[rows:, :WIDE]
        real = real.reshape(X6, Y16, WIDE)
        imag = imag.reshape(X6, Y16, WIDE)
        turned_r = real * twiddle_c - imag * twiddle_s
        turned_i = real * twiddle_s + imag * twiddle_c
        low_ref[item * rows : (item + 1) * rows, :] = turned_r.reshape(rows, WIDE).astype(BF16)
        low_ref[(ITEMS + item) * rows : (ITEMS + item + 1) * rows, :] = turned_i.reshape(
            rows, WIDE
        ).astype(BF16)
    row_move.wait()
    per_slab = ITEMS * 2 * X6
    count = SLABS // 4
    moves = []
    for part in range(4):
        planes = jnp.dot(
            row_ref[part * count * per_slab : (part + 1) * count * per_slab, :],
            low_ref[...],
            preferred_element_type=F32,
        ).reshape(count, per_slab, WIDE)
        slabs = slice(part * count, (part + 1) * count)
        slab_ref[slabs] = planes.astype(BF16)
        if block_ref is not None:
            spare = planes[:, :32, SPARE:] + block_ref[...][None]
            slab_ref[slabs, :32, SPARE:] = spare.astype(BF16)
        moves.append(
            pltpu.make_async_copy(
                slab_ref.at[pl.ds(part * count, count)],
                out_ref.at[pl.ds(part * count, count)],
                slab_sems.at[part],
            )
        )
        moves[-1].start()
    for move in (*moves, *kept):
        move.wait()


def planes_of(v, c, tables, block=(), through=()):
    per_slab = ITEMS * 2 * X6
    lane, row, twiddle = tables
    extra = (*block, *through)
    return pl.pallas_call(
        functools.partial(plane_kernel, through=len(through)),
        out_shape=[
            pltpu.HBM((SLABS, per_slab, WIDE), BF16),
            *(pltpu.HBM(x.shape, x.dtype) for x in through),
        ],
        in_specs=[VMEM] * 6
        + [HBM] * 2
        + [VMEM] * (1 + len(block))
        + [pl.BlockSpec(memory_space=pl.ANY)] * len(through),
        out_specs=[HBM] * (1 + len(through)),
        scratch_shapes=[
            pltpu.VMEM((2 * ITEMS * X6 * Y16, WIDE), BF16),
            pltpu.VMEM(lane.shape, BF16),
            pltpu.VMEM(row.shape, BF16),
            pltpu.VMEM((SLABS, per_slab, WIDE), BF16),
            pltpu.SemaphoreType.DMA((LANE_CUTS,)),
            pltpu.SemaphoreType.DMA,
            pltpu.SemaphoreType.DMA((4,)),
            pltpu.SemaphoreType.DMA((max(len(through), 1),)),
        ],
        compiler_params=pltpu.CompilerParams(vmem_limit_bytes=16 << 20),
        cost_estimate=pl.CostEstimate(
            flops=PLANES_FLOPS, bytes_accessed=100_000, transcendentals=0
        ),
        name="planes",
    )(*v, *c, in_hbm(lane), in_hbm(row), twiddle, *extra)


PLANES_FLOPS = 50_000_000


def pick(density_ref, flat_ref, kx_ref, store):
    def body(step, carry):
        lanes = pl.ds(pl.multiple_of(step * TILE, TILE), TILE)
        spot = lax.broadcasted_iota(jnp.int32, (WIDE, TILE), 0)
        chosen = jnp.where(spot == flat_ref[:, lanes], 1.0, 0.0).astype(BF16)
        values = jnp.dot(density_ref[...], chosen, preferred_element_type=F32)
        kx = lax.broadcasted_iota(jnp.int32, (N, TILE), 0) == kx_ref[:, lanes]
        values = jnp.where(kx[None], values.reshape(2 * ITEMS, N, TILE), 0.0)
        store(lanes, values.sum(axis=1))
        return carry

    lax.fori_loop(0, G_DEV // TILE, body, 0)


def transform_x(t_ref, x_hbm, x_ref, sems, density_ref):
    moves = cut_copies(x_hbm, x_ref, sems, X_CUTS, 0)
    size = x_ref.shape[0] // X_CUTS
    planes = t_ref[...].reshape(SLABS * ITEMS * 2 * X6, WIDE)
    for i in range(X_CUTS):
        moves[i].wait()
        window = slice(i * size, (i + 1) * size)
        density_ref[window, :] = jnp.dot(
            x_ref[window, :], planes, preferred_element_type=F32
        ).astype(BF16)


def first_kernel(
    t_ref, x_hbm, own_ref, own_kx_ref, far_ref, far_kx_ref, own_out, far_out, low, x_ref, sems
):
    transform_x(t_ref, x_hbm, x_ref, sems, low)

    def store_far(lanes, values):
        far_out[:, lanes] = values.astype(BF16)

    def store_own(lanes, values):
        own_out[:, lanes] = values

    pick(low, far_ref, far_kx_ref, store_far)
    pick(low, own_ref, own_kx_ref, store_own)


def second_far_kernel(
    t_ref, x_hbm, far_ref, far_kx_ref, first_ref, far_out, low, block_out, x_ref, sems
):
    transform_x(t_ref, x_hbm, x_ref, sems, low)
    far_out[0] = first_ref[...]

    def store_far(lanes, values):
        far_out[1, :, lanes] = values.astype(BF16)

    pick(low, far_ref, far_kx_ref, store_far)
    spare = t_ref[:, :32, SPARE:].astype(F32).sum(axis=0)
    spare = spare[:16] + spare[16:]
    spare = spare + pltpu.roll(spare, 128 - NBLOCK, 1)
    block_out[...] = spare


def second_own_kernel(low, own_ref, own_kx_ref, own_out):
    def store_own(lanes, values):
        own_out[:, lanes] = values

    pick(low, own_ref, own_kx_ref, store_own)


OWN = jax.ShapeDtypeStruct((2 * ITEMS, G_DEV), F32)
LOW = (2 * ITEMS * N, WIDE)
X_SCRATCH = [
    pltpu.VMEM((2 * ITEMS * N, SLABS * ITEMS * 2 * X6), BF16),
    pltpu.SemaphoreType.DMA((X_CUTS,)),
]


def first_points(planes, table, own, far):
    return pl.pallas_call(
        first_kernel,
        out_shape=(OWN, jax.ShapeDtypeStruct((2 * ITEMS, G_DEV), BF16)),
        in_specs=[VMEM, HBM] + [VMEM] * 4,
        scratch_shapes=[pltpu.VMEM(LOW, BF16), *X_SCRATCH],
        compiler_params=pltpu.CompilerParams(vmem_limit_bytes=16 << 20),
        cost_estimate=pl.CostEstimate(
            flops=100_000_000, bytes_accessed=100_000, transcendentals=0
        ),
        name="first_points",
    )(planes, in_hbm(table), *own, *far)


def second_far_points(planes, table, far, first):
    return pl.pallas_call(
        second_far_kernel,
        out_shape=(
            jax.ShapeDtypeStruct((CHUNKS, 2 * ITEMS, G_DEV), BF16),
            jax.ShapeDtypeStruct(LOW, BF16),
            jax.ShapeDtypeStruct((16, 128), F32),
        ),
        in_specs=[VMEM, HBM] + [VMEM] * 3,
        scratch_shapes=X_SCRATCH,
        compiler_params=pltpu.CompilerParams(vmem_limit_bytes=16 << 20),
        cost_estimate=pl.CostEstimate(
            flops=100_000_000, bytes_accessed=100_000, transcendentals=0
        ),
        name="second_far_points",
    )(planes, in_hbm(table), *far, first)


def second_own_points(low, own):
    return pl.pallas_call(
        second_own_kernel,
        out_shape=OWN,
        compiler_params=pltpu.CompilerParams(vmem_limit_bytes=16 << 20),
        cost_estimate=pl.CostEstimate(
            flops=2_400_000_000, bytes_accessed=1_300_000, transcendentals=0
        ),
        name="second_own_points",
    )(low, *own)


def split_kernel(own0_ref, own1_ref, far_ref, block_ref, out_ref):
    real, imag = [], []
    for chunk, own_ref in enumerate((own0_ref, own1_ref)):
        own_r = own_ref[:ITEMS, :]
        own_i = own_ref[ITEMS:, :]
        far_r = far_ref[chunk, :ITEMS, :].astype(F32)
        far_i = far_ref[chunk, ITEMS:, :].astype(F32)
        real += [own_r + far_r, own_i + far_i]
        imag += [own_i - far_i, far_r - own_r]
    pairs = jnp.concatenate(real + imag, axis=0).astype(BF16)
    block = block_ref[...].astype(BF16)
    for band in range(16):
        out_ref[band, :32, :] = pairs[:, band * 128 : (band + 1) * 128]
        out_ref[band, 32:, :] = block


def split_pairs(own0, own1, far, block):
    return pl.pallas_call(
        split_kernel,
        out_shape=jax.ShapeDtypeStruct((16, 48, 128), BF16),
        compiler_params=pltpu.CompilerParams(vmem_limit_bytes=4 << 20),
        cost_estimate=pl.CostEstimate(
            flops=1_000_000, bytes_accessed=500_000, transcendentals=0
        ),
        name="split",
    )(own0, own1, far, block)


def block_kernel(v0, v1, v2, v3, c0, c1, c2, c3, lane_ref, row_ref, out_ref):
    waves = (v0, v1, v2, v3)
    for chunk, waves_c in enumerate(((c0, c1), (c2, c3))):
        for half in range(2):
            for item in range(ITEMS):
                pair = waves[2 * (item // 2) + half][...] * waves_c[item % 2][...]
                sums = jnp.dot(pair, lane_ref[...], preferred_element_type=F32) * row_ref[...]
                total = sums.sum(axis=0, keepdims=True)
                high = total.astype(BF16).astype(F32)
                index = (chunk * 2 + half) * ITEMS + item
                out_ref[index : index + 1, :] = high
                out_ref[16 + index : 17 + index, :] = total - high


def block_sums(v, c, lanes, rows):
    return pl.pallas_call(
        block_kernel,
        out_shape=jax.ShapeDtypeStruct((32, 128), F32),
        compiler_params=pltpu.CompilerParams(vmem_limit_bytes=4 << 20),
        cost_estimate=pl.CostEstimate(
            flops=10_000_000, bytes_accessed=100_000, transcendentals=0
        ),
        name="block",
    )(*v, *c, lanes, rows)


def sum_kernel(pairs_ref, weight_ref, column_ref, out_ref):
    pairs = 16 * 16
    block = pairs_ref[:, 32:, :].reshape(pairs, 128)
    total = None
    for part in range(2):
        left = pairs_ref[:, 16 * part : 16 * (part + 1), :].reshape(pairs, 128)
        columns = jnp.dot(block, column_ref[part], preferred_element_type=F32)
        right = (columns * weight_ref[...]).astype(BF16)
        term = lax.dot_general(
            left, right, (((0,), (0,)), ((), ())), preferred_element_type=F32
        )
        total = term if total is None else total + term
    out_ref[...] = total


def wave_rows(wave):
    return wave.reshape(X6, Y6, Y16, N).transpose(0, 2, 1, 3).reshape(X6 * Y16, Y6 * N)


def spread(cells, masks):
    arrived = [lax.ppermute(cells, COL, [(k, k ^ mask) for k in range(SLABS)]) for mask in masks]
    return sum(arrived, cells)


def cosine(phase):
    return jnp.cos((phase % N).astype(F32) * (2.0 * math.pi / N))


def per_device(
    valence_wave,
    conduction_wave,
    valence_index,
    occupied_energy,
    conduction_energy,
    frequency,
    gvec_cell,
    block_cell,
):
    col = lax.axis_index(COL)
    wave_v = wave_rows(valence_wave)
    wave_c = wave_rows(conduction_wave)
    v = [wave_v]
    for mask in (1, 2, 3):
        v.append(lax.ppermute(wave_v, VGROUP, [(i, i ^ mask) for i in range(4)]))
    ahead = [(i, (i + 1) % 4) for i in range(4)]
    behind = [(i, (i + 3) % 4) for i in range(4)]
    c = [wave_c, lax.ppermute(wave_c, "z1", ahead)]

    spots = jnp.arange(128, dtype=jnp.int32)
    cells = jnp.where(spots % NBLOCK == col, block_cell[0], 0)
    cells = spread(cells, (1, 2, 3))

    tables = (lane_table(), row_table(), twiddle_table())
    through = (wave_c, c[1], cells[None], gvec_cell.reshape(16, 128))
    planes0, wave_c, wave_c1, cells, list_cell = planes_of(v, c, tables, through=through)
    sent0 = lax.all_to_all(planes0, COL, 0, 0, tiled=True)
    c.append(lax.ppermute(wave_c, "z1", behind))
    c.append(lax.ppermute(wave_c1, "z1", ahead))

    cells = spread(cells[0], (4, 8, 12))
    block_x = cells // 576
    block_y = spots % NBLOCK * 6 + cells // N % 6
    block_z = cells % N
    group = spots // NBLOCK - 2
    quarter = N // 4
    lane = jnp.arange(Y6 * N, dtype=jnp.int32)[:, None]
    lanes = cosine(
        lane // N * 16 * block_y + lane % N * block_z + jnp.where(group % 2 == 1, quarter, 0)
    ).astype(BF16)
    row = jnp.arange(X6 * Y16, dtype=jnp.int32)[:, None]
    shift = jnp.where(group == 1, 3 * quarter, jnp.where(group == 2, quarter, 0))
    rows = cosine((row // Y16 + X6 * col) * block_x + row % Y16 * block_y + shift)
    scale = 1.0 / (N * math.sqrt(N))
    rows = jnp.where((group >= 0) & (group < 4), rows * scale, 0.0)
    block = block_sums(v, c, lanes, rows)
    (planes1,) = planes_of(v, c[2:], tables, block=(block,))
    sent1 = lax.all_to_all(planes1, COL, 0, 0, tiled=True)

    mirror_of = [(k, SLABS - 1 - k) for k in range(SLABS)]
    far_cell = lax.ppermute(list_cell, COL, mirror_of).reshape(G_DEV)
    far_x, far_y, far_z = far_cell // 576, far_cell // N % 6, far_cell % N
    own = ((gvec_cell % 576)[None], (gvec_cell // 576)[None])
    far = (((6 - far_y) * N + (N - far_z) % N)[None], ((N - far_x) % N)[None])

    pair_v, pair_c = pair_table()
    occupied = jnp.arange(occupied_energy.shape[0], dtype=jnp.int32)
    valence_energy = jnp.sum(
        jnp.where(valence_index[:, None] == occupied[None, :], occupied_energy[None, :], 0.0),
        axis=1,
    )
    count_v, count_c = valence_index.shape[0], conduction_energy.shape[0]
    energy_v = jnp.sum(
        jnp.where(pair_v[:, None] == np.arange(count_v)[None], valence_energy[None], 0.0), axis=1
    )
    energy_c = jnp.sum(
        jnp.where(pair_c[:, None] == np.arange(count_c)[None], conduction_energy[None], 0.0),
        axis=1,
    )
    gap = (energy_c - energy_v)[:, None]
    omega = jnp.repeat(frequency, 2 * NBLOCK)[None]
    weight = -4.0 * gap / (gap * gap + omega * omega) * (1.0 / math.sqrt(count_v * count_c))

    own0, far0 = first_points(sent0, x_table(), own, far)
    mirrored, low, columns = second_far_points(sent1, x_table(), far, far0)
    mirrored = lax.ppermute(mirrored, COL, mirror_of)
    own1 = second_own_points(low, own)
    pairs = split_pairs(own0, own1, mirrored, columns)
    pairs = lax.all_to_all(pairs, BAND, 0, 0, tiled=True)
    return pl.pallas_call(
        sum_kernel,
        out_shape=jax.ShapeDtypeStruct((128, 128), F32),
        compiler_params=pltpu.CompilerParams(vmem_limit_bytes=4 << 20),
        name="pair_sum",
    )(pairs, weight, column_tables())


def solution(mesh):
    fine = Mesh(
        mesh.devices.reshape(4, 2, 2, 4, 2, 2), ("z1", "z0", "yl", "x", "yh", "co")
    )
    return jax.shard_map(
        per_device,
        mesh=fine,
        in_specs=(
            P(BAND, COL, None),
            P(BAND, COL, None),
            P(),
            P(),
            P(),
            P(),
            P(COL),
            P(COL),
        ),
        out_specs=P(COL + BAND, None),
        check_vma=False,
    )
```

```python
import functools
import math

import jax
import jax.numpy as jnp
import ml_dtypes
import numpy as np
from jax import lax
from jax.experimental import pallas as pl
from jax.experimental.pallas import tpu as pltpu
from jax.sharding import Mesh
from jax.sharding import PartitionSpec as P

BF16 = jnp.bfloat16
F32 = jnp.float32

N = 96
SLABS = 16
X6 = 6
Y6 = 6
Y16 = 16
K7 = 7
FLAT = K7 * N
WIDE = 768
GROUPS = (
    (((0, 0), (0, 1)),),
    (((1, 0), (1, 1), (0, 3), (1, 3)), ((0, 2), (1, 2))),
)
ITEM_LIST = [item for chunk in GROUPS for group in chunk for item in group]
SPARE = 640
G_DEV = 2048
NBLOCK = 16
TILE = 512

ITEM_ROWS = 2 * X6
BAND = ("z1", "z0", "yl")
VGROUP = ("z0", "yl")
COL = ("x", "yh", "co")


def unit(phase, period):
    angle = 2.0 * np.pi * (np.asarray(phase) % period) / period
    return np.cos(angle), -np.sin(angle)


def bf16(table):
    return np.asarray(table, np.float32).astype(ml_dtypes.bfloat16)


@functools.cache
def lane_table():
    y6, z = np.divmod(np.arange(Y6 * N), N)
    k7, kz = np.divmod(np.arange(FLAT), N)
    phase = 16 * y6[:, None] * k7[None, :] + z[:, None] * kz[None, :]
    cosine, sine = unit(phase, N)
    table = np.zeros((Y6 * N, 2 * WIDE))
    table[:, :FLAT] = cosine
    table[:, WIDE : WIDE + FLAT] = sine
    return bf16(table)


@functools.cache
def twiddle_table():
    k7 = np.arange(FLAT) // N
    cosine, sine = unit(np.arange(Y16)[:, None] * k7[None, :], N)
    table = np.zeros((2, Y16, WIDE), np.float32)
    table[0, :, :FLAT] = cosine / N
    table[1, :, :FLAT] = sine / N
    return table


@functools.cache
def row_table(items):
    table = np.zeros((SLABS, items, 2, X6, 2, items, X6, Y16))
    cosine, sine = unit(np.arange(SLABS)[:, None] * np.arange(Y16)[None, :], SLABS)
    for item in range(items):
        for x in range(X6):
            table[:, item, 0, x, 0, item, x] = cosine
            table[:, item, 0, x, 1, item, x] = -sine
            table[:, item, 1, x, 0, item, x] = sine
            table[:, item, 1, x, 1, item, x] = cosine
    return bf16(table.reshape(SLABS * items * 2 * X6, 2 * items * X6 * Y16))


@functools.cache
def x_table(items):
    table = np.zeros((2, items, N, SLABS, items, 2, X6))
    cosine, sine = unit(np.arange(N)[:, None] * np.arange(N)[None, :], N)
    cosine = (cosine * 0.5 / math.sqrt(N)).reshape(N, SLABS, X6)
    sine = (sine * 0.5 / math.sqrt(N)).reshape(N, SLABS, X6)
    for item in range(items):
        table[0, item, :, :, item, 0] = cosine
        table[0, item, :, :, item, 1] = -sine
        table[1, item, :, :, item, 0] = sine
        table[1, item, :, :, item, 1] = cosine
    return bf16(table.reshape(2 * items * N, SLABS * items * 2 * X6))


@functools.cache
def pair_table():
    valence, conduction = [], []
    for band in range(16):
        z1, group = divmod(band, 4)
        for half in range(2):
            for pair, slot in ITEM_LIST:
                valence.append(z1 * 4 + (group ^ (2 * pair + half)))
                conduction.append((z1 - slot) % 4 * 4 + group)
    return np.array(valence), np.array(conduction)


@functools.cache
def column_tables():
    tables = np.zeros((2, 128, 4, 2, NBLOCK))
    m = np.arange(NBLOCK)
    tables[0, 32 + m, :, 0, m] = 1.0
    tables[0, 64 + m, :, 1, m] = -1.0
    tables[1, 64 + m, :, 0, m] = 1.0
    tables[1, 32 + m, :, 1, m] = 1.0
    return bf16(tables.reshape(2, 128, 128))


VMEM = pl.BlockSpec(memory_space=pltpu.VMEM)
HBM = pl.BlockSpec(memory_space=pltpu.HBM)
ANY = pl.BlockSpec(memory_space=pl.ANY)
SLAB_CUTS = 4


def plane_kernel(*refs, groups, slots, through):
    refs = list(refs)
    take = lambda count: [refs.pop(0) for _ in range(count)]
    waves = dict(zip(slots[0], take(len(slots[0]))))
    waves_c = dict(zip(slots[1], take(len(slots[1]))))
    lane_ref, twiddle_ref = take(2)
    row_refs = take(len(groups))
    kept = take(through)
    block_refs = take(len(refs) - 4 - through - len(groups))
    (out_ref,) = take(1)
    kept_out = take(through)
    low_refs = take(len(groups))
    slab_ref, slab_sems, keep_sems = refs
    moves = [
        pltpu.make_async_copy(source, target, keep_sems.at[i])
        for i, (source, target) in enumerate(zip(kept, kept_out))
    ]
    for move in moves:
        move.start()
    rows = X6 * Y16
    twiddle_c = twiddle_ref[0][None]
    twiddle_s = twiddle_ref[1][None]
    for group, low_ref in zip(groups, low_refs):
        for index, (pair, slot) in enumerate(group):
            wave_c = waves_c[slot][...]
            pairs = jnp.concatenate(
                [waves[2 * pair][...] * wave_c, waves[2 * pair + 1][...] * wave_c], axis=0
            )
            moved = jnp.dot(pairs, lane_ref[...], preferred_element_type=F32)
            real = moved[:rows, :WIDE] - moved[rows:, WIDE:]
            imag = moved[:rows, WIDE:] + moved[rows:, :WIDE]
            real = real.reshape(X6, Y16, WIDE)
            imag = imag.reshape(X6, Y16, WIDE)
            turned_r = real * twiddle_c - imag * twiddle_s
            turned_i = real * twiddle_s + imag * twiddle_c
            low_ref[index * rows : (index + 1) * rows, :] = turned_r.reshape(rows, WIDE).astype(
                BF16
            )
            index += len(group)
            low_ref[index * rows : (index + 1) * rows, :] = turned_i.reshape(rows, WIDE).astype(
                BF16
            )
    count = SLABS // SLAB_CUTS
    for part in range(SLAB_CUTS):
        slabs = slice(part * count, (part + 1) * count)
        first = 0
        for group, low_ref, row_ref in zip(groups, low_refs, row_refs):
            size = len(group) * ITEM_ROWS
            planes = jnp.dot(
                row_ref[part * count * size : (part + 1) * count * size, :],
                low_ref[...],
                preferred_element_type=F32,
            ).reshape(count, size, WIDE)
            slab_ref[slabs, first : first + size, :] = planes.astype(BF16)
            if first == 0 and block_refs:
                spare = planes[:, :32, SPARE:] + block_refs[0][...][None]
                slab_ref[slabs, :32, SPARE:] = spare.astype(BF16)
            first += size
        window = pl.ds(part * count, count)
        moves.append(
            pltpu.make_async_copy(slab_ref.at[window], out_ref.at[window], slab_sems.at[part])
        )
        moves[-1].start()
    for move in moves:
        move.wait()


def planes_of(chunk, v, c, through=(), block=()):
    groups = GROUPS[chunk]
    items = [item for group in groups for item in group]
    slots_v = sorted({2 * pair + half for pair, _ in items for half in range(2)})
    slots_c = sorted({slot for _, slot in items})
    rows = len(items) * ITEM_ROWS
    tables = [row_table(len(group)) for group in groups]
    return pl.pallas_call(
        functools.partial(
            plane_kernel, groups=groups, slots=(slots_v, slots_c), through=len(through)
        ),
        out_shape=[
            pltpu.HBM((SLABS, rows, WIDE), BF16),
            *(pltpu.HBM(x.shape, x.dtype) for x in through),
        ],
        in_specs=[VMEM] * (len(slots_v) + len(slots_c) + 2 + len(tables))
        + [ANY] * len(through)
        + [VMEM] * len(block),
        out_specs=[HBM] * (1 + len(through)),
        scratch_shapes=[
            *(pltpu.VMEM((2 * len(group) * X6 * Y16, WIDE), BF16) for group in groups),
            pltpu.VMEM((SLABS, rows, WIDE), BF16),
            pltpu.SemaphoreType.DMA((SLAB_CUTS,)),
            pltpu.SemaphoreType.DMA((max(len(through), 1),)),
        ],
        compiler_params=pltpu.CompilerParams(vmem_limit_bytes=16 << 20),
        cost_estimate=pl.CostEstimate(
            flops=50_000_000, bytes_accessed=100_000, transcendentals=0
        ),
        name="planes",
    )(
        *(v[slot] for slot in slots_v),
        *(c[slot] for slot in slots_c),
        lane_table(),
        twiddle_table(),
        *tables,
        *through,
        *block,
    )


def pick(density_ref, flat_ref, kx_ref, store):
    rows = density_ref.shape[0]

    def body(step, carry):
        lanes = pl.ds(pl.multiple_of(step * TILE, TILE), TILE)
        spot = lax.broadcasted_iota(jnp.int32, (WIDE, TILE), 0)
        chosen = jnp.where(spot == flat_ref[:, lanes], 1.0, 0.0).astype(BF16)
        values = jnp.dot(density_ref[...], chosen, preferred_element_type=F32)
        kx = lax.broadcasted_iota(jnp.int32, (N, TILE), 0) == kx_ref[:, lanes]
        values = jnp.where(kx[None], values.reshape(rows // N, N, TILE), 0.0)
        store(lanes, values.sum(axis=1))
        return carry

    lax.fori_loop(0, G_DEV // TILE, body, 0)


def transform_x(chunk, t_ref, x_refs, low):
    first, place = 0, 0
    for group, x_ref in zip(GROUPS[chunk], x_refs):
        size = len(group) * ITEM_ROWS
        planes = t_ref[:, first : first + size, :]
        if size % 16:
            planes = planes.astype(F32)
        planes = planes.reshape(SLABS * size, WIDE).astype(BF16)
        rows = 2 * len(group) * N
        low[place : place + rows, :] = jnp.dot(
            x_ref[...], planes, preferred_element_type=F32
        ).astype(BF16)
        first += size
        place += rows


def first_kernel(
    t_ref, x_ref, own_ref, own_kx_ref, far_ref, far_kx_ref, own_out, far_out, low
):
    transform_x(0, t_ref, (x_ref,), low)

    def store_far(lanes, values):
        far_out[:, lanes] = values.astype(BF16)

    def store_own(lanes, values):
        own_out[:, lanes] = values

    pick(low, far_ref, far_kx_ref, store_far)
    pick(low, own_ref, own_kx_ref, store_own)


def second_far_kernel(
    t_ref, x0_ref, x1_ref, far_ref, far_kx_ref, first_ref, far_out, low, block_out
):
    transform_x(1, t_ref, (x0_ref, x1_ref), low)
    rows = first_ref.shape[0]
    far_out[:rows, :] = first_ref[...]

    def store_far(lanes, values):
        far_out[rows:, lanes] = values.astype(BF16)

    pick(low, far_ref, far_kx_ref, store_far)
    spare = t_ref[:, :32, SPARE:].astype(F32).sum(axis=0)
    spare = spare[:16] + spare[16:]
    spare = spare + pltpu.roll(spare, 128 - NBLOCK, 1)
    block_out[...] = spare


def second_own_kernel(low, own_ref, own_kx_ref, own_out):
    def store_own(lanes, values):
        own_out[:, lanes] = values

    pick(low, own_ref, own_kx_ref, store_own)


FIRST, SECOND = (2 * sum(len(group) for group in chunk) for chunk in GROUPS)


def first_points(planes, own, far):
    return pl.pallas_call(
        first_kernel,
        out_shape=(
            jax.ShapeDtypeStruct((FIRST, G_DEV), F32),
            jax.ShapeDtypeStruct((FIRST, G_DEV), BF16),
        ),
        scratch_shapes=[pltpu.VMEM((FIRST * N, WIDE), BF16)],
        compiler_params=pltpu.CompilerParams(vmem_limit_bytes=16 << 20),
        cost_estimate=pl.CostEstimate(
            flops=100_000_000, bytes_accessed=100_000, transcendentals=0
        ),
        name="first_points",
    )(planes, x_table(FIRST // 2), *own, *far)


def second_far_points(planes, far, first):
    return pl.pallas_call(
        second_far_kernel,
        out_shape=(
            jax.ShapeDtypeStruct((FIRST + SECOND, G_DEV), BF16),
            jax.ShapeDtypeStruct((SECOND * N, WIDE), BF16),
            jax.ShapeDtypeStruct((16, 128), F32),
        ),
        compiler_params=pltpu.CompilerParams(vmem_limit_bytes=16 << 20),
        cost_estimate=pl.CostEstimate(
            flops=100_000_000, bytes_accessed=100_000, transcendentals=0
        ),
        name="second_far_points",
    )(planes, *(x_table(len(group)) for group in GROUPS[1]), *far, first)


def second_own_points(low, own):
    return pl.pallas_call(
        second_own_kernel,
        out_shape=jax.ShapeDtypeStruct((SECOND, G_DEV), F32),
        compiler_params=pltpu.CompilerParams(vmem_limit_bytes=16 << 20),
        cost_estimate=pl.CostEstimate(
            flops=2_400_000_000, bytes_accessed=1_300_000, transcendentals=0
        ),
        name="second_own_points",
    )(low, *own)


def split_kernel(own0_ref, own1_ref, far_ref, block_ref, out_ref):
    parts = [[], [], [], []]
    first, place = 0, 0
    for own_ref, chunk in zip((own0_ref, own1_ref), GROUPS):
        first = 0
        for group in chunk:
            size = len(group)
            own_r = own_ref[first : first + size, :]
            own_i = own_ref[first + size : first + 2 * size, :]
            far_r = far_ref[place : place + size, :].astype(F32)
            far_i = far_ref[place + size : place + 2 * size, :].astype(F32)
            parts[0].append(own_r + far_r)
            parts[1].append(own_i + far_i)
            parts[2].append(own_i - far_i)
            parts[3].append(far_r - own_r)
            first += 2 * size
            place += 2 * size
    pairs = jnp.concatenate(sum(parts, []), axis=0).astype(BF16)
    block = block_ref[...].astype(BF16)
    for band in range(16):
        out_ref[band, :32, :] = pairs[:, band * 128 : (band + 1) * 128]
        out_ref[band, 32:, :] = block


def split_pairs(own0, own1, far, block):
    return pl.pallas_call(
        split_kernel,
        out_shape=jax.ShapeDtypeStruct((16, 48, 128), BF16),
        compiler_params=pltpu.CompilerParams(vmem_limit_bytes=8 << 20),
        cost_estimate=pl.CostEstimate(
            flops=1_000_000, bytes_accessed=500_000, transcendentals=0
        ),
        name="split",
    )(own0, own1, far, block)


def block_kernel(v0, v1, v2, v3, c0, c1, c2, c3, lane_ref, row_ref, out_ref):
    waves = (v0, v1, v2, v3)
    waves_c = (c0, c1, c2, c3)
    for half in range(2):
        for item, (pair, slot) in enumerate(ITEM_LIST):
            product = waves[2 * pair + half][...] * waves_c[slot][...]
            sums = jnp.dot(product, lane_ref[...], preferred_element_type=F32) * row_ref[...]
            total = sums.sum(axis=0, keepdims=True)
            high = total.astype(BF16).astype(F32)
            index = half * len(ITEM_LIST) + item
            out_ref[index : index + 1, :] = high
            out_ref[16 + index : 17 + index, :] = total - high


def block_sums(v, c, lanes, rows):
    return pl.pallas_call(
        block_kernel,
        out_shape=jax.ShapeDtypeStruct((32, 128), F32),
        compiler_params=pltpu.CompilerParams(vmem_limit_bytes=4 << 20),
        cost_estimate=pl.CostEstimate(
            flops=10_000_000, bytes_accessed=100_000, transcendentals=0
        ),
        name="block",
    )(*v, *c, lanes, rows)


def sum_kernel(pairs_ref, weight_ref, column_ref, out_ref):
    pairs = 16 * 16
    block = pairs_ref[:, 32:, :].reshape(pairs, 128)
    total = None
    for part in range(2):
        left = pairs_ref[:, 16 * part : 16 * (part + 1), :].reshape(pairs, 128)
        columns = jnp.dot(block, column_ref[part], preferred_element_type=F32)
        right = (columns * weight_ref[...]).astype(BF16)
        term = lax.dot_general(
            left, right, (((0,), (0,)), ((), ())), preferred_element_type=F32
        )
        total = term if total is None else total + term
    out_ref[...] = total


def wave_rows(wave):
    return wave.reshape(X6, Y6, Y16, N).transpose(0, 2, 1, 3).reshape(X6 * Y16, Y6 * N)


def spread(cells, masks):
    arrived = [lax.ppermute(cells, COL, [(k, k ^ mask) for k in range(SLABS)]) for mask in masks]
    return sum(arrived, cells)


def cosine(phase):
    return jnp.cos((phase % N).astype(F32) * (2.0 * math.pi / N))


def per_device(
    valence_wave,
    conduction_wave,
    valence_index,
    occupied_energy,
    conduction_energy,
    frequency,
    gvec_cell,
    block_cell,
):
    col = lax.axis_index(COL)
    wave_v = wave_rows(valence_wave)
    wave_c = wave_rows(conduction_wave)
    twin = [[(i, i ^ mask) for i in range(4)] for mask in range(4)]
    ahead = [(i, (i + 1) % 4) for i in range(4)]
    behind = [(i, (i + 3) % 4) for i in range(4)]
    v = [wave_v, lax.ppermute(wave_v, VGROUP, twin[1])]
    c = [wave_c, lax.ppermute(wave_c, "z1", ahead)]

    spots = jnp.arange(128, dtype=jnp.int32)
    cells = jnp.where(spots % NBLOCK == col, block_cell[0], 0)
    cells = spread(cells, (1, 2, 3))
    cells = spread(cells, (4, 8, 12))

    mirror_of = [(k, SLABS - 1 - k) for k in range(SLABS)]
    far_cell = lax.ppermute(gvec_cell, COL, mirror_of).reshape(16, 128)
    planes0, far_cell, *passed = planes_of(0, v, c, through=(far_cell, *v, *c))
    sent0 = lax.all_to_all(planes0, COL, 0, 0, tiled=True)
    v.append(lax.ppermute(passed[0], VGROUP, twin[2]))
    v.append(lax.ppermute(passed[1], VGROUP, twin[2]))
    c.append(lax.ppermute(passed[3], "z1", ahead))
    c.append(lax.ppermute(passed[2], "z1", behind))

    far_cell = far_cell.reshape(G_DEV)
    far_x, far_y, far_z = far_cell // 576, far_cell // N % 6, far_cell % N
    own = ((gvec_cell % 576)[None], (gvec_cell // 576)[None])
    far = (((6 - far_y) * N + (N - far_z) % N)[None], ((N - far_x) % N)[None])

    block_x = cells // 576
    block_y = spots % NBLOCK * 6 + cells // N % 6
    block_z = cells % N
    group = spots // NBLOCK - 2
    quarter = N // 4
    lane = jnp.arange(Y6 * N, dtype=jnp.int32)[:, None]
    lanes = cosine(
        lane // N * 16 * block_y + lane % N * block_z + jnp.where(group % 2 == 1, quarter, 0)
    ).astype(BF16)
    row = jnp.arange(X6 * Y16, dtype=jnp.int32)[:, None]
    shift = jnp.where(group == 1, 3 * quarter, jnp.where(group == 2, quarter, 0))
    rows = cosine((row // Y16 + X6 * col) * block_x + row % Y16 * block_y + shift)
    scale = 1.0 / (N * math.sqrt(N))
    rows = jnp.where((group >= 0) & (group < 4), rows * scale, 0.0)
    block = block_sums(v, c, lanes, rows)
    (planes1,) = planes_of(1, v, c, block=(block,))
    sent1 = lax.all_to_all(planes1, COL, 0, 0, tiled=True)

    pair_v, pair_c = pair_table()
    occupied = jnp.arange(occupied_energy.shape[0], dtype=jnp.int32)
    valence_energy = jnp.sum(
        jnp.where(valence_index[:, None] == occupied[None, :], occupied_energy[None, :], 0.0),
        axis=1,
    )
    count_v, count_c = valence_index.shape[0], conduction_energy.shape[0]
    energy_v = jnp.sum(
        jnp.where(pair_v[:, None] == np.arange(count_v)[None], valence_energy[None], 0.0), axis=1
    )
    energy_c = jnp.sum(
        jnp.where(pair_c[:, None] == np.arange(count_c)[None], conduction_energy[None], 0.0),
        axis=1,
    )
    gap = (energy_c - energy_v)[:, None]
    omega = jnp.repeat(frequency, 2 * NBLOCK)[None]
    weight = -4.0 * gap / (gap * gap + omega * omega) * (1.0 / math.sqrt(count_v * count_c))

    own0, far0 = first_points(sent0, own, far)
    mirrored, low, columns = second_far_points(sent1, far, far0)
    mirrored = lax.ppermute(mirrored, COL, mirror_of)
    own1 = second_own_points(low, own)
    pairs = split_pairs(own0, own1, mirrored, columns)
    pairs = lax.all_to_all(pairs, BAND, 0, 0, tiled=True)
    return pl.pallas_call(
        sum_kernel,
        out_shape=jax.ShapeDtypeStruct((128, 128), F32),
        compiler_params=pltpu.CompilerParams(vmem_limit_bytes=4 << 20),
        name="pair_sum",
    )(pairs, weight, column_tables())


def solution(mesh):
    fine = Mesh(
        mesh.devices.reshape(4, 2, 2, 4, 2, 2), ("z1", "z0", "yl", "x", "yh", "co")
    )
    return jax.shard_map(
        per_device,
        mesh=fine,
        in_specs=(
            P(BAND, COL, None),
            P(BAND, COL, None),
            P(),
            P(),
            P(),
            P(),
            P(COL),
            P(COL),
        ),
        out_specs=P(COL + BAND, None),
        check_vma=False,
    )
```

```python
import functools
import math

import jax
import jax.numpy as jnp
import ml_dtypes
import numpy as np
from jax import lax
from jax.experimental import pallas as pl
from jax.experimental.pallas import tpu as pltpu
from jax.sharding import Mesh
from jax.sharding import PartitionSpec as P

BF16 = jnp.bfloat16
F32 = jnp.float32

N = 96
SLABS = 16
X6 = 6
Y6 = 6
Y16 = 16
K7 = 7
FLAT = K7 * N
WIDE = 768
GROUPS = (((0, 1, 7),), ((2, 6, 3), (5, 4)))
SLOTS = [slot for chunk in GROUPS for group in chunk for slot in group]
SPARE = 640
G_DEV = 2048
NBLOCK = 16
TILE = 512

BAND = ("z", "yl")
COL = ("x", "yh", "co")


def unit(phase, period):
    angle = 2.0 * np.pi * (np.asarray(phase) % period) / period
    return np.cos(angle), -np.sin(angle)


def bf16(table):
    return np.asarray(table, np.float32).astype(ml_dtypes.bfloat16)


@functools.cache
def lane_table():
    y6, z = np.divmod(np.arange(Y6 * N), N)
    k7, kz = np.divmod(np.arange(FLAT), N)
    phase = 16 * y6[:, None] * k7[None, :] + z[:, None] * kz[None, :]
    cosine, sine = unit(phase, N)
    table = np.zeros((Y6 * N, 2 * WIDE))
    table[:, :FLAT] = cosine
    table[:, WIDE : WIDE + FLAT] = sine
    return bf16(table)


@functools.cache
def twiddle_table():
    k7 = np.arange(FLAT) // N
    cosine, sine = unit(np.arange(Y16)[:, None] * k7[None, :], N)
    table = np.zeros((2, Y16, WIDE), np.float32)
    table[0, :, :FLAT] = cosine / N
    table[1, :, :FLAT] = sine / N
    return table


def slab_rows(items):
    return -(-items * 2 * X6 // 8) * 8


@functools.cache
def row_table(items):
    table = np.zeros((SLABS, items, 2, X6, 2, items, X6, Y16))
    cosine, sine = unit(np.arange(SLABS)[:, None] * np.arange(Y16)[None, :], SLABS)
    for item in range(items):
        for x in range(X6):
            table[:, item, 0, x, 0, item, x] = cosine
            table[:, item, 0, x, 1, item, x] = -sine
            table[:, item, 1, x, 0, item, x] = sine
            table[:, item, 1, x, 1, item, x] = cosine
    rows = items * 2 * X6
    whole = np.zeros((SLABS, slab_rows(items), 2 * items * X6 * Y16))
    whole[:, :rows] = table.reshape(SLABS, rows, -1)
    return bf16(whole.reshape(SLABS * slab_rows(items), -1))


@functools.cache
def x_table(items):
    table = np.zeros((2, items, N, SLABS, items, 2, X6))
    cosine, sine = unit(np.arange(N)[:, None] * np.arange(N)[None, :], N)
    cosine = (cosine * 0.5 / math.sqrt(N)).reshape(N, SLABS, X6)
    sine = (sine * 0.5 / math.sqrt(N)).reshape(N, SLABS, X6)
    for item in range(items):
        table[0, item, :, :, item, 0] = cosine
        table[0, item, :, :, item, 1] = -sine
        table[1, item, :, :, item, 0] = sine
        table[1, item, :, :, item, 1] = cosine
    rows = items * 2 * X6
    whole = np.zeros((2 * items * N, SLABS, slab_rows(items)))
    whole[:, :, :rows] = table.reshape(2 * items * N, SLABS, rows)
    return bf16(whole.reshape(2 * items * N, -1))


@functools.cache
def pair_table():
    valence, conduction = [], []
    for band in range(16):
        z, yl = divmod(band, 2)
        for half in range(2):
            for slot in SLOTS:
                valence.append(z * 2 + (yl ^ half))
                conduction.append((z - slot) % 8 * 2 + yl)
    return np.array(valence), np.array(conduction)


@functools.cache
def column_tables():
    tables = np.zeros((2, 128, 4, 2, NBLOCK))
    m = np.arange(NBLOCK)
    tables[0, 32 + m, :, 0, m] = 1.0
    tables[0, 64 + m, :, 1, m] = -1.0
    tables[1, 64 + m, :, 0, m] = 1.0
    tables[1, 32 + m, :, 1, m] = 1.0
    return bf16(tables.reshape(2, 128, 128))


VMEM = pl.BlockSpec(memory_space=pltpu.VMEM)
HBM = pl.BlockSpec(memory_space=pltpu.HBM)
ANY = pl.BlockSpec(memory_space=pl.ANY)
SLAB_CUTS = 4


def plane_kernel(*refs, groups, place, through):
    refs = list(refs)
    take = lambda count: [refs.pop(0) for _ in range(count)]
    v0_ref, v1_ref = take(2)
    c_refs = [take(len(group)) for group in groups]
    lane_ref, twiddle_ref, extra_ref = take(3)
    row_refs = take(len(groups))
    kept = take(through)
    (out_ref,) = take(1)
    kept_out = take(through)
    low_refs = take(len(groups))
    slab_ref, slab_sems, keep_sems = refs
    moves = [
        pltpu.make_async_copy(source, target, keep_sems.at[i])
        for i, (source, target) in enumerate(zip(kept, kept_out))
    ]
    for move in moves:
        move.start()
    rows = X6 * Y16
    twiddle_c = twiddle_ref[0][None]
    twiddle_s = twiddle_ref[1][None]
    for group, waves_c, low_ref in zip(groups, c_refs, low_refs):
        for index, c_ref in enumerate(waves_c):
            wave_c = c_ref[...]
            pairs = jnp.concatenate([v0_ref[...] * wave_c, v1_ref[...] * wave_c], axis=0)
            moved = jnp.dot(pairs, lane_ref[...], preferred_element_type=F32)
            real = moved[:rows, :WIDE] - moved[rows:, WIDE:]
            imag = moved[:rows, WIDE:] + moved[rows:, :WIDE]
            real = real.reshape(X6, Y16, WIDE)
            imag = imag.reshape(X6, Y16, WIDE)
            turned_r = real * twiddle_c - imag * twiddle_s
            turned_i = real * twiddle_s + imag * twiddle_c
            low_ref[index * rows : (index + 1) * rows, :] = turned_r.reshape(rows, WIDE).astype(
                BF16
            )
            index += len(group)
            low_ref[index * rows : (index + 1) * rows, :] = turned_i.reshape(rows, WIDE).astype(
                BF16
            )
    count = SLABS // SLAB_CUTS
    extra = extra_ref[...]
    for part in range(SLAB_CUTS):
        slabs = slice(part * count, (part + 1) * count)
        first = 0
        for group, low_ref, row_ref in zip(groups, low_refs, row_refs):
            size = slab_rows(len(group))
            planes = jnp.dot(
                row_ref[part * count * size : (part + 1) * count * size, :],
                low_ref[...],
                preferred_element_type=F32,
            ).reshape(count, size, WIDE)
            slab_ref[slabs, first : first + size, :] = planes.astype(BF16)
            if first == place:
                spare = planes[:, : extra.shape[0], SPARE:] + extra[None]
                slab_ref[slabs, first : first + extra.shape[0], SPARE:] = spare.astype(BF16)
            first += size
        window = pl.ds(part * count, count)
        moves.append(
            pltpu.make_async_copy(slab_ref.at[window], out_ref.at[window], slab_sems.at[part])
        )
        moves[-1].start()
    for move in moves:
        move.wait()


PLACE = slab_rows(len(GROUPS[1][0]))


def planes_of(chunk, v, c, extra, through=()):
    groups = GROUPS[chunk]
    slots = [slot for group in groups for slot in group]
    rows = sum(slab_rows(len(group)) for group in groups)
    tables = [row_table(len(group)) for group in groups]
    return pl.pallas_call(
        functools.partial(
            plane_kernel, groups=groups, place=chunk * PLACE, through=len(through)
        ),
        out_shape=[
            pltpu.HBM((SLABS, rows, WIDE), BF16),
            *(pltpu.HBM(x.shape, x.dtype) for x in through),
        ],
        in_specs=[VMEM] * (2 + len(slots) + 3 + len(tables)) + [ANY] * len(through),
        out_specs=[HBM] * (1 + len(through)),
        scratch_shapes=[
            *(pltpu.VMEM((2 * len(group) * X6 * Y16, WIDE), BF16) for group in groups),
            pltpu.VMEM((SLABS, rows, WIDE), BF16),
            pltpu.SemaphoreType.DMA((SLAB_CUTS,)),
            pltpu.SemaphoreType.DMA((max(len(through), 1),)),
        ],
        compiler_params=pltpu.CompilerParams(vmem_limit_bytes=16 << 20),
        cost_estimate=pl.CostEstimate(
            flops=50_000_000, bytes_accessed=100_000, transcendentals=0
        ),
        name="planes",
    )(
        *v,
        *(c[slot] for slot in slots),
        lane_table(),
        twiddle_table(),
        extra,
        *tables,
        *through,
    )


def pick(density_ref, flat_ref, kx_ref, store):
    rows = density_ref.shape[0]

    def body(step, carry):
        lanes = pl.ds(pl.multiple_of(step * TILE, TILE), TILE)
        spot = lax.broadcasted_iota(jnp.int32, (WIDE, TILE), 0)
        chosen = jnp.where(spot == flat_ref[:, lanes], 1.0, 0.0).astype(BF16)
        values = jnp.dot(density_ref[...], chosen, preferred_element_type=F32)
        kx = lax.broadcasted_iota(jnp.int32, (N, TILE), 0) == kx_ref[:, lanes]
        values = jnp.where(kx[None], values.reshape(rows // N, N, TILE), 0.0)
        store(lanes, values.sum(axis=1))
        return carry

    lax.fori_loop(0, G_DEV // TILE, body, 0)


def transform_x(chunk, t_ref, x_refs, low):
    first, place = 0, 0
    for group, x_ref in zip(GROUPS[chunk], x_refs):
        size = slab_rows(len(group))
        planes = t_ref[:, first : first + size, :]
        if size % 16:
            planes = planes.astype(F32)
        planes = planes.reshape(SLABS * size, WIDE).astype(BF16)
        rows = 2 * len(group) * N
        low[place : place + rows, :] = jnp.dot(
            x_ref[...], planes, preferred_element_type=F32
        ).astype(BF16)
        first += size
        place += rows


def first_kernel(
    t_ref, x_ref, own_ref, own_kx_ref, far_ref, far_kx_ref, own_out, far_out, low
):
    transform_x(0, t_ref, (x_ref,), low)

    def store_far(lanes, values):
        far_out[:, lanes] = values.astype(BF16)

    def store_own(lanes, values):
        own_out[:, lanes] = values

    pick(low, far_ref, far_kx_ref, store_far)
    pick(low, own_ref, own_kx_ref, store_own)


def second_far_kernel(
    t_ref, x0_ref, x1_ref, far_ref, far_kx_ref, first_ref, far_out, low, block_out
):
    transform_x(1, t_ref, (x0_ref, x1_ref), low)
    rows = first_ref.shape[0]
    far_out[:rows, :] = first_ref[...]

    def store_far(lanes, values):
        far_out[rows:, lanes] = values.astype(BF16)

    pick(low, far_ref, far_kx_ref, store_far)
    spare = t_ref[:, PLACE : PLACE + 16, SPARE:].astype(F32).sum(axis=0)
    spare = spare + pltpu.roll(spare, 128 - NBLOCK, 1)
    block_out[...] = spare


def second_own_kernel(low, own_ref, own_kx_ref, own_out):
    def store_own(lanes, values):
        own_out[:, lanes] = values

    pick(low, own_ref, own_kx_ref, store_own)


FIRST, SECOND = (2 * sum(len(group) for group in chunk) for chunk in GROUPS)


def first_points(planes, own, far):
    return pl.pallas_call(
        first_kernel,
        out_shape=(
            jax.ShapeDtypeStruct((FIRST, G_DEV), F32),
            jax.ShapeDtypeStruct((FIRST, G_DEV), BF16),
        ),
        scratch_shapes=[pltpu.VMEM((FIRST * N, WIDE), BF16)],
        compiler_params=pltpu.CompilerParams(vmem_limit_bytes=16 << 20),
        cost_estimate=pl.CostEstimate(
            flops=100_000_000, bytes_accessed=100_000, transcendentals=0
        ),
        name="first_points",
    )(planes, x_table(FIRST // 2), *own, *far)


def second_far_points(planes, far, first):
    return pl.pallas_call(
        second_far_kernel,
        out_shape=(
            jax.ShapeDtypeStruct((FIRST + SECOND, G_DEV), BF16),
            jax.ShapeDtypeStruct((SECOND * N, WIDE), BF16),
            jax.ShapeDtypeStruct((16, 128), F32),
        ),
        compiler_params=pltpu.CompilerParams(vmem_limit_bytes=16 << 20),
        cost_estimate=pl.CostEstimate(
            flops=100_000_000, bytes_accessed=100_000, transcendentals=0
        ),
        name="second_far_points",
    )(planes, *(x_table(len(group)) for group in GROUPS[1]), *far, first)


def second_own_points(low, own):
    return pl.pallas_call(
        second_own_kernel,
        out_shape=jax.ShapeDtypeStruct((SECOND, G_DEV), F32),
        compiler_params=pltpu.CompilerParams(vmem_limit_bytes=16 << 20),
        cost_estimate=pl.CostEstimate(
            flops=2_400_000_000, bytes_accessed=1_300_000, transcendentals=0
        ),
        name="second_own_points",
    )(low, *own)


def split_kernel(own0_ref, own1_ref, far_ref, block_ref, out_ref):
    parts = [[], [], [], []]
    first, place = 0, 0
    for own_ref, chunk in zip((own0_ref, own1_ref), GROUPS):
        first = 0
        for group in chunk:
            size = len(group)
            own_r = own_ref[first : first + size, :]
            own_i = own_ref[first + size : first + 2 * size, :]
            far_r = far_ref[place : place + size, :].astype(F32)
            far_i = far_ref[place + size : place + 2 * size, :].astype(F32)
            parts[0].append(own_r + far_r)
            parts[1].append(own_i + far_i)
            parts[2].append(own_i - far_i)
            parts[3].append(far_r - own_r)
            first += 2 * size
            place += 2 * size
    pairs = jnp.concatenate(sum(parts, []), axis=0).astype(BF16)
    block = block_ref[...].astype(BF16)
    for band in range(16):
        out_ref[band, :32, :] = pairs[:, band * 128 : (band + 1) * 128]
        out_ref[band, 32:, :] = block


def split_pairs(own0, own1, far, block):
    return pl.pallas_call(
        split_kernel,
        out_shape=jax.ShapeDtypeStruct((16, 48, 128), BF16),
        compiler_params=pltpu.CompilerParams(vmem_limit_bytes=8 << 20),
        cost_estimate=pl.CostEstimate(
            flops=1_000_000, bytes_accessed=500_000, transcendentals=0
        ),
        name="split",
    )(own0, own1, far, block)


def block_kernel(*refs):
    *waves, lane_ref, row_ref, out_ref = refs
    waves_v, waves_c = waves[:2], waves[2:]
    for half in range(2):
        for item, slot in enumerate(SLOTS):
            product = waves_v[half][...] * waves_c[slot][...]
            sums = jnp.dot(product, lane_ref[...], preferred_element_type=F32) * row_ref[...]
            index = half * len(SLOTS) + item
            out_ref[index : index + 1, :] = sums.sum(axis=0, keepdims=True)
    sums = out_ref[...]
    sums = sums + pltpu.roll(sums, 128 - NBLOCK, 1)
    high = sums.astype(BF16).astype(F32)
    rest = pltpu.roll(sums - high, NBLOCK, 1)
    lane = lax.broadcasted_iota(jnp.int32, sums.shape, 1)
    sums = jnp.where(lane // NBLOCK % 2 == 0, high, rest)
    out_ref[...] = jnp.where((lane >= 32) & (lane < 96), sums, 0.0)


def block_sums(v, c, lanes, rows):
    return pl.pallas_call(
        block_kernel,
        out_shape=jax.ShapeDtypeStruct((16, 128), F32),
        compiler_params=pltpu.CompilerParams(vmem_limit_bytes=4 << 20),
        cost_estimate=pl.CostEstimate(
            flops=10_000_000, bytes_accessed=100_000, transcendentals=0
        ),
        name="block",
    )(*v, *c, lanes, rows)


def sum_kernel(pairs_ref, weight_ref, column_ref, out_ref):
    pairs = 16 * 16
    block = pairs_ref[:, 32:, :].reshape(pairs, 128)
    total = None
    for part in range(2):
        left = pairs_ref[:, 16 * part : 16 * (part + 1), :].reshape(pairs, 128)
        columns = jnp.dot(block, column_ref[part], preferred_element_type=F32)
        right = (columns * weight_ref[...]).astype(BF16)
        term = lax.dot_general(
            left, right, (((0,), (0,)), ((), ())), preferred_element_type=F32
        )
        total = term if total is None else total + term
    out_ref[...] = total


def wave_rows(wave):
    return wave.reshape(X6, Y6, Y16, N).transpose(0, 2, 1, 3).reshape(X6 * Y16, Y6 * N)


def cosine(phase):
    return jnp.cos((phase % N).astype(F32) * (2.0 * math.pi / N))


def per_device(
    valence_wave,
    conduction_wave,
    valence_index,
    occupied_energy,
    conduction_energy,
    frequency,
    gvec_cell,
    block_cell,
):
    col = lax.axis_index(COL)
    wave_v = wave_rows(valence_wave)
    wave_c = wave_rows(conduction_wave)
    ahead = [(i, (i + 1) % 8) for i in range(8)]
    behind = [(i, (i + 7) % 8) for i in range(8)]
    v = [wave_v, lax.ppermute(wave_v, "yl", [(0, 1), (1, 0)])]
    c = [wave_c] + [None] * 7
    for slot in (1, 2, 3, 4):
        c[slot] = lax.ppermute(c[slot - 1], "z", ahead)
        if slot < 4:
            c[8 - slot] = lax.ppermute(c[(9 - slot) % 8], "z", behind)

    mirror_of = [(k, SLABS - 1 - k) for k in range(SLABS)]
    far_cell = lax.ppermute(gvec_cell, COL, mirror_of).reshape(16, 128)
    spots = jnp.arange(128, dtype=jnp.int32)
    cell = jnp.where((spots % NBLOCK == col) & (spots >= 32), block_cell[0], 0)
    marks = jnp.concatenate([jnp.stack([cell // 256, cell % 256]), jnp.zeros((6, 128), jnp.int32)])
    planes0, far_cell = planes_of(0, v, c, marks.astype(F32), through=(far_cell,))
    sent0 = lax.all_to_all(planes0, COL, 0, 0, tiled=True)

    far_cell = far_cell.reshape(G_DEV)
    far_x, far_y, far_z = far_cell // 576, far_cell // N % 6, far_cell % N
    own = ((gvec_cell % 576)[None], (gvec_cell // 576)[None])
    far = (((6 - far_y) * N + (N - far_z) % N)[None], ((N - far_x) % N)[None])

    marks = sent0[:, :2, SPARE:].astype(F32).sum(axis=0)
    cells = jnp.where(spots >= 32, (256.0 * marks[0] + marks[1]).astype(jnp.int32), 0)
    block_x = cells // 576
    block_y = spots % NBLOCK * 6 + cells // N % 6
    block_z = cells % N
    group = spots // NBLOCK - 2
    quarter = N // 4
    lane = jnp.arange(Y6 * N, dtype=jnp.int32)[:, None]
    lanes = cosine(
        lane // N * 16 * block_y + lane % N * block_z + jnp.where(group % 2 == 1, quarter, 0)
    ).astype(BF16)
    row = jnp.arange(X6 * Y16, dtype=jnp.int32)[:, None]
    shift = jnp.where(group == 1, 3 * quarter, jnp.where(group == 2, quarter, 0))
    rows = cosine((row // Y16 + X6 * col) * block_x + row % Y16 * block_y + shift)
    scale = 1.0 / (N * math.sqrt(N))
    rows = jnp.where((group >= 0) & (group < 4), rows * scale, 0.0)
    block = block_sums(v, c, lanes, rows)
    (planes1,) = planes_of(1, v, c, block)
    sent1 = lax.all_to_all(planes1, COL, 0, 0, tiled=True)

    pair_v, pair_c = pair_table()
    occupied = jnp.arange(occupied_energy.shape[0], dtype=jnp.int32)
    valence_energy = jnp.sum(
        jnp.where(valence_index[:, None] == occupied[None, :], occupied_energy[None, :], 0.0),
        axis=1,
    )
    count_v, count_c = valence_index.shape[0], conduction_energy.shape[0]
    energy_v = jnp.sum(
        jnp.where(pair_v[:, None] == np.arange(count_v)[None], valence_energy[None], 0.0), axis=1
    )
    energy_c = jnp.sum(
        jnp.where(pair_c[:, None] == np.arange(count_c)[None], conduction_energy[None], 0.0),
        axis=1,
    )
    gap = (energy_c - energy_v)[:, None]
    omega = jnp.repeat(frequency, 2 * NBLOCK)[None]
    weight = -4.0 * gap / (gap * gap + omega * omega) * (1.0 / math.sqrt(count_v * count_c))

    own0, far0 = first_points(sent0, own, far)
    mirrored, low, columns = second_far_points(sent1, far, far0)
    mirrored = lax.ppermute(mirrored, COL, mirror_of)
    own1 = second_own_points(low, own)
    pairs = split_pairs(own0, own1, mirrored, columns)
    pairs = lax.all_to_all(pairs, BAND, 0, 0, tiled=True)
    return pl.pallas_call(
        sum_kernel,
        out_shape=jax.ShapeDtypeStruct((128, 128), F32),
        compiler_params=pltpu.CompilerParams(vmem_limit_bytes=4 << 20),
        name="pair_sum",
    )(pairs, weight, column_tables())


def solution(mesh):
    fine = Mesh(
        mesh.devices.reshape(8, 2, 4, 2, 2), ("z", "yl", "x", "yh", "co")
    )
    return jax.shard_map(
        per_device,
        mesh=fine,
        in_specs=(
            P(BAND, COL, None),
            P(BAND, COL, None),
            P(),
            P(),
            P(),
            P(),
            P(COL),
            P(COL),
        ),
        out_specs=P(COL + BAND, None),
        check_vma=False,
    )
```

```python
import functools
import math

import jax
import jax.numpy as jnp
import ml_dtypes
import numpy as np
from jax import lax
from jax.experimental import pallas as pl
from jax.experimental.pallas import tpu as pltpu
from jax.sharding import Mesh
from jax.sharding import PartitionSpec as P

BF16 = jnp.bfloat16
F32 = jnp.float32

N = 96
SLABS = 16
X6 = 6
Y6 = 6
Y16 = 16
K7 = 7
FLAT = K7 * N
WIDE = 768
GROUPS = ((0, 1), (7, 2), (6, 3), (5, 4))
SLOTS = [slot for group in GROUPS for slot in group]
ITEMS = len(SLOTS)
SPARE = 640
G_DEV = 2048
NBLOCK = 16
TILE = 512
ROWS = ITEMS * 2 * X6

BAND = ("z", "yl")
COL = ("x", "yh", "co")


def unit(phase, period):
    angle = 2.0 * np.pi * (np.asarray(phase) % period) / period
    return np.cos(angle), -np.sin(angle)


def bf16(table):
    return np.asarray(table, np.float32).astype(ml_dtypes.bfloat16)


@functools.cache
def lane_table():
    y6, z = np.divmod(np.arange(Y6 * N), N)
    k7, kz = np.divmod(np.arange(FLAT), N)
    phase = 16 * y6[:, None] * k7[None, :] + z[:, None] * kz[None, :]
    cosine, sine = unit(phase, N)
    table = np.zeros((Y6 * N, 2 * WIDE))
    table[:, :FLAT] = cosine
    table[:, WIDE : WIDE + FLAT] = sine
    return bf16(table)


@functools.cache
def twiddle_table():
    k7 = np.arange(FLAT) // N
    cosine, sine = unit(np.arange(Y16)[:, None] * k7[None, :], N)
    table = np.zeros((2, Y16, WIDE), np.float32)
    table[0, :, :FLAT] = cosine / N
    table[1, :, :FLAT] = sine / N
    return table


@functools.cache
def row_table(items):
    table = np.zeros((SLABS, items, 2, X6, 2, items, X6, Y16))
    cosine, sine = unit(np.arange(SLABS)[:, None] * np.arange(Y16)[None, :], SLABS)
    for item in range(items):
        for x in range(X6):
            table[:, item, 0, x, 0, item, x] = cosine
            table[:, item, 0, x, 1, item, x] = -sine
            table[:, item, 1, x, 0, item, x] = sine
            table[:, item, 1, x, 1, item, x] = cosine
    return bf16(table.reshape(SLABS * items * 2 * X6, 2 * items * X6 * Y16))


@functools.cache
def x_table(items):
    table = np.zeros((2, items, N, SLABS, items, 2, X6))
    cosine, sine = unit(np.arange(N)[:, None] * np.arange(N)[None, :], N)
    cosine = (cosine * 0.5 / math.sqrt(N)).reshape(N, SLABS, X6)
    sine = (sine * 0.5 / math.sqrt(N)).reshape(N, SLABS, X6)
    for item in range(items):
        table[0, item, :, :, item, 0] = cosine
        table[0, item, :, :, item, 1] = -sine
        table[1, item, :, :, item, 0] = sine
        table[1, item, :, :, item, 1] = cosine
    return bf16(table.reshape(2 * items * N, SLABS * items * 2 * X6))


@functools.cache
def pair_table():
    valence, conduction = [], []
    for band in range(16):
        z, yl = divmod(band, 2)
        for half in range(2):
            for slot in SLOTS:
                valence.append(z * 2 + (yl ^ half))
                conduction.append((z - slot) % 8 * 2 + yl)
    return np.array(valence), np.array(conduction)


@functools.cache
def column_tables():
    tables = np.zeros((2, 128, 4, 2, NBLOCK))
    m = np.arange(NBLOCK)
    tables[0, 32 + m, :, 0, m] = 1.0
    tables[0, 64 + m, :, 1, m] = -1.0
    tables[1, 64 + m, :, 0, m] = 1.0
    tables[1, 32 + m, :, 1, m] = 1.0
    return bf16(tables.reshape(2, 128, 128))


VMEM = pl.BlockSpec(memory_space=pltpu.VMEM)
HBM = pl.BlockSpec(memory_space=pltpu.HBM)
ANY = pl.BlockSpec(memory_space=pl.ANY)
SLAB_CUTS = 4
PLANES_FLOPS = (600_000_000, 600_000_000, 600_000_000, 600_000_000)


def plane_kernel(*refs, items, first, through, chained, spare):
    refs = list(refs)
    take = lambda count: [refs.pop(0) for _ in range(count)]
    v0_ref, v1_ref = take(2)
    waves_c = take(items)
    lane_ref, twiddle_ref, row_ref = take(3)
    extra = take(spare)
    kept = take(through)
    take(chained)
    (out_ref,) = take(1)
    kept_out = take(through)
    low_ref, slab_ref, slab_sems, keep_sems = refs
    moves = [
        pltpu.make_async_copy(source, target, keep_sems.at[i])
        for i, (source, target) in enumerate(zip(kept, kept_out))
    ]
    for move in moves:
        move.start()
    rows = X6 * Y16
    twiddle_c = twiddle_ref[0][None]
    twiddle_s = twiddle_ref[1][None]
    for index, c_ref in enumerate(waves_c):
        wave_c = c_ref[...]
        pairs = jnp.concatenate([v0_ref[...] * wave_c, v1_ref[...] * wave_c], axis=0)
        moved = jnp.dot(pairs, lane_ref[...], preferred_element_type=F32)
        real = moved[:rows, :WIDE] - moved[rows:, WIDE:]
        imag = moved[:rows, WIDE:] + moved[rows:, :WIDE]
        real = real.reshape(X6, Y16, WIDE)
        imag = imag.reshape(X6, Y16, WIDE)
        turned_r = real * twiddle_c - imag * twiddle_s
        turned_i = real * twiddle_s + imag * twiddle_c
        low_ref[index * rows : (index + 1) * rows, :] = turned_r.reshape(rows, WIDE).astype(BF16)
        index += items
        low_ref[index * rows : (index + 1) * rows, :] = turned_i.reshape(rows, WIDE).astype(BF16)
    count = SLABS // SLAB_CUTS
    size = items * 2 * X6
    for part in range(SLAB_CUTS):
        slabs = slice(part * count, (part + 1) * count)
        planes = jnp.dot(
            row_ref[part * count * size : (part + 1) * count * size, :],
            low_ref[...],
            preferred_element_type=F32,
        ).reshape(count, size, WIDE)
        slab_ref[slabs] = planes.astype(BF16)
        if spare:
            block = extra[0][...]
            tail = planes[:, : block.shape[0], SPARE:] + block[None]
            slab_ref[slabs, : block.shape[0], SPARE:] = tail.astype(BF16)
        window = pl.ds(part * count, count)
        moves.append(
            pltpu.make_async_copy(
                slab_ref.at[window],
                out_ref.at[window, pl.ds(first, size)],
                slab_sems.at[part],
            )
        )
        moves[-1].start()
    for move in moves:
        move.wait()


def planes_of(group, v, c, extra=(), through=(), buffer=()):
    slots = GROUPS[group]
    items = len(slots)
    first = sum(len(before) for before in GROUPS[:group]) * 2 * X6
    inputs = (
        *v,
        *(c[slot] for slot in slots),
        lane_table(),
        twiddle_table(),
        row_table(items),
        *extra,
        *through,
        *buffer,
    )
    outside = len(through) + len(buffer)
    return pl.pallas_call(
        functools.partial(
            plane_kernel,
            items=items,
            first=first,
            through=len(through),
            chained=len(buffer),
            spare=len(extra),
        ),
        out_shape=[
            pltpu.HBM((SLABS, ROWS, WIDE), BF16),
            *(pltpu.HBM(x.shape, x.dtype) for x in through),
        ],
        in_specs=[VMEM] * (len(inputs) - outside) + [ANY] * len(through) + [HBM] * len(buffer),
        out_specs=[HBM] * (1 + len(through)),
        input_output_aliases={len(inputs) - 1: 0} if buffer else {},
        scratch_shapes=[
            pltpu.VMEM((2 * items * X6 * Y16, WIDE), BF16),
            pltpu.VMEM((SLABS, items * 2 * X6, WIDE), BF16),
            pltpu.SemaphoreType.DMA((SLAB_CUTS,)),
            pltpu.SemaphoreType.DMA((max(len(through), 1),)),
        ],
        compiler_params=pltpu.CompilerParams(vmem_limit_bytes=16 << 20),
        cost_estimate=pl.CostEstimate(
            flops=PLANES_FLOPS[group] * items, bytes_accessed=100_000, transcendentals=0
        ),
        name="planes",
    )(*inputs)


def pick(density_ref, flat_ref, kx_ref, store):
    rows = density_ref.shape[0]

    def body(step, carry):
        lanes = pl.ds(pl.multiple_of(step * TILE, TILE), TILE)
        spot = lax.broadcasted_iota(jnp.int32, (WIDE, TILE), 0)
        chosen = jnp.where(spot == flat_ref[:, lanes], 1.0, 0.0).astype(BF16)
        values = jnp.dot(density_ref[...], chosen, preferred_element_type=F32)
        kx = lax.broadcasted_iota(jnp.int32, (N, TILE), 0) == kx_ref[:, lanes]
        values = jnp.where(kx[None], values.reshape(rows // N, N, TILE), 0.0)
        store(lanes, values.sum(axis=1))
        return carry

    lax.fori_loop(0, G_DEV // TILE, body, 0)


X_ITEMS = 4


def transform_x(t_ref, x_ref, low):
    size = X_ITEMS * 2 * X6
    rows = X_ITEMS * N
    for item in range(0, ITEMS, X_ITEMS):
        planes = t_ref[:, item * 2 * X6 : item * 2 * X6 + size, :].reshape(SLABS * size, WIDE)
        for part in range(2):
            place = (part * ITEMS + item) * N
            low[place : place + rows, :] = jnp.dot(
                x_ref[part * rows : (part + 1) * rows, :], planes, preferred_element_type=F32
            ).astype(BF16)


PLACE = sum(len(group) for group in GROUPS[:-1]) * 2 * X6


def far_kernel(t_ref, x_ref, far_ref, far_kx_ref, far_out, low, block_out):
    transform_x(t_ref, x_ref, low)

    def store_far(lanes, values):
        far_out[:, lanes] = values.astype(BF16)

    pick(low, far_ref, far_kx_ref, store_far)
    spare = t_ref[:, PLACE : PLACE + 16, SPARE:].astype(F32).sum(axis=0)
    spare = spare + pltpu.roll(spare, 128 - NBLOCK, 1)
    block_out[...] = spare


def own_kernel(low, own_ref, own_kx_ref, own_out):
    def store_own(lanes, values):
        own_out[:, lanes] = values

    pick(low, own_ref, own_kx_ref, store_own)


def far_points(planes, far):
    return pl.pallas_call(
        far_kernel,
        out_shape=(
            jax.ShapeDtypeStruct((2 * ITEMS, G_DEV), BF16),
            jax.ShapeDtypeStruct((2 * ITEMS * N, WIDE), BF16),
            jax.ShapeDtypeStruct((16, 128), F32),
        ),
        compiler_params=pltpu.CompilerParams(vmem_limit_bytes=20 << 20),
        cost_estimate=pl.CostEstimate(
            flops=100_000_000, bytes_accessed=100_000, transcendentals=0
        ),
        name="far_points",
    )(planes, x_table(X_ITEMS), *far)


def own_points(low, own):
    return pl.pallas_call(
        own_kernel,
        out_shape=jax.ShapeDtypeStruct((2 * ITEMS, G_DEV), F32),
        compiler_params=pltpu.CompilerParams(vmem_limit_bytes=20 << 20),
        cost_estimate=pl.CostEstimate(
            flops=5_000_000_000, bytes_accessed=2_500_000, transcendentals=0
        ),
        name="own_points",
    )(low, *own)


def split_kernel(own_ref, far_ref, block_ref, out_ref):
    own_r, own_i = own_ref[:ITEMS, :], own_ref[ITEMS:, :]
    far_r = far_ref[:ITEMS, :].astype(F32)
    far_i = far_ref[ITEMS:, :].astype(F32)
    pairs = jnp.concatenate(
        [own_r + far_r, own_i + far_i, own_i - far_i, far_r - own_r], axis=0
    ).astype(BF16)
    block = block_ref[...].astype(BF16)
    for band in range(16):
        out_ref[band, :32, :] = pairs[:, band * 128 : (band + 1) * 128]
        out_ref[band, 32:, :] = block


def split_pairs(own, far, block):
    return pl.pallas_call(
        split_kernel,
        out_shape=jax.ShapeDtypeStruct((16, 48, 128), BF16),
        compiler_params=pltpu.CompilerParams(vmem_limit_bytes=8 << 20),
        cost_estimate=pl.CostEstimate(
            flops=1_000_000, bytes_accessed=500_000, transcendentals=0
        ),
        name="split",
    )(own, far, block)


def block_kernel(*refs):
    *waves, lane_ref, row_ref, out_ref = refs
    waves_v, waves_c = waves[:2], waves[2:]
    for half in range(2):
        for item, slot in enumerate(SLOTS):
            product = waves_v[half][...] * waves_c[slot][...]
            sums = jnp.dot(product, lane_ref[...], preferred_element_type=F32) * row_ref[...]
            index = half * len(SLOTS) + item
            out_ref[index : index + 1, :] = sums.sum(axis=0, keepdims=True)
    sums = out_ref[...]
    sums = sums + pltpu.roll(sums, 128 - NBLOCK, 1)
    high = sums.astype(BF16).astype(F32)
    rest = pltpu.roll(sums - high, NBLOCK, 1)
    lane = lax.broadcasted_iota(jnp.int32, sums.shape, 1)
    sums = jnp.where(lane // NBLOCK % 2 == 0, high, rest)
    out_ref[...] = jnp.where((lane >= 32) & (lane < 96), sums, 0.0)


def block_sums(v, c, lanes, rows):
    return pl.pallas_call(
        block_kernel,
        out_shape=jax.ShapeDtypeStruct((16, 128), F32),
        compiler_params=pltpu.CompilerParams(vmem_limit_bytes=4 << 20),
        cost_estimate=pl.CostEstimate(
            flops=10_000_000, bytes_accessed=100_000, transcendentals=0
        ),
        name="block",
    )(*v, *c, lanes, rows)


def sum_kernel(pairs_ref, weight_ref, column_ref, out_ref):
    pairs = 16 * 16
    block = pairs_ref[:, 32:, :].reshape(pairs, 128)
    total = None
    for part in range(2):
        left = pairs_ref[:, 16 * part : 16 * (part + 1), :].reshape(pairs, 128)
        columns = jnp.dot(block, column_ref[part], preferred_element_type=F32)
        right = (columns * weight_ref[...]).astype(BF16)
        term = lax.dot_general(
            left, right, (((0,), (0,)), ((), ())), preferred_element_type=F32
        )
        total = term if total is None else total + term
    out_ref[...] = total


def wave_rows(wave):
    return wave.reshape(X6, Y6, Y16, N).transpose(0, 2, 1, 3).reshape(X6 * Y16, Y6 * N)


def cosine(phase):
    return jnp.cos((phase % N).astype(F32) * (2.0 * math.pi / N))


def per_device(
    valence_wave,
    conduction_wave,
    valence_index,
    occupied_energy,
    conduction_energy,
    frequency,
    gvec_cell,
    block_cell,
):
    col = lax.axis_index(COL)
    wave_v = wave_rows(valence_wave)
    wave_c = wave_rows(conduction_wave)
    ahead = [(i, (i + 1) % 8) for i in range(8)]
    behind = [(i, (i + 7) % 8) for i in range(8)]
    v = [wave_v, lax.ppermute(wave_v, "yl", [(0, 1), (1, 0)])]
    c = [wave_c] + [None] * 7
    for slot in (1, 2, 3, 4):
        c[slot] = lax.ppermute(c[slot - 1], "z", ahead)
        if slot < 4:
            c[8 - slot] = lax.ppermute(c[(9 - slot) % 8], "z", behind)

    spots = jnp.arange(128, dtype=jnp.int32)
    cells = jnp.where(spots % NBLOCK == col, block_cell[0], 0)
    for mask in (1, 2):
        cells = cells + lax.ppermute(cells, COL, [(k, k ^ mask) for k in range(SLABS)])

    mirror_of = [(k, SLABS - 1 - k) for k in range(SLABS)]
    far_cell = lax.ppermute(gvec_cell, COL, mirror_of).reshape(16, 128)
    (planes,) = planes_of(0, v, c)
    planes, far_cell, cells = planes_of(
        1, v, c, through=(far_cell, cells[None]), buffer=(planes,)
    )
    far_cell = far_cell.reshape(G_DEV)
    far_x, far_y, far_z = far_cell // 576, far_cell // N % 6, far_cell % N
    own = ((gvec_cell % 576)[None], (gvec_cell // 576)[None])
    far = (((6 - far_y) * N + (N - far_z) % N)[None], ((N - far_x) % N)[None])

    cells = cells[0]
    arrived = [
        lax.ppermute(cells, COL, [(k, k ^ mask) for k in range(SLABS)]) for mask in (4, 8, 12)
    ]
    cells = sum(arrived, cells)
    block_x = cells // 576
    block_y = spots % NBLOCK * 6 + cells // N % 6
    block_z = cells % N
    group = spots // NBLOCK - 2
    quarter = N // 4
    lane = jnp.arange(Y6 * N, dtype=jnp.int32)[:, None]
    lanes = cosine(
        lane // N * 16 * block_y + lane % N * block_z + jnp.where(group % 2 == 1, quarter, 0)
    ).astype(BF16)
    row = jnp.arange(X6 * Y16, dtype=jnp.int32)[:, None]
    shift = jnp.where(group == 1, 3 * quarter, jnp.where(group == 2, quarter, 0))
    rows = cosine((row // Y16 + X6 * col) * block_x + row % Y16 * block_y + shift)
    scale = 1.0 / (N * math.sqrt(N))
    rows = jnp.where((group >= 0) & (group < 4), rows * scale, 0.0)
    block = block_sums(v, c, lanes, rows)

    (planes,) = planes_of(2, v, c, buffer=(planes,))
    (planes,) = planes_of(3, v, c, extra=(block,), buffer=(planes,))
    planes = lax.all_to_all(planes, COL, 0, 0, tiled=True)

    pair_v, pair_c = pair_table()
    occupied = jnp.arange(occupied_energy.shape[0], dtype=jnp.int32)
    valence_energy = jnp.sum(
        jnp.where(valence_index[:, None] == occupied[None, :], occupied_energy[None, :], 0.0),
        axis=1,
    )
    count_v, count_c = valence_index.shape[0], conduction_energy.shape[0]
    energy_v = jnp.sum(
        jnp.where(pair_v[:, None] == np.arange(count_v)[None], valence_energy[None], 0.0), axis=1
    )
    energy_c = jnp.sum(
        jnp.where(pair_c[:, None] == np.arange(count_c)[None], conduction_energy[None], 0.0),
        axis=1,
    )
    gap = (energy_c - energy_v)[:, None]
    omega = jnp.repeat(frequency, 2 * NBLOCK)[None]
    weight = -4.0 * gap / (gap * gap + omega * omega) * (1.0 / math.sqrt(count_v * count_c))

    mirrored, low, columns = far_points(planes, far)
    mirrored = lax.ppermute(mirrored, COL, mirror_of)
    pairs = split_pairs(own_points(low, own), mirrored, columns)
    pairs = lax.all_to_all(pairs, BAND, 0, 0, tiled=True)
    return pl.pallas_call(
        sum_kernel,
        out_shape=jax.ShapeDtypeStruct((128, 128), F32),
        compiler_params=pltpu.CompilerParams(vmem_limit_bytes=4 << 20),
        name="pair_sum",
    )(pairs, weight, column_tables())


def solution(mesh):
    fine = Mesh(
        mesh.devices.reshape(8, 2, 4, 2, 2), ("z", "yl", "x", "yh", "co")
    )
    return jax.shard_map(
        per_device,
        mesh=fine,
        in_specs=(
            P(BAND, COL, None),
            P(BAND, COL, None),
            P(),
            P(),
            P(),
            P(),
            P(COL),
            P(COL),
        ),
        out_specs=P(COL + BAND, None),
        check_vma=False,
    )
```

```python
import functools
import math

import jax
import jax.numpy as jnp
import ml_dtypes
import numpy as np
from jax import lax
from jax.experimental import pallas as pl
from jax.experimental.pallas import tpu as pltpu
from jax.sharding import Mesh
from jax.sharding import PartitionSpec as P

BF16 = jnp.bfloat16
F32 = jnp.float32

N = 96
SLABS = 16
X6 = 6
Y6 = 6
Y16 = 16
K7 = 7
FLAT = K7 * N
WIDE = 768
GROUPS = ((0, 1), (7, 2), (6, 3), (5, 4))
SLOTS = [slot for group in GROUPS for slot in group]
ITEMS = len(SLOTS)
SPARE = 640
G_DEV = 2048
NBLOCK = 16
TILE = 512
CHUNK_ROWS = (24, 72)
X_GROUPS = ((2,), (4, 2))

BAND = ("z", "yl")
COL = ("x", "yh", "co")


def unit(phase, period):
    angle = 2.0 * np.pi * (np.asarray(phase) % period) / period
    return np.cos(angle), -np.sin(angle)


def bf16(table):
    return np.asarray(table, np.float32).astype(ml_dtypes.bfloat16)


@functools.cache
def lane_table():
    y6, z = np.divmod(np.arange(Y6 * N), N)
    k7, kz = np.divmod(np.arange(FLAT), N)
    phase = 16 * y6[:, None] * k7[None, :] + z[:, None] * kz[None, :]
    cosine, sine = unit(phase, N)
    table = np.zeros((Y6 * N, 2 * WIDE))
    table[:, :FLAT] = cosine
    table[:, WIDE : WIDE + FLAT] = sine
    return bf16(table)


@functools.cache
def twiddle_table():
    k7 = np.arange(FLAT) // N
    cosine, sine = unit(np.arange(Y16)[:, None] * k7[None, :], N)
    table = np.zeros((2, Y16, WIDE), np.float32)
    table[0, :, :FLAT] = cosine / N
    table[1, :, :FLAT] = sine / N
    return table


@functools.cache
def row_table(items):
    table = np.zeros((SLABS, items, 2, X6, 2, items, X6, Y16))
    cosine, sine = unit(np.arange(SLABS)[:, None] * np.arange(Y16)[None, :], SLABS)
    for item in range(items):
        for x in range(X6):
            table[:, item, 0, x, 0, item, x] = cosine
            table[:, item, 0, x, 1, item, x] = -sine
            table[:, item, 1, x, 0, item, x] = sine
            table[:, item, 1, x, 1, item, x] = cosine
    return bf16(table.reshape(SLABS * items * 2 * X6, 2 * items * X6 * Y16))


@functools.cache
def x_table(items):
    table = np.zeros((2, items, N, SLABS, items, 2, X6))
    cosine, sine = unit(np.arange(N)[:, None] * np.arange(N)[None, :], N)
    cosine = (cosine * 0.5 / math.sqrt(N)).reshape(N, SLABS, X6)
    sine = (sine * 0.5 / math.sqrt(N)).reshape(N, SLABS, X6)
    for item in range(items):
        table[0, item, :, :, item, 0] = cosine
        table[0, item, :, :, item, 1] = -sine
        table[1, item, :, :, item, 0] = sine
        table[1, item, :, :, item, 1] = cosine
    return bf16(table.reshape(2 * items * N, SLABS * items * 2 * X6))


@functools.cache
def pair_table():
    valence, conduction = [], []
    for band in range(16):
        z, yl = divmod(band, 2)
        for half in range(2):
            for slot in SLOTS:
                valence.append(z * 2 + (yl ^ half))
                conduction.append((z - slot) % 8 * 2 + yl)
    return np.array(valence), np.array(conduction)


@functools.cache
def column_tables():
    tables = np.zeros((2, 128, 4, 2, NBLOCK))
    m = np.arange(NBLOCK)
    tables[0, 32 + m, :, 0, m] = 1.0
    tables[0, 64 + m, :, 1, m] = -1.0
    tables[1, 64 + m, :, 0, m] = 1.0
    tables[1, 32 + m, :, 1, m] = 1.0
    return bf16(tables.reshape(2, 128, 128))


VMEM = pl.BlockSpec(memory_space=pltpu.VMEM)
HBM = pl.BlockSpec(memory_space=pltpu.HBM)
ANY = pl.BlockSpec(memory_space=pl.ANY)
SLAB_CUTS = 4
PLANES_FLOPS = (30_000_000, 30_000_000, 30_000_000, 30_000_000)


def plane_kernel(*refs, items, first, through, chained, marked):
    refs = list(refs)
    take = lambda count: [refs.pop(0) for _ in range(count)]
    v0_ref, v1_ref = take(2)
    waves_c = take(items)
    lane_ref, twiddle_ref, row_ref = take(3)
    marks = take(marked)
    kept = take(through)
    take(chained)
    (out_ref,) = take(1)
    kept_out = take(through)
    low_ref, slab_ref, slab_sems, keep_sems = refs
    moves = [
        pltpu.make_async_copy(source, target, keep_sems.at[i])
        for i, (source, target) in enumerate(zip(kept, kept_out))
    ]
    for move in moves:
        move.start()
    rows = X6 * Y16
    twiddle_c = twiddle_ref[0][None]
    twiddle_s = twiddle_ref[1][None]
    for index, c_ref in enumerate(waves_c):
        wave_c = c_ref[...]
        pairs = jnp.concatenate([v0_ref[...] * wave_c, v1_ref[...] * wave_c], axis=0)
        moved = jnp.dot(pairs, lane_ref[...], preferred_element_type=F32)
        real = moved[:rows, :WIDE] - moved[rows:, WIDE:]
        imag = moved[:rows, WIDE:] + moved[rows:, :WIDE]
        real = real.reshape(X6, Y16, WIDE)
        imag = imag.reshape(X6, Y16, WIDE)
        turned_r = real * twiddle_c - imag * twiddle_s
        turned_i = real * twiddle_s + imag * twiddle_c
        low_ref[index * rows : (index + 1) * rows, :] = turned_r.reshape(rows, WIDE).astype(BF16)
        index += items
        low_ref[index * rows : (index + 1) * rows, :] = turned_i.reshape(rows, WIDE).astype(BF16)
    count = SLABS // SLAB_CUTS
    size = items * 2 * X6
    for part in range(SLAB_CUTS):
        slabs = slice(part * count, (part + 1) * count)
        planes = jnp.dot(
            row_ref[part * count * size : (part + 1) * count * size, :],
            low_ref[...],
            preferred_element_type=F32,
        ).reshape(count, size, WIDE)
        slab_ref[slabs] = planes.astype(BF16)
        if marks:
            tail = planes[:, :8, SPARE:] + marks[0][...][None]
            slab_ref[slabs, :8, SPARE:] = tail.astype(BF16)
        window = pl.ds(part * count, count)
        moves.append(
            pltpu.make_async_copy(
                slab_ref.at[window],
                out_ref.at[window, pl.ds(first, size)],
                slab_sems.at[part],
            )
        )
        moves[-1].start()
    for move in moves:
        move.wait()


def planes_of(group, v, c, marks=(), through=(), buffer=()):
    slots = GROUPS[group]
    items = len(slots)
    first = max(group - 1, 0) * items * 2 * X6
    rows = CHUNK_ROWS[min(group, 1)]
    inputs = (
        *v,
        *(c[slot] for slot in slots),
        lane_table(),
        twiddle_table(),
        row_table(items),
        *marks,
        *through,
        *buffer,
    )
    outside = len(through) + len(buffer)
    return pl.pallas_call(
        functools.partial(
            plane_kernel,
            items=items,
            first=first,
            through=len(through),
            chained=len(buffer),
            marked=len(marks),
        ),
        out_shape=[
            pltpu.HBM((SLABS, rows, WIDE), BF16),
            *(pltpu.HBM(x.shape, x.dtype) for x in through),
        ],
        in_specs=[VMEM] * (len(inputs) - outside) + [ANY] * len(through) + [HBM] * len(buffer),
        out_specs=[HBM] * (1 + len(through)),
        input_output_aliases={len(inputs) - 1: 0} if buffer else {},
        scratch_shapes=[
            pltpu.VMEM((2 * items * X6 * Y16, WIDE), BF16),
            pltpu.VMEM((SLABS, items * 2 * X6, WIDE), BF16),
            pltpu.SemaphoreType.DMA((SLAB_CUTS,)),
            pltpu.SemaphoreType.DMA((max(len(through), 1),)),
        ],
        compiler_params=pltpu.CompilerParams(vmem_limit_bytes=16 << 20),
        cost_estimate=pl.CostEstimate(
            flops=PLANES_FLOPS[group] * items, bytes_accessed=100_000, transcendentals=0
        ),
        name="planes",
    )(*inputs)


def pick(density_ref, flat_ref, kx_ref, store):
    rows = density_ref.shape[0]

    def body(step, carry):
        lanes = pl.ds(pl.multiple_of(step * TILE, TILE), TILE)
        spot = lax.broadcasted_iota(jnp.int32, (WIDE, TILE), 0)
        chosen = jnp.where(spot == flat_ref[:, lanes], 1.0, 0.0).astype(BF16)
        values = jnp.dot(density_ref[...], chosen, preferred_element_type=F32)
        kx = lax.broadcasted_iota(jnp.int32, (N, TILE), 0) == kx_ref[:, lanes]
        values = jnp.where(kx[None], values.reshape(rows // N, N, TILE), 0.0)
        store(lanes, values.sum(axis=1))
        return carry

    lax.fori_loop(0, G_DEV // TILE, body, 0)


def transform_x(chunk, t_ref, x_refs, low):
    first, place = 0, 0
    for items, x_ref in zip(X_GROUPS[chunk], x_refs):
        size = items * 2 * X6
        planes = t_ref[:, first : first + size, :]
        if size % 16:
            planes = planes.astype(F32)
        planes = planes.reshape(SLABS * size, WIDE).astype(BF16)
        rows = 2 * items * N
        low[place : place + rows, :] = jnp.dot(
            x_ref[...], planes, preferred_element_type=F32
        ).astype(BF16)
        first += size
        place += rows


def first_kernel(
    t_ref, x_ref, own_ref, own_kx_ref, far_ref, far_kx_ref, own_out, far_out, low
):
    transform_x(0, t_ref, (x_ref,), low)

    def store_far(lanes, values):
        far_out[:, lanes] = values.astype(BF16)

    def store_own(lanes, values):
        own_out[:, lanes] = values

    pick(low, far_ref, far_kx_ref, store_far)
    pick(low, own_ref, own_kx_ref, store_own)


def second_far_kernel(
    t_ref, x0_ref, x1_ref, far_ref, far_kx_ref, first_ref, far_out, low, block_out
):
    transform_x(1, t_ref, (x0_ref, x1_ref), low)
    rows = first_ref.shape[0]
    far_out[:rows, :] = first_ref[...]

    def store_far(lanes, values):
        far_out[rows:, lanes] = values.astype(BF16)

    pick(low, far_ref, far_kx_ref, store_far)
    spare = t_ref[:, :16, SPARE:].astype(F32).sum(axis=0)
    spare = spare + pltpu.roll(spare, 128 - NBLOCK, 1)
    block_out[...] = spare


def second_own_kernel(low, own_ref, own_kx_ref, own_out):
    def store_own(lanes, values):
        own_out[:, lanes] = values

    pick(low, own_ref, own_kx_ref, store_own)


FIRST, SECOND = (2 * sum(chunk) for chunk in X_GROUPS)


def first_points(planes, own, far):
    return pl.pallas_call(
        first_kernel,
        out_shape=(
            jax.ShapeDtypeStruct((FIRST, G_DEV), F32),
            jax.ShapeDtypeStruct((FIRST, G_DEV), BF16),
        ),
        scratch_shapes=[pltpu.VMEM((FIRST * N, WIDE), BF16)],
        compiler_params=pltpu.CompilerParams(vmem_limit_bytes=16 << 20),
        cost_estimate=pl.CostEstimate(
            flops=100_000_000, bytes_accessed=100_000, transcendentals=0
        ),
        name="first_points",
    )(planes, x_table(FIRST // 2), *own, *far)


def second_far_points(planes, far, first):
    return pl.pallas_call(
        second_far_kernel,
        out_shape=(
            jax.ShapeDtypeStruct((FIRST + SECOND, G_DEV), BF16),
            jax.ShapeDtypeStruct((SECOND * N, WIDE), BF16),
            jax.ShapeDtypeStruct((16, 128), F32),
        ),
        compiler_params=pltpu.CompilerParams(vmem_limit_bytes=16 << 20),
        cost_estimate=pl.CostEstimate(
            flops=100_000_000, bytes_accessed=100_000, transcendentals=0
        ),
        name="second_far_points",
    )(planes, *(x_table(items) for items in X_GROUPS[1]), *far, first)


def second_own_points(low, own):
    return pl.pallas_call(
        second_own_kernel,
        out_shape=jax.ShapeDtypeStruct((SECOND, G_DEV), F32),
        compiler_params=pltpu.CompilerParams(vmem_limit_bytes=16 << 20),
        cost_estimate=pl.CostEstimate(
            flops=2_400_000_000, bytes_accessed=1_300_000, transcendentals=0
        ),
        name="second_own_points",
    )(low, *own)


def split_kernel(own0_ref, own1_ref, far_ref, block_ref, out_ref):
    parts = [[], [], [], []]
    first, place = 0, 0
    for own_ref, chunk in zip((own0_ref, own1_ref), X_GROUPS):
        first = 0
        for size in chunk:
            own_r = own_ref[first : first + size, :]
            own_i = own_ref[first + size : first + 2 * size, :]
            far_r = far_ref[place : place + size, :].astype(F32)
            far_i = far_ref[place + size : place + 2 * size, :].astype(F32)
            parts[0].append(own_r + far_r)
            parts[1].append(own_i + far_i)
            parts[2].append(own_i - far_i)
            parts[3].append(far_r - own_r)
            first += 2 * size
            place += 2 * size
    pairs = jnp.concatenate(sum(parts, []), axis=0).astype(BF16)
    block = block_ref[...].astype(BF16)
    for band in range(16):
        out_ref[band, :32, :] = pairs[:, band * 128 : (band + 1) * 128]
        out_ref[band, 32:, :] = block


def split_pairs(own0, own1, far, block):
    return pl.pallas_call(
        split_kernel,
        out_shape=jax.ShapeDtypeStruct((16, 48, 128), BF16),
        compiler_params=pltpu.CompilerParams(vmem_limit_bytes=8 << 20),
        cost_estimate=pl.CostEstimate(
            flops=1_000_000, bytes_accessed=500_000, transcendentals=0
        ),
        name="split",
    )(own0, own1, far, block)


def phase_cosine(phase):
    turns = jnp.floor((phase + 0.5) * (1.0 / N))
    return jnp.cos((phase - N * turns) * (2.0 * math.pi / N))


def block_kernel(*refs):
    waves, refs = refs[:2 + len(SLOTS)], refs[2 + len(SLOTS) :]
    info_ref, marks_hbm, _, out_hbm, marks_ref, tail_ref, sums_ref, sems = refs
    waves_v, waves_c = waves[:2], waves[2:]
    tail = (slice(None), pl.ds(0, 16), pl.ds(SPARE, 128))
    fetch = pltpu.make_async_copy(out_hbm.at[tail], tail_ref, sems.at[0])
    fetch.start()
    place = marks_hbm.at[:, pl.ds(0, 8), pl.ds(SPARE, 128)]
    marks_in = pltpu.make_async_copy(place, marks_ref, sems.at[1])
    marks_in.start()
    info = info_ref[...]
    marks_in.wait()
    marks = marks_ref[...].astype(F32).sum(axis=0)
    used = info[3:4] != 0.0
    cell = jnp.where(used, 256.0 * marks[0:1] + marks[1:2], 0.0)
    block_x = jnp.floor((cell + 0.5) * (1.0 / 576.0))
    cell = cell - 576.0 * block_x
    block_y = jnp.floor((cell + 0.5) * (1.0 / N))
    block_z = cell - N * block_y
    block_y = block_y + info[0:1]
    lane = lax.broadcasted_iota(jnp.int32, (Y6 * N, 128), 0).astype(F32)
    y6 = jnp.floor((lane + 0.5) * (1.0 / N))
    lanes = phase_cosine(16.0 * y6 * block_y + (lane - N * y6) * block_z + info[1:2]).astype(BF16)
    row = lax.broadcasted_iota(jnp.int32, (X6 * Y16, 128), 0).astype(F32)
    x = jnp.floor((row + 0.5) * (1.0 / Y16))
    rows = phase_cosine((x + info[4:5]) * block_x + (row - Y16 * x) * block_y + info[2:3])
    rows = rows * info[3:4]
    for half in range(2):
        for item, slot in enumerate(SLOTS):
            product = waves_v[half][...] * waves_c[slot][...]
            sums = jnp.dot(product, lanes, preferred_element_type=F32) * rows
            index = half * len(SLOTS) + item
            sums_ref[index : index + 1, :] = sums.sum(axis=0, keepdims=True)
    sums = sums_ref[...]
    sums = sums + pltpu.roll(sums, 128 - NBLOCK, 1)
    high = sums.astype(BF16).astype(F32)
    rest = pltpu.roll(sums - high, NBLOCK, 1)
    spot = lax.broadcasted_iota(jnp.int32, sums.shape, 1)
    sums = jnp.where(spot // NBLOCK % 2 == 0, high, rest)
    fetch.wait()
    tails = tail_ref[...].astype(F32)
    tail_ref[...] = jnp.where((spot >= 32) & (spot < 96), sums, tails).astype(BF16)
    store = pltpu.make_async_copy(tail_ref, out_hbm.at[tail], sems.at[2])
    store.start()
    store.wait()


def with_block_sums(v, c, info, arrived, planes):
    inputs = (*v, *c, info, arrived, planes)
    return pl.pallas_call(
        block_kernel,
        out_shape=pltpu.HBM(planes.shape, planes.dtype),
        in_specs=[VMEM] * (len(inputs) - 2) + [ANY, HBM],
        out_specs=HBM,
        input_output_aliases={len(inputs) - 1: 0},
        scratch_shapes=[
            pltpu.VMEM((SLABS, 8, 128), BF16),
            pltpu.VMEM((SLABS, 16, 128), BF16),
            pltpu.VMEM((16, 128), F32),
            pltpu.SemaphoreType.DMA((3,)),
        ],
        compiler_params=pltpu.CompilerParams(vmem_limit_bytes=6 << 20),
        cost_estimate=pl.CostEstimate(
            flops=10_000_000, bytes_accessed=100_000, transcendentals=0
        ),
        name="block",
    )(*inputs)


def sum_kernel(pairs_ref, weight_ref, column_ref, out_ref):
    pairs = 16 * 16
    block = pairs_ref[:, 32:, :].reshape(pairs, 128)
    total = None
    for part in range(2):
        left = pairs_ref[:, 16 * part : 16 * (part + 1), :].reshape(pairs, 128)
        columns = jnp.dot(block, column_ref[part], preferred_element_type=F32)
        right = (columns * weight_ref[...]).astype(BF16)
        term = lax.dot_general(
            left, right, (((0,), (0,)), ((), ())), preferred_element_type=F32
        )
        total = term if total is None else total + term
    out_ref[...] = total


def wave_rows(wave):
    return wave.reshape(X6, Y6, Y16, N).transpose(0, 2, 1, 3).reshape(X6 * Y16, Y6 * N)


def per_device(
    valence_wave,
    conduction_wave,
    valence_index,
    occupied_energy,
    conduction_energy,
    frequency,
    gvec_cell,
    block_cell,
):
    col = lax.axis_index(COL)
    wave_v = wave_rows(valence_wave)
    wave_c = wave_rows(conduction_wave)
    ahead = [(i, (i + 1) % 8) for i in range(8)]
    behind = [(i, (i + 7) % 8) for i in range(8)]
    v = [wave_v, lax.ppermute(wave_v, "yl", [(0, 1), (1, 0)])]
    c = [wave_c] + [None] * 7
    for slot in (1, 2, 3, 4):
        c[slot] = lax.ppermute(c[slot - 1], "z", ahead)
        if slot < 4:
            c[8 - slot] = lax.ppermute(c[(9 - slot) % 8], "z", behind)

    mirror_of = [(k, SLABS - 1 - k) for k in range(SLABS)]
    far_cell = lax.ppermute(gvec_cell, COL, mirror_of).reshape(16, 128)
    spots = jnp.arange(128, dtype=jnp.int32)
    cell = jnp.where((spots % NBLOCK == col) & (spots >= 32), block_cell[0], 0)
    marks = jnp.concatenate([jnp.stack([cell // 256, cell % 256]), jnp.zeros((6, 128), jnp.int32)])
    planes0, far_cell = planes_of(0, v, c, marks=(marks.astype(F32),), through=(far_cell,))
    sent0 = lax.all_to_all(planes0, COL, 0, 0, tiled=True)
    (planes1,) = planes_of(1, v, c)
    (planes1,) = planes_of(2, v, c, buffer=(planes1,))
    (planes1,) = planes_of(3, v, c, buffer=(planes1,))

    group = np.arange(128) // NBLOCK - 2
    used = (group >= 0) & (group < 4)
    info = np.zeros((8, 128), np.float32)
    info[0] = np.arange(128) % NBLOCK * 6
    info[1] = np.where(group % 2 == 1, N // 4, 0)
    info[2] = np.where(group == 1, 3 * N // 4, np.where(group == 2, N // 4, 0))
    info[3] = np.where(used, 1.0 / (N * math.sqrt(N)), 0.0)
    info = info + jnp.where(np.arange(8)[:, None] == 4, (X6 * col).astype(F32), 0.0)
    planes1 = with_block_sums(v, c, info, sent0, planes1)
    sent1 = lax.all_to_all(planes1, COL, 0, 0, tiled=True)

    far_cell = far_cell.reshape(G_DEV)
    far_x, far_y, far_z = far_cell // 576, far_cell // N % 6, far_cell % N
    own = ((gvec_cell % 576)[None], (gvec_cell // 576)[None])
    far = (((6 - far_y) * N + (N - far_z) % N)[None], ((N - far_x) % N)[None])

    pair_v, pair_c = pair_table()
    occupied = jnp.arange(occupied_energy.shape[0], dtype=jnp.int32)
    valence_energy = jnp.sum(
        jnp.where(valence_index[:, None] == occupied[None, :], occupied_energy[None, :], 0.0),
        axis=1,
    )
    count_v, count_c = valence_index.shape[0], conduction_energy.shape[0]
    energy_v = jnp.sum(
        jnp.where(pair_v[:, None] == np.arange(count_v)[None], valence_energy[None], 0.0), axis=1
    )
    energy_c = jnp.sum(
        jnp.where(pair_c[:, None] == np.arange(count_c)[None], conduction_energy[None], 0.0),
        axis=1,
    )
    gap = (energy_c - energy_v)[:, None]
    omega = jnp.repeat(frequency, 2 * NBLOCK)[None]
    weight = -4.0 * gap / (gap * gap + omega * omega) * (1.0 / math.sqrt(count_v * count_c))

    own0, far0 = first_points(sent0, own, far)
    mirrored, low, columns = second_far_points(sent1, far, far0)
    mirrored = lax.ppermute(mirrored, COL, mirror_of)
    own1 = second_own_points(low, own)
    pairs = split_pairs(own0, own1, mirrored, columns)
    pairs = lax.all_to_all(pairs, BAND, 0, 0, tiled=True)
    return pl.pallas_call(
        sum_kernel,
        out_shape=jax.ShapeDtypeStruct((128, 128), F32),
        compiler_params=pltpu.CompilerParams(vmem_limit_bytes=4 << 20),
        name="pair_sum",
    )(pairs, weight, column_tables())


def solution(mesh):
    fine = Mesh(
        mesh.devices.reshape(8, 2, 4, 2, 2), ("z", "yl", "x", "yh", "co")
    )
    return jax.shard_map(
        per_device,
        mesh=fine,
        in_specs=(
            P(BAND, COL, None),
            P(BAND, COL, None),
            P(),
            P(),
            P(),
            P(),
            P(COL),
            P(COL),
        ),
        out_specs=P(COL + BAND, None),
        check_vma=False,
    )
```

```python
import functools
import math

import jax
import jax.numpy as jnp
import ml_dtypes
import numpy as np
from jax import lax
from jax.experimental import pallas as pl
from jax.experimental.pallas import tpu as pltpu
from jax.sharding import Mesh
from jax.sharding import PartitionSpec as P

BF16 = jnp.bfloat16
F32 = jnp.float32

N = 96
SLABS = 16
X6 = 6
Y6 = 6
Y16 = 16
K7 = 7
FLAT = K7 * N
WIDE = 768
GROUPS = ((0, 1), (6, 2), (7, 3), (5, 4))
SLOTS = [slot for group in GROUPS for slot in group]
ITEMS = len(SLOTS)
SPARE = 640
G_DEV = 2048
NBLOCK = 16
TILE = 512
CHUNK_ROWS = (24, 72)
X_GROUPS = ((2,), (2, 2, 2))

BAND = ("z", "yl")
COL = ("x", "yh", "co")


def unit(phase, period):
    angle = 2.0 * np.pi * (np.asarray(phase) % period) / period
    return np.cos(angle), -np.sin(angle)


def bf16(table):
    return np.asarray(table, np.float32).astype(ml_dtypes.bfloat16)


@functools.cache
def lane_table():
    y6, z = np.divmod(np.arange(Y6 * N), N)
    k7, kz = np.divmod(np.arange(FLAT), N)
    phase = 16 * y6[:, None] * k7[None, :] + z[:, None] * kz[None, :]
    cosine, sine = unit(phase, N)
    table = np.zeros((Y6 * N, 2 * WIDE))
    table[:, :FLAT] = cosine
    table[:, WIDE : WIDE + FLAT] = sine
    return bf16(table)


@functools.cache
def twiddle_table():
    k7 = np.arange(FLAT) // N
    cosine, sine = unit(np.arange(Y16)[:, None] * k7[None, :], N)
    table = np.zeros((2, Y16, WIDE), np.float32)
    table[0, :, :FLAT] = cosine / N
    table[1, :, :FLAT] = sine / N
    return table


@functools.cache
def row_table(items):
    table = np.zeros((SLABS, items, 2, X6, 2, items, X6, Y16))
    cosine, sine = unit(np.arange(SLABS)[:, None] * np.arange(Y16)[None, :], SLABS)
    for item in range(items):
        for x in range(X6):
            table[:, item, 0, x, 0, item, x] = cosine
            table[:, item, 0, x, 1, item, x] = -sine
            table[:, item, 1, x, 0, item, x] = sine
            table[:, item, 1, x, 1, item, x] = cosine
    return bf16(table.reshape(SLABS * items * 2 * X6, 2 * items * X6 * Y16))


@functools.cache
def x_table(items):
    table = np.zeros((2, items, N, SLABS, items, 2, X6))
    cosine, sine = unit(np.arange(N)[:, None] * np.arange(N)[None, :], N)
    cosine = (cosine * 0.5 / math.sqrt(N)).reshape(N, SLABS, X6)
    sine = (sine * 0.5 / math.sqrt(N)).reshape(N, SLABS, X6)
    for item in range(items):
        table[0, item, :, :, item, 0] = cosine
        table[0, item, :, :, item, 1] = -sine
        table[1, item, :, :, item, 0] = sine
        table[1, item, :, :, item, 1] = cosine
    return bf16(table.reshape(2 * items * N, SLABS * items * 2 * X6))


@functools.cache
def pair_table():
    valence, conduction = [], []
    for band in range(16):
        z, yl = divmod(band, 2)
        for half in range(2):
            for slot in SLOTS:
                valence.append(z * 2 + (yl ^ half))
                conduction.append((z - slot) % 8 * 2 + yl)
    return np.array(valence), np.array(conduction)


@functools.cache
def column_tables():
    tables = np.zeros((2, 128, 4, 2, NBLOCK))
    m = np.arange(NBLOCK)
    tables[0, 32 + m, :, 0, m] = 1.0
    tables[0, 64 + m, :, 1, m] = -1.0
    tables[1, 64 + m, :, 0, m] = 1.0
    tables[1, 32 + m, :, 1, m] = 1.0
    return bf16(tables.reshape(2, 128, 128))


VMEM = pl.BlockSpec(memory_space=pltpu.VMEM)
HBM = pl.BlockSpec(memory_space=pltpu.HBM)
ANY = pl.BlockSpec(memory_space=pl.ANY)
SLAB_CUTS = 4


def in_hbm(x):
    return pltpu.with_memory_space_constraint(x, pltpu.HBM)


PLANES_FLOPS = (30_000_000, 30_000_000, 30_000_000, 30_000_000)


def plane_kernel(*refs, items, first, through, chained, marked):
    refs = list(refs)
    take = lambda count: [refs.pop(0) for _ in range(count)]
    v0_ref, v1_ref = take(2)
    waves_c = take(items)
    lane_ref, twiddle_ref, row_ref = take(3)
    marks = take(marked)
    kept = take(through)
    take(chained)
    (out_ref,) = take(1)
    kept_out = take(through)
    low_ref, slab_ref, slab_sems, keep_sems = refs
    moves = [
        pltpu.make_async_copy(source, target, keep_sems.at[i])
        for i, (source, target) in enumerate(zip(kept, kept_out))
    ]
    for move in moves:
        move.start()
    rows = X6 * Y16
    twiddle_c = twiddle_ref[0][None]
    twiddle_s = twiddle_ref[1][None]
    for index, c_ref in enumerate(waves_c):
        wave_c = c_ref[...]
        pairs = jnp.concatenate([v0_ref[...] * wave_c, v1_ref[...] * wave_c], axis=0)
        moved = jnp.dot(pairs, lane_ref[...], preferred_element_type=F32)
        real = moved[:rows, :WIDE] - moved[rows:, WIDE:]
        imag = moved[:rows, WIDE:] + moved[rows:, :WIDE]
        real = real.reshape(X6, Y16, WIDE)
        imag = imag.reshape(X6, Y16, WIDE)
        turned_r = real * twiddle_c - imag * twiddle_s
        turned_i = real * twiddle_s + imag * twiddle_c
        low_ref[index * rows : (index + 1) * rows, :] = turned_r.reshape(rows, WIDE).astype(BF16)
        index += items
        low_ref[index * rows : (index + 1) * rows, :] = turned_i.reshape(rows, WIDE).astype(BF16)
    count = SLABS // SLAB_CUTS
    size = items * 2 * X6
    for part in range(SLAB_CUTS):
        slabs = slice(part * count, (part + 1) * count)
        planes = jnp.dot(
            row_ref[part * count * size : (part + 1) * count * size, :],
            low_ref[...],
            preferred_element_type=F32,
        ).reshape(count, size, WIDE)
        slab_ref[slabs] = planes.astype(BF16)
        if marks:
            tail = planes[:, :8, SPARE:] + marks[0][...][None]
            slab_ref[slabs, :8, SPARE:] = tail.astype(BF16)
        window = pl.ds(part * count, count)
        moves.append(
            pltpu.make_async_copy(
                slab_ref.at[window],
                out_ref.at[window, pl.ds(first, size)],
                slab_sems.at[part],
            )
        )
        moves[-1].start()
    for move in moves:
        move.wait()


def planes_of(group, v, c, marks=(), through=(), after=(), buffer=()):
    slots = GROUPS[group]
    items = len(slots)
    first = max(group - 1, 0) * items * 2 * X6
    rows = CHUNK_ROWS[min(group, 1)]
    inputs = (
        *v,
        *(c[slot] for slot in slots),
        lane_table(),
        twiddle_table(),
        row_table(items),
        *marks,
        *through,
        *after,
        *buffer,
    )
    outside = len(through) + len(after) + len(buffer)
    return pl.pallas_call(
        functools.partial(
            plane_kernel,
            items=items,
            first=first,
            through=len(through),
            chained=len(after) + len(buffer),
            marked=len(marks),
        ),
        out_shape=[
            pltpu.HBM((SLABS, rows, WIDE), BF16),
            *(pltpu.HBM(x.shape, x.dtype) for x in through),
        ],
        in_specs=[VMEM] * (len(inputs) - outside)
        + [ANY] * (len(through) + len(after))
        + [HBM] * len(buffer),
        out_specs=[HBM] * (1 + len(through)),
        input_output_aliases={len(inputs) - 1: 0} if buffer else {},
        scratch_shapes=[
            pltpu.VMEM((2 * items * X6 * Y16, WIDE), BF16),
            pltpu.VMEM((SLABS, items * 2 * X6, WIDE), BF16),
            pltpu.SemaphoreType.DMA((SLAB_CUTS,)),
            pltpu.SemaphoreType.DMA((max(len(through), 1),)),
        ],
        compiler_params=pltpu.CompilerParams(vmem_limit_bytes=16 << 20),
        cost_estimate=pl.CostEstimate(
            flops=PLANES_FLOPS[group] * items, bytes_accessed=100_000, transcendentals=0
        ),
        name="planes",
    )(*inputs)


def pick(density_ref, flat_ref, kx_ref, store):
    rows = density_ref.shape[0]

    def body(step, carry):
        lanes = pl.ds(pl.multiple_of(step * TILE, TILE), TILE)
        spot = lax.broadcasted_iota(jnp.int32, (WIDE, TILE), 0)
        chosen = jnp.where(spot == flat_ref[:, lanes], 1.0, 0.0).astype(BF16)
        values = jnp.dot(density_ref[...], chosen, preferred_element_type=F32)
        kx = lax.broadcasted_iota(jnp.int32, (N, TILE), 0) == kx_ref[:, lanes]
        values = jnp.where(kx[None], values.reshape(rows // N, N, TILE), 0.0)
        store(lanes, values.sum(axis=1))
        return carry

    lax.fori_loop(0, G_DEV // TILE, body, 0, unroll=True)


def transform_x(chunk, t_ref, x_refs, low):
    first, place = 0, 0
    for items, x_ref in zip(X_GROUPS[chunk], x_refs):
        size = items * 2 * X6
        planes = t_ref[:, first : first + size, :]
        if size % 16:
            planes = planes.astype(F32)
        planes = planes.reshape(SLABS * size, WIDE).astype(BF16)
        rows = 2 * items * N
        low[place : place + rows, :] = jnp.dot(
            x_ref[...], planes, preferred_element_type=F32
        ).astype(BF16)
        first += size
        place += rows


def first_kernel(
    t_ref, x_ref, own_ref, own_kx_ref, far_ref, far_kx_ref, own_out, far_out, low
):
    transform_x(0, t_ref, (x_ref,), low)

    def store_far(lanes, values):
        far_out[:, lanes] = values.astype(BF16)

    def store_own(lanes, values):
        own_out[:, lanes] = values

    pick(low, far_ref, far_kx_ref, store_far)
    pick(low, own_ref, own_kx_ref, store_own)


def second_far_kernel(
    t_ref, x_ref, far_ref, far_kx_ref, first_ref, far_out, low, block_out
):
    transform_x(1, t_ref, (x_ref,) * len(X_GROUPS[1]), low)
    rows = first_ref.shape[0]
    far_out[:rows, :] = first_ref[...]

    def store_far(lanes, values):
        far_out[rows:, lanes] = values.astype(BF16)

    pick(low, far_ref, far_kx_ref, store_far)
    spare = t_ref[:, :16, SPARE:].astype(F32).sum(axis=0)
    spare = spare + pltpu.roll(spare, 128 - NBLOCK, 1)
    block_out[...] = spare


def second_own_kernel(low, own_ref, own_kx_ref, own_out):
    def store_own(lanes, values):
        own_out[:, lanes] = values

    pick(low, own_ref, own_kx_ref, store_own)


FIRST, SECOND = (2 * sum(chunk) for chunk in X_GROUPS)


def first_points(planes, own, far):
    return pl.pallas_call(
        first_kernel,
        out_shape=(
            jax.ShapeDtypeStruct((FIRST, G_DEV), F32),
            jax.ShapeDtypeStruct((FIRST, G_DEV), BF16),
        ),
        scratch_shapes=[pltpu.VMEM((FIRST * N, WIDE), BF16)],
        compiler_params=pltpu.CompilerParams(vmem_limit_bytes=16 << 20),
        cost_estimate=pl.CostEstimate(
            flops=100_000_000, bytes_accessed=100_000, transcendentals=0
        ),
        name="first_points",
    )(planes, x_table(FIRST // 2), *own, *far)


def second_far_points(planes, far, first):
    return pl.pallas_call(
        second_far_kernel,
        out_shape=(
            jax.ShapeDtypeStruct((FIRST + SECOND, G_DEV), BF16),
            jax.ShapeDtypeStruct((SECOND * N, WIDE), BF16),
            jax.ShapeDtypeStruct((16, 128), F32),
        ),
        compiler_params=pltpu.CompilerParams(vmem_limit_bytes=16 << 20),
        cost_estimate=pl.CostEstimate(
            flops=100_000_000, bytes_accessed=100_000, transcendentals=0
        ),
        name="second_far_points",
    )(planes, x_table(X_GROUPS[1][0]), *far, first)


def second_own_points(low, own):
    return pl.pallas_call(
        second_own_kernel,
        out_shape=jax.ShapeDtypeStruct((SECOND, G_DEV), F32),
        compiler_params=pltpu.CompilerParams(vmem_limit_bytes=16 << 20),
        cost_estimate=pl.CostEstimate(
            flops=2_400_000_000, bytes_accessed=1_300_000, transcendentals=0
        ),
        name="second_own_points",
    )(low, *own)


def split_kernel(own0_ref, own1_ref, far_ref, block_ref, out_ref):
    parts = [[], [], [], []]
    first, place = 0, 0
    for own_ref, chunk in zip((own0_ref, own1_ref), X_GROUPS):
        first = 0
        for size in chunk:
            own_r = own_ref[first : first + size, :]
            own_i = own_ref[first + size : first + 2 * size, :]
            far_r = far_ref[place : place + size, :].astype(F32)
            far_i = far_ref[place + size : place + 2 * size, :].astype(F32)
            parts[0].append(own_r + far_r)
            parts[1].append(own_i + far_i)
            parts[2].append(own_i - far_i)
            parts[3].append(far_r - own_r)
            first += 2 * size
            place += 2 * size
    pairs = jnp.concatenate(sum(parts, []), axis=0).astype(BF16)
    block = block_ref[...].astype(BF16)
    for band in range(16):
        out_ref[band, :32, :] = pairs[:, band * 128 : (band + 1) * 128]
        out_ref[band, 32:, :] = block


def split_pairs(own0, own1, far, block):
    return pl.pallas_call(
        split_kernel,
        out_shape=jax.ShapeDtypeStruct((16, 48, 128), BF16),
        compiler_params=pltpu.CompilerParams(vmem_limit_bytes=8 << 20),
        cost_estimate=pl.CostEstimate(
            flops=1_000_000, bytes_accessed=500_000, transcendentals=0
        ),
        name="split",
    )(own0, own1, far, block)


def phase_cosine(phase):
    turns = jnp.floor((phase + 0.5) * (1.0 / N))
    rest = phase - N * turns
    angle = (N // 4 - jnp.minimum(rest, N - rest)) * (2.0 * math.pi / N)
    square = angle * angle
    series = -1.0 / 39916800.0
    for factor in (1.0 / 362880.0, -1.0 / 5040.0, 1.0 / 120.0, -1.0 / 6.0, 1.0):
        series = series * square + factor
    return angle * series


def block_kernel(*refs):
    waves_hbm, refs = refs[: 2 + len(SLOTS)], refs[2 + len(SLOTS) :]
    info_ref, marks_hbm, _, out_hbm, *refs = refs
    waves_ref, product_ref, marks_ref, tail_ref, sums_ref, wave_sems, sems = refs
    waves_in = [
        pltpu.make_async_copy(wave, waves_ref.at[i], wave_sems.at[i])
        for i, wave in enumerate(waves_hbm)
    ]
    place = marks_hbm.at[:, pl.ds(0, 8), pl.ds(SPARE, 128)]
    marks_in = pltpu.make_async_copy(place, marks_ref, sems.at[1])
    marks_in.start()
    for move in waves_in:
        move.start()
    tail = (slice(None), pl.ds(0, 16), pl.ds(SPARE, 128))
    fetch = pltpu.make_async_copy(out_hbm.at[tail], tail_ref, sems.at[0])
    fetch.start()
    info = info_ref[...]
    marks_in.wait()
    marks = marks_ref[...].astype(F32).sum(axis=0)
    used = info[3:4] != 0.0
    cell = jnp.where(used, 256.0 * marks[0:1] + marks[1:2], 0.0)
    block_x = jnp.floor((cell + 0.5) * (1.0 / 576.0))
    cell = cell - 576.0 * block_x
    block_y = jnp.floor((cell + 0.5) * (1.0 / N))
    block_z = cell - N * block_y
    block_y = block_y + info[0:1]
    lane = lax.broadcasted_iota(jnp.int32, (Y6 * N, 128), 0).astype(F32)
    y6 = jnp.floor((lane + 0.5) * (1.0 / N))
    lanes = phase_cosine(16.0 * y6 * block_y + (lane - N * y6) * block_z + info[1:2]).astype(BF16)
    rows = X6 * Y16
    row = lax.broadcasted_iota(jnp.int32, (rows, 128), 0).astype(F32)
    x = jnp.floor((row + 0.5) * (1.0 / Y16))
    turned = phase_cosine((x + info[4:5]) * block_x + (row - Y16 * x) * block_y + info[2:3])
    turned = turned * info[3:4]
    for move in waves_in:
        move.wait()
    for half in range(2):
        for item, slot in enumerate(SLOTS):
            index = half * len(SLOTS) + item
            product_ref[index * rows : (index + 1) * rows, :] = (
                waves_ref[half] * waves_ref[2 + slot]
            )
    sums = jnp.dot(product_ref[...], lanes, preferred_element_type=F32)
    sums_ref[...] = (sums.reshape(2 * ITEMS, rows, 128) * turned[None]).sum(axis=1)
    sums = sums_ref[...]
    sums = sums + pltpu.roll(sums, 128 - NBLOCK, 1)
    high = sums.astype(BF16).astype(F32)
    rest = pltpu.roll(sums - high, NBLOCK, 1)
    spot = lax.broadcasted_iota(jnp.int32, sums.shape, 1)
    sums = jnp.where(spot // NBLOCK % 2 == 0, high, rest)
    fetch.wait()
    tails = tail_ref[...].astype(F32)
    tail_ref[...] = jnp.where((spot >= 32) & (spot < 96), sums, tails).astype(BF16)
    store = pltpu.make_async_copy(tail_ref, out_hbm.at[tail], sems.at[2])
    store.start()
    store.wait()


def with_block_sums(v, c, info, arrived, planes):
    waves = [in_hbm(wave) for wave in (*v, *c)]
    inputs = (*waves, info, arrived, planes)
    return pl.pallas_call(
        block_kernel,
        out_shape=pltpu.HBM(planes.shape, planes.dtype),
        in_specs=[HBM] * len(waves) + [VMEM, ANY, HBM],
        out_specs=HBM,
        input_output_aliases={len(inputs) - 1: 0},
        scratch_shapes=[
            pltpu.VMEM((len(waves), X6 * Y16, Y6 * N), BF16),
            pltpu.VMEM((2 * ITEMS * X6 * Y16, Y6 * N), BF16),
            pltpu.VMEM((SLABS, 8, 128), BF16),
            pltpu.VMEM((SLABS, 16, 128), BF16),
            pltpu.VMEM((2 * ITEMS, 128), F32),
            pltpu.SemaphoreType.DMA((len(waves),)),
            pltpu.SemaphoreType.DMA((3,)),
        ],
        compiler_params=pltpu.CompilerParams(vmem_limit_bytes=10 << 20),
        cost_estimate=pl.CostEstimate(
            flops=10_000_000, bytes_accessed=100_000, transcendentals=0
        ),
        name="block",
    )(*inputs)


def sum_kernel(pairs_ref, weight_ref, column_ref, out_ref):
    pairs = 16 * 16
    block = pairs_ref[:, 32:, :].reshape(pairs, 128)
    total = None
    for part in range(2):
        left = pairs_ref[:, 16 * part : 16 * (part + 1), :].reshape(pairs, 128)
        columns = jnp.dot(block, column_ref[part], preferred_element_type=F32)
        right = (columns * weight_ref[...]).astype(BF16)
        term = lax.dot_general(
            left, right, (((0,), (0,)), ((), ())), preferred_element_type=F32
        )
        total = term if total is None else total + term
    out_ref[...] = total


def wave_rows(wave):
    return wave.reshape(X6, Y6, Y16, N).transpose(0, 2, 1, 3).reshape(X6 * Y16, Y6 * N)


def per_device(
    valence_wave,
    conduction_wave,
    valence_index,
    occupied_energy,
    conduction_energy,
    frequency,
    gvec_cell,
    block_cell,
):
    col = lax.axis_index(COL)
    wave_v = wave_rows(valence_wave)
    wave_c = wave_rows(conduction_wave)
    ahead = [(i, (i + 1) % 8) for i in range(8)]
    behind = [(i, (i + 7) % 8) for i in range(8)]
    v = [wave_v, lax.ppermute(wave_v, "yl", [(0, 1), (1, 0)])]
    c = [wave_c] + [None] * 7
    for slot in (1, 2, 3, 4):
        c[slot] = lax.ppermute(c[slot - 1], "z", ahead)
        if slot < 4:
            c[8 - slot] = lax.ppermute(c[(9 - slot) % 8], "z", behind)

    mirror_of = [(k, SLABS - 1 - k) for k in range(SLABS)]
    far_cell = lax.ppermute(gvec_cell, COL, mirror_of).reshape(16, 128)
    spots = jnp.arange(128, dtype=jnp.int32)
    cell = jnp.where((spots % NBLOCK == col) & (spots >= 32), block_cell[0], 0)
    marks = jnp.concatenate([jnp.stack([cell // 256, cell % 256]), jnp.zeros((6, 128), jnp.int32)])
    planes0, far_cell = planes_of(
        0, v, c, marks=(marks.astype(F32),), through=(far_cell,), after=(c[7],)
    )
    sent0 = lax.all_to_all(planes0, COL, 0, 0, tiled=True)
    (planes1,) = planes_of(1, v, c)
    (planes1,) = planes_of(2, v, c, buffer=(planes1,))
    (planes1,) = planes_of(3, v, c, buffer=(planes1,))

    group = np.arange(128) // NBLOCK - 2
    used = (group >= 0) & (group < 4)
    info = np.zeros((8, 128), np.float32)
    info[0] = np.arange(128) % NBLOCK * 6
    info[1] = np.where(group % 2 == 1, N // 4, 0)
    info[2] = np.where(group == 1, 3 * N // 4, np.where(group == 2, N // 4, 0))
    info[3] = np.where(used, 1.0 / (N * math.sqrt(N)), 0.0)
    info = info + jnp.where(np.arange(8)[:, None] == 4, (X6 * col).astype(F32), 0.0)
    planes1 = with_block_sums(v, c, info, sent0, planes1)
    sent1 = lax.all_to_all(planes1, COL, 0, 0, tiled=True)

    far_cell = far_cell.reshape(G_DEV)
    far_x, far_y, far_z = far_cell // 576, far_cell // N % 6, far_cell % N
    own = ((gvec_cell % 576)[None], (gvec_cell // 576)[None])
    far = (((6 - far_y) * N + (N - far_z) % N)[None], ((N - far_x) % N)[None])

    pair_v, pair_c = pair_table()
    occupied = jnp.arange(occupied_energy.shape[0], dtype=jnp.int32)
    valence_energy = jnp.sum(
        jnp.where(valence_index[:, None] == occupied[None, :], occupied_energy[None, :], 0.0),
        axis=1,
    )
    count_v, count_c = valence_index.shape[0], conduction_energy.shape[0]
    energy_v = jnp.sum(
        jnp.where(pair_v[:, None] == np.arange(count_v)[None], valence_energy[None], 0.0), axis=1
    )
    energy_c = jnp.sum(
        jnp.where(pair_c[:, None] == np.arange(count_c)[None], conduction_energy[None], 0.0),
        axis=1,
    )
    gap = (energy_c - energy_v)[:, None]
    omega = jnp.repeat(frequency, 2 * NBLOCK)[None]
    weight = -4.0 * gap / (gap * gap + omega * omega) * (1.0 / math.sqrt(count_v * count_c))

    own0, far0 = first_points(sent0, own, far)
    mirrored, low, columns = second_far_points(sent1, far, far0)
    mirrored = lax.ppermute(mirrored, COL, mirror_of)
    own1 = second_own_points(low, own)
    pairs = split_pairs(own0, own1, mirrored, columns)
    pairs = lax.all_to_all(pairs, BAND, 0, 0, tiled=True)
    return pl.pallas_call(
        sum_kernel,
        out_shape=jax.ShapeDtypeStruct((128, 128), F32),
        compiler_params=pltpu.CompilerParams(vmem_limit_bytes=4 << 20),
        name="pair_sum",
    )(pairs, weight, column_tables())


def solution(mesh):
    fine = Mesh(
        mesh.devices.reshape(8, 2, 4, 2, 2), ("z", "yl", "x", "yh", "co")
    )
    return jax.shard_map(
        per_device,
        mesh=fine,
        in_specs=(
            P(BAND, COL, None),
            P(BAND, COL, None),
            P(),
            P(),
            P(),
            P(),
            P(COL),
            P(COL),
        ),
        out_specs=P(COL + BAND, None),
        check_vma=False,
    )
```

```python
import functools
import math

import jax
import jax.numpy as jnp
import ml_dtypes
import numpy as np
from jax import lax
from jax.experimental import pallas as pl
from jax.experimental.pallas import tpu as pltpu
from jax.sharding import Mesh
from jax.sharding import PartitionSpec as P

BF16 = jnp.bfloat16
F32 = jnp.float32

N = 96
SLABS = 16
X6 = 6
Y6 = 6
Y16 = 16
K7 = 7
FLAT = K7 * N
WIDE = 768
GROUPS = ((0, 1), (6, 2), (7, 3), (5, 4))
SLOTS = [slot for group in GROUPS for slot in group]
ITEMS = len(SLOTS)
SPARE = 640
G_DEV = 2048
NBLOCK = 16
TILE = 512
CHUNK_ROWS = (24, 72)
X_GROUPS = ((2,), (2, 2, 2))

BAND = ("z", "yl")
COL = ("x", "yh", "co")


def unit(phase, period):
    angle = 2.0 * np.pi * (np.asarray(phase) % period) / period
    return np.cos(angle), -np.sin(angle)


def bf16(table):
    return np.asarray(table, np.float32).astype(ml_dtypes.bfloat16)


@functools.cache
def lane_table():
    y6, z = np.divmod(np.arange(Y6 * N), N)
    k7, kz = np.divmod(np.arange(FLAT), N)
    phase = 16 * y6[:, None] * k7[None, :] + z[:, None] * kz[None, :]
    cosine, sine = unit(phase, N)
    table = np.zeros((Y6 * N, 2 * WIDE))
    table[:, :FLAT] = cosine
    table[:, WIDE : WIDE + FLAT] = sine
    return bf16(table)


@functools.cache
def twiddle_table():
    k7 = np.arange(FLAT) // N
    cosine, sine = unit(np.arange(Y16)[:, None] * k7[None, :], N)
    table = np.zeros((2, Y16, WIDE), np.float32)
    table[0, :, :FLAT] = cosine / N
    table[1, :, :FLAT] = sine / N
    return table


@functools.cache
def row_table(items):
    table = np.zeros((SLABS, items, 2, X6, 2, items, X6, Y16))
    cosine, sine = unit(np.arange(SLABS)[:, None] * np.arange(Y16)[None, :], SLABS)
    for item in range(items):
        for x in range(X6):
            table[:, item, 0, x, 0, item, x] = cosine
            table[:, item, 0, x, 1, item, x] = -sine
            table[:, item, 1, x, 0, item, x] = sine
            table[:, item, 1, x, 1, item, x] = cosine
    return bf16(table.reshape(SLABS * items * 2 * X6, 2 * items * X6 * Y16))


@functools.cache
def x_table(items):
    table = np.zeros((2, items, N, SLABS, items, 2, X6))
    cosine, sine = unit(np.arange(N)[:, None] * np.arange(N)[None, :], N)
    cosine = (cosine * 0.5 / math.sqrt(N)).reshape(N, SLABS, X6)
    sine = (sine * 0.5 / math.sqrt(N)).reshape(N, SLABS, X6)
    for item in range(items):
        table[0, item, :, :, item, 0] = cosine
        table[0, item, :, :, item, 1] = -sine
        table[1, item, :, :, item, 0] = sine
        table[1, item, :, :, item, 1] = cosine
    return bf16(table.reshape(2 * items * N, SLABS * items * 2 * X6))


@functools.cache
def pair_table():
    valence, conduction = [], []
    for band in range(16):
        z, yl = divmod(band, 2)
        for half in range(2):
            for slot in SLOTS:
                valence.append(z * 2 + (yl ^ half))
                conduction.append((z - slot) % 8 * 2 + yl)
    return np.array(valence), np.array(conduction)


@functools.cache
def column_tables():
    tables = np.zeros((2, 128, 4, 2, NBLOCK))
    m = np.arange(NBLOCK)
    tables[0, 32 + m, :, 0, m] = 1.0
    tables[0, 64 + m, :, 1, m] = -1.0
    tables[1, 64 + m, :, 0, m] = 1.0
    tables[1, 32 + m, :, 1, m] = 1.0
    return bf16(tables.reshape(2, 128, 128))


VMEM = pl.BlockSpec(memory_space=pltpu.VMEM)
HBM = pl.BlockSpec(memory_space=pltpu.HBM)
ANY = pl.BlockSpec(memory_space=pl.ANY)
SLAB_CUTS = 4


def in_hbm(x):
    return pltpu.with_memory_space_constraint(x, pltpu.HBM)


PLANES_FLOPS = (30_000_000, 30_000_000, 30_000_000, 30_000_000)


def whole_wave(arrived, slot):
    if slot == 4:
        half = X6 * Y16 // 2
        return jnp.concatenate([arrived[4][:half, :], arrived[8][half:, :]], axis=0)
    return arrived[slot][...]


def plane_kernel(*refs, slots, items, first, through, chained, marked):
    refs = list(refs)
    take = lambda count: [refs.pop(0) for _ in range(count)]
    v0_ref, v1_ref = take(2)
    waves_c = take(len(slots))
    lane_ref, twiddle_ref = take(2)
    marks = take(marked)
    (row_hbm,) = take(1)
    kept = take(through)
    take(chained)
    (out_ref,) = take(1)
    kept_out = take(through)
    low_ref, slab_ref, row_ref, slab_sems, keep_sems, row_sem = refs
    row_in = pltpu.make_async_copy(row_hbm, row_ref, row_sem)
    row_in.start()
    moves = [
        pltpu.make_async_copy(source, target, keep_sems.at[i])
        for i, (source, target) in enumerate(zip(kept, kept_out))
    ]
    for move in moves:
        move.start()
    rows = X6 * Y16
    twiddle_c = twiddle_ref[0][None]
    twiddle_s = twiddle_ref[1][None]
    arrived = dict(zip(slots, waves_c))
    for index, slot in enumerate(slots[:items]):
        wave_c = whole_wave(arrived, slot)
        pairs = jnp.concatenate([v0_ref[...] * wave_c, v1_ref[...] * wave_c], axis=0)
        moved = jnp.dot(pairs, lane_ref[...], preferred_element_type=F32)
        real = moved[:rows, :WIDE] - moved[rows:, WIDE:]
        imag = moved[:rows, WIDE:] + moved[rows:, :WIDE]
        real = real.reshape(X6, Y16, WIDE)
        imag = imag.reshape(X6, Y16, WIDE)
        turned_r = real * twiddle_c - imag * twiddle_s
        turned_i = real * twiddle_s + imag * twiddle_c
        low_ref[index * rows : (index + 1) * rows, :] = turned_r.reshape(rows, WIDE).astype(BF16)
        index += items
        low_ref[index * rows : (index + 1) * rows, :] = turned_i.reshape(rows, WIDE).astype(BF16)
    row_in.wait()
    count = SLABS // SLAB_CUTS
    size = items * 2 * X6
    for part in range(SLAB_CUTS):
        slabs = slice(part * count, (part + 1) * count)
        planes = jnp.dot(
            row_ref[part * count * size : (part + 1) * count * size, :],
            low_ref[...],
            preferred_element_type=F32,
        ).reshape(count, size, WIDE)
        slab_ref[slabs] = planes.astype(BF16)
        if marks:
            tail = planes[:, :8, SPARE:] + marks[0][...][None]
            slab_ref[slabs, :8, SPARE:] = tail.astype(BF16)
        window = pl.ds(part * count, count)
        moves.append(
            pltpu.make_async_copy(
                slab_ref.at[window],
                out_ref.at[window, pl.ds(first, size)],
                slab_sems.at[part],
            )
        )
        moves[-1].start()
    for move in moves:
        move.wait()


def planes_of(group, v, c, marks=(), through=(), after=(), buffer=()):
    slots = GROUPS[group]
    items = len(slots)
    slots = slots + (8,) if 4 in slots else slots
    first = max(group - 1, 0) * items * 2 * X6
    rows = CHUNK_ROWS[min(group, 1)]
    inputs = (
        *v,
        *(c[slot] for slot in slots),
        lane_table(),
        twiddle_table(),
        *marks,
        in_hbm(jnp.asarray(row_table(items))),
        *through,
        *after,
        *buffer,
    )
    outside = len(through) + len(after) + len(buffer)
    return pl.pallas_call(
        functools.partial(
            plane_kernel,
            slots=slots,
            items=items,
            first=first,
            through=len(through),
            chained=len(after) + len(buffer),
            marked=len(marks),
        ),
        out_shape=[
            pltpu.HBM((SLABS, rows, WIDE), BF16),
            *(pltpu.HBM(x.shape, x.dtype) for x in through),
        ],
        in_specs=[VMEM] * (len(inputs) - outside)
        + [ANY] * (len(through) + len(after))
        + [HBM] * len(buffer),
        out_specs=[HBM] * (1 + len(through)),
        input_output_aliases={len(inputs) - 1: 0} if buffer else {},
        scratch_shapes=[
            pltpu.VMEM((2 * items * X6 * Y16, WIDE), BF16),
            pltpu.VMEM((SLABS, items * 2 * X6, WIDE), BF16),
            pltpu.VMEM((SLABS * items * 2 * X6, 2 * items * X6 * Y16), BF16),
            pltpu.SemaphoreType.DMA((SLAB_CUTS,)),
            pltpu.SemaphoreType.DMA((max(len(through), 1),)),
            pltpu.SemaphoreType.DMA,
        ],
        compiler_params=pltpu.CompilerParams(vmem_limit_bytes=16 << 20),
        cost_estimate=pl.CostEstimate(
            flops=PLANES_FLOPS[group] * items, bytes_accessed=100_000, transcendentals=0
        ),
        name="planes",
    )(*inputs)


def pick(density_ref, flat_ref, kx_ref, store):
    rows = density_ref.shape[0]

    def body(step, carry):
        lanes = pl.ds(pl.multiple_of(step * TILE, TILE), TILE)
        spot = lax.broadcasted_iota(jnp.int32, (WIDE, TILE), 0)
        chosen = jnp.where(spot == flat_ref[:, lanes], 1.0, 0.0).astype(BF16)
        values = jnp.dot(density_ref[...], chosen, preferred_element_type=F32)
        kx = lax.broadcasted_iota(jnp.int32, (N, TILE), 0) == kx_ref[:, lanes]
        values = jnp.where(kx[None], values.reshape(rows // N, N, TILE), 0.0)
        store(lanes, values.sum(axis=1))
        return carry

    lax.fori_loop(0, G_DEV // TILE, body, 0, unroll=True)


def transform_x(chunk, t_ref, x_refs, low):
    first, place = 0, 0
    for items, x_ref in zip(X_GROUPS[chunk], x_refs):
        size = items * 2 * X6
        planes = t_ref[:, first : first + size, :]
        if size % 16:
            planes = planes.astype(F32)
        planes = planes.reshape(SLABS * size, WIDE).astype(BF16)
        rows = 2 * items * N
        low[place : place + rows, :] = jnp.dot(
            x_ref[...], planes, preferred_element_type=F32
        ).astype(BF16)
        first += size
        place += rows


def first_kernel(
    t_ref, x_ref, own_ref, own_kx_ref, far_ref, far_kx_ref, own_out, far_out, low
):
    transform_x(0, t_ref, (x_ref,), low)

    def store_far(lanes, values):
        far_out[:, lanes] = values.astype(BF16)

    def store_own(lanes, values):
        own_out[:, lanes] = values

    pick(low, far_ref, far_kx_ref, store_far)
    pick(low, own_ref, own_kx_ref, store_own)


def second_far_kernel(
    t_ref, x_ref, far_ref, far_kx_ref, first_ref, far_out, low, block_out
):
    transform_x(1, t_ref, (x_ref,) * len(X_GROUPS[1]), low)
    rows = first_ref.shape[0]
    far_out[:rows, :] = first_ref[...]

    def store_far(lanes, values):
        far_out[rows:, lanes] = values.astype(BF16)

    pick(low, far_ref, far_kx_ref, store_far)
    spare = t_ref[:, :16, SPARE:].astype(F32).sum(axis=0)
    spare = spare + pltpu.roll(spare, 128 - NBLOCK, 1)
    block_out[...] = spare


def second_own_kernel(low, own_ref, own_kx_ref, own_out):
    def store_own(lanes, values):
        own_out[:, lanes] = values

    pick(low, own_ref, own_kx_ref, store_own)


FIRST, SECOND = (2 * sum(chunk) for chunk in X_GROUPS)


def first_points(planes, own, far):
    return pl.pallas_call(
        first_kernel,
        out_shape=(
            jax.ShapeDtypeStruct((FIRST, G_DEV), F32),
            jax.ShapeDtypeStruct((FIRST, G_DEV), BF16),
        ),
        scratch_shapes=[pltpu.VMEM((FIRST * N, WIDE), BF16)],
        compiler_params=pltpu.CompilerParams(vmem_limit_bytes=16 << 20),
        cost_estimate=pl.CostEstimate(
            flops=100_000_000, bytes_accessed=100_000, transcendentals=0
        ),
        name="first_points",
    )(planes, x_table(FIRST // 2), *own, *far)


def second_far_points(planes, far, first):
    return pl.pallas_call(
        second_far_kernel,
        out_shape=(
            jax.ShapeDtypeStruct((FIRST + SECOND, G_DEV), BF16),
            jax.ShapeDtypeStruct((SECOND * N, WIDE), BF16),
            jax.ShapeDtypeStruct((16, 128), F32),
        ),
        compiler_params=pltpu.CompilerParams(vmem_limit_bytes=16 << 20),
        cost_estimate=pl.CostEstimate(
            flops=100_000_000, bytes_accessed=100_000, transcendentals=0
        ),
        name="second_far_points",
    )(planes, x_table(X_GROUPS[1][0]), *far, first)


def second_own_points(low, own):
    return pl.pallas_call(
        second_own_kernel,
        out_shape=jax.ShapeDtypeStruct((SECOND, G_DEV), F32),
        compiler_params=pltpu.CompilerParams(vmem_limit_bytes=16 << 20),
        cost_estimate=pl.CostEstimate(
            flops=2_400_000_000, bytes_accessed=1_300_000, transcendentals=0
        ),
        name="second_own_points",
    )(low, *own)


def split_kernel(own0_ref, own1_ref, far_ref, block_ref, out_ref):
    parts = [[], [], [], []]
    first, place = 0, 0
    for own_ref, chunk in zip((own0_ref, own1_ref), X_GROUPS):
        first = 0
        for size in chunk:
            own_r = own_ref[first : first + size, :]
            own_i = own_ref[first + size : first + 2 * size, :]
            far_r = far_ref[place : place + size, :].astype(F32)
            far_i = far_ref[place + size : place + 2 * size, :].astype(F32)
            parts[0].append(own_r + far_r)
            parts[1].append(own_i + far_i)
            parts[2].append(own_i - far_i)
            parts[3].append(far_r - own_r)
            first += 2 * size
            place += 2 * size
    pairs = jnp.concatenate(sum(parts, []), axis=0).astype(BF16)
    block = block_ref[...].astype(BF16)
    for band in range(16):
        out_ref[band, :32, :] = pairs[:, band * 128 : (band + 1) * 128]
        out_ref[band, 32:, :] = block


def split_pairs(own0, own1, far, block):
    return pl.pallas_call(
        split_kernel,
        out_shape=jax.ShapeDtypeStruct((16, 48, 128), BF16),
        compiler_params=pltpu.CompilerParams(vmem_limit_bytes=8 << 20),
        cost_estimate=pl.CostEstimate(
            flops=1_000_000, bytes_accessed=500_000, transcendentals=0
        ),
        name="split",
    )(own0, own1, far, block)


def phase_cosine(phase):
    turns = jnp.floor((phase + 0.5) * (1.0 / N))
    rest = phase - N * turns
    angle = (N // 4 - jnp.minimum(rest, N - rest)) * (2.0 * math.pi / N)
    square = angle * angle
    series = -1.0 / 39916800.0
    for factor in (1.0 / 362880.0, -1.0 / 5040.0, 1.0 / 120.0, -1.0 / 6.0, 1.0):
        series = series * square + factor
    return angle * series


def block_kernel(*refs):
    waves_hbm, refs = refs[:11], refs[11:]
    info_ref, marks_hbm, _, out_hbm, *refs = refs
    waves_ref, product_ref, marks_ref, tail_ref, sums_ref, wave_sems, sems = refs
    waves_in = [
        pltpu.make_async_copy(wave, waves_ref.at[i], wave_sems.at[i])
        for i, wave in enumerate(waves_hbm)
    ]
    place = marks_hbm.at[:, pl.ds(0, 8), pl.ds(SPARE, 128)]
    marks_in = pltpu.make_async_copy(place, marks_ref, sems.at[1])
    marks_in.start()
    for move in waves_in:
        move.start()
    tail = (slice(None), pl.ds(0, 16), pl.ds(SPARE, 128))
    fetch = pltpu.make_async_copy(out_hbm.at[tail], tail_ref, sems.at[0])
    fetch.start()
    info = info_ref[...]
    marks_in.wait()
    marks = marks_ref[...].astype(F32).sum(axis=0)
    used = info[3:4] != 0.0
    cell = jnp.where(used, 256.0 * marks[0:1] + marks[1:2], 0.0)
    block_x = jnp.floor((cell + 0.5) * (1.0 / 576.0))
    cell = cell - 576.0 * block_x
    block_y = jnp.floor((cell + 0.5) * (1.0 / N))
    block_z = cell - N * block_y
    block_y = block_y + info[0:1]
    lane = lax.broadcasted_iota(jnp.int32, (Y6 * N, 128), 0).astype(F32)
    y6 = jnp.floor((lane + 0.5) * (1.0 / N))
    lanes = phase_cosine(16.0 * y6 * block_y + (lane - N * y6) * block_z + info[1:2]).astype(BF16)
    rows = X6 * Y16
    row = lax.broadcasted_iota(jnp.int32, (rows, 128), 0).astype(F32)
    x = jnp.floor((row + 0.5) * (1.0 / Y16))
    turned = phase_cosine((x + info[4:5]) * block_x + (row - Y16 * x) * block_y + info[2:3])
    turned = turned * info[3:4]
    for move in waves_in:
        move.wait()
    arrived = {slot: waves_ref.at[2 + slot] for slot in range(9)}
    for half in range(2):
        for item, slot in enumerate(SLOTS):
            index = half * len(SLOTS) + item
            product_ref[index * rows : (index + 1) * rows, :] = waves_ref[half] * whole_wave(
                arrived, slot
            )
    sums = jnp.dot(product_ref[...], lanes, preferred_element_type=F32)
    sums_ref[...] = (sums.reshape(2 * ITEMS, rows, 128) * turned[None]).sum(axis=1)
    sums = sums_ref[...]
    sums = sums + pltpu.roll(sums, 128 - NBLOCK, 1)
    high = sums.astype(BF16).astype(F32)
    rest = pltpu.roll(sums - high, NBLOCK, 1)
    spot = lax.broadcasted_iota(jnp.int32, sums.shape, 1)
    sums = jnp.where(spot // NBLOCK % 2 == 0, high, rest)
    fetch.wait()
    tails = tail_ref[...].astype(F32)
    tail_ref[...] = jnp.where((spot >= 32) & (spot < 96), sums, tails).astype(BF16)
    store = pltpu.make_async_copy(tail_ref, out_hbm.at[tail], sems.at[2])
    store.start()
    store.wait()


def with_block_sums(v, c, info, arrived, planes):
    waves = [in_hbm(wave) for wave in (*v, *c)]
    inputs = (*waves, info, arrived, planes)
    return pl.pallas_call(
        block_kernel,
        out_shape=pltpu.HBM(planes.shape, planes.dtype),
        in_specs=[HBM] * len(waves) + [VMEM, ANY, HBM],
        out_specs=HBM,
        input_output_aliases={len(inputs) - 1: 0},
        scratch_shapes=[
            pltpu.VMEM((len(waves), X6 * Y16, Y6 * N), BF16),
            pltpu.VMEM((2 * ITEMS * X6 * Y16, Y6 * N), BF16),
            pltpu.VMEM((SLABS, 8, 128), BF16),
            pltpu.VMEM((SLABS, 16, 128), BF16),
            pltpu.VMEM((2 * ITEMS, 128), F32),
            pltpu.SemaphoreType.DMA((len(waves),)),
            pltpu.SemaphoreType.DMA((3,)),
        ],
        compiler_params=pltpu.CompilerParams(vmem_limit_bytes=10 << 20),
        cost_estimate=pl.CostEstimate(
            flops=10_000_000, bytes_accessed=100_000, transcendentals=0
        ),
        name="block",
    )(*inputs)


def sum_kernel(pairs_ref, weight_ref, column_ref, out_ref):
    pairs = 16 * 16
    block = pairs_ref[:, 32:, :].reshape(pairs, 128)
    total = None
    for part in range(2):
        left = pairs_ref[:, 16 * part : 16 * (part + 1), :].reshape(pairs, 128)
        columns = jnp.dot(block, column_ref[part], preferred_element_type=F32)
        right = (columns * weight_ref[...]).astype(BF16)
        term = lax.dot_general(
            left, right, (((0,), (0,)), ((), ())), preferred_element_type=F32
        )
        total = term if total is None else total + term
    out_ref[...] = total


def wave_rows(wave):
    return wave.reshape(X6, Y6, Y16, N).transpose(0, 2, 1, 3).reshape(X6 * Y16, Y6 * N)


def per_device(
    valence_wave,
    conduction_wave,
    valence_index,
    occupied_energy,
    conduction_energy,
    frequency,
    gvec_cell,
    block_cell,
):
    col = lax.axis_index(COL)
    wave_v = wave_rows(valence_wave)
    wave_c = wave_rows(conduction_wave)
    ahead = [(i, (i + 1) % 8) for i in range(8)]
    behind = [(i, (i + 7) % 8) for i in range(8)]
    v = [wave_v, lax.ppermute(wave_v, "yl", [(0, 1), (1, 0)])]
    c = [wave_c] + [None] * 8
    for slot in (1, 2, 3, 4):
        c[slot] = lax.ppermute(c[slot - 1], "z", ahead)
        if slot < 4:
            c[8 - slot] = lax.ppermute(c[(9 - slot) % 8], "z", behind)
    c[8] = lax.ppermute(c[5], "z", behind)

    mirror_of = [(k, SLABS - 1 - k) for k in range(SLABS)]
    far_cell = lax.ppermute(gvec_cell, COL, mirror_of).reshape(16, 128)
    spots = jnp.arange(128, dtype=jnp.int32)
    cell = jnp.where((spots % NBLOCK == col) & (spots >= 32), block_cell[0], 0)
    marks = jnp.concatenate([jnp.stack([cell // 256, cell % 256]), jnp.zeros((6, 128), jnp.int32)])
    planes0, far_cell = planes_of(
        0, v, c, marks=(marks.astype(F32),), through=(far_cell,), after=(c[7],)
    )
    sent0 = lax.all_to_all(planes0, COL, 0, 0, tiled=True)
    (planes1,) = planes_of(1, v, c)
    (planes1,) = planes_of(2, v, c, buffer=(planes1,))
    (planes1,) = planes_of(3, v, c, buffer=(planes1,))

    group = np.arange(128) // NBLOCK - 2
    used = (group >= 0) & (group < 4)
    info = np.zeros((8, 128), np.float32)
    info[0] = np.arange(128) % NBLOCK * 6
    info[1] = np.where(group % 2 == 1, N // 4, 0)
    info[2] = np.where(group == 1, 3 * N // 4, np.where(group == 2, N // 4, 0))
    info[3] = np.where(used, 1.0 / (N * math.sqrt(N)), 0.0)
    info = info + jnp.where(np.arange(8)[:, None] == 4, (X6 * col).astype(F32), 0.0)
    planes1 = with_block_sums(v, c, info, sent0, planes1)
    sent1 = lax.all_to_all(planes1, COL, 0, 0, tiled=True)

    far_cell = far_cell.reshape(G_DEV)
    far_x, far_y, far_z = far_cell // 576, far_cell // N % 6, far_cell % N
    own = ((gvec_cell % 576)[None], (gvec_cell // 576)[None])
    far = (((6 - far_y) * N + (N - far_z) % N)[None], ((N - far_x) % N)[None])

    pair_v, pair_c = pair_table()
    occupied = jnp.arange(occupied_energy.shape[0], dtype=jnp.int32)
    valence_energy = jnp.sum(
        jnp.where(valence_index[:, None] == occupied[None, :], occupied_energy[None, :], 0.0),
        axis=1,
    )
    count_v, count_c = valence_index.shape[0], conduction_energy.shape[0]
    energy_v = jnp.sum(
        jnp.where(pair_v[:, None] == np.arange(count_v)[None], valence_energy[None], 0.0), axis=1
    )
    energy_c = jnp.sum(
        jnp.where(pair_c[:, None] == np.arange(count_c)[None], conduction_energy[None], 0.0),
        axis=1,
    )
    gap = (energy_c - energy_v)[:, None]
    omega = jnp.repeat(frequency, 2 * NBLOCK)[None]
    weight = -4.0 * gap / (gap * gap + omega * omega) * (1.0 / math.sqrt(count_v * count_c))

    own0, far0 = first_points(sent0, own, far)
    mirrored, low, columns = second_far_points(sent1, far, far0)
    mirrored = lax.ppermute(mirrored, COL, mirror_of)
    own1 = second_own_points(low, own)
    pairs = split_pairs(own0, own1, mirrored, columns)
    pairs = lax.all_to_all(pairs, BAND, 0, 0, tiled=True)
    return pl.pallas_call(
        sum_kernel,
        out_shape=jax.ShapeDtypeStruct((128, 128), F32),
        compiler_params=pltpu.CompilerParams(vmem_limit_bytes=4 << 20),
        name="pair_sum",
    )(pairs, weight, column_tables())


def solution(mesh):
    fine = Mesh(
        mesh.devices.reshape(8, 2, 4, 2, 2), ("z", "yl", "x", "yh", "co")
    )
    return jax.shard_map(
        per_device,
        mesh=fine,
        in_specs=(
            P(BAND, COL, None),
            P(BAND, COL, None),
            P(),
            P(),
            P(),
            P(),
            P(COL),
            P(COL),
        ),
        out_specs=P(COL + BAND, None),
        check_vma=False,
    )
```

```python
import functools
import math

import jax
import jax.numpy as jnp
import ml_dtypes
import numpy as np
from jax import lax
from jax.experimental import pallas as pl
from jax.experimental.pallas import tpu as pltpu
from jax.sharding import Mesh
from jax.sharding import PartitionSpec as P

BF16 = jnp.bfloat16
F32 = jnp.float32

N = 96
SLABS = 16
X6 = 6
Y6 = 6
Y16 = 16
K7 = 7
FLAT = K7 * N
WIDE = 768
GROUPS = ((0, 1), (7, 2), (6, 3), (5, 4))
SLOTS = [slot for group in GROUPS for slot in group]
ITEMS = len(SLOTS)
SPARE = 640
G_DEV = 2048
NBLOCK = 16
TILE = 512
ROWS = 48
X_GROUPS = ((2, 2), (2, 2))

BAND = ("z", "yl")
COL = ("x", "yh", "co")


def unit(phase, period):
    angle = 2.0 * np.pi * (np.asarray(phase) % period) / period
    return np.cos(angle), -np.sin(angle)


def bf16(table):
    return np.asarray(table, np.float32).astype(ml_dtypes.bfloat16)


@functools.cache
def lane_table():
    y6, z = np.divmod(np.arange(Y6 * N), N)
    k7, kz = np.divmod(np.arange(FLAT), N)
    phase = 16 * y6[:, None] * k7[None, :] + z[:, None] * kz[None, :]
    cosine, sine = unit(phase, N)
    table = np.zeros((Y6 * N, 2 * WIDE))
    table[:, :FLAT] = cosine
    table[:, WIDE : WIDE + FLAT] = sine
    return bf16(table)


@functools.cache
def twiddle_table():
    k7 = np.arange(FLAT) // N
    cosine, sine = unit(np.arange(Y16)[:, None] * k7[None, :], N)
    table = np.zeros((2, Y16, WIDE), np.float32)
    table[0, :, :FLAT] = cosine / N
    table[1, :, :FLAT] = sine / N
    return table


@functools.cache
def row_table(items):
    table = np.zeros((SLABS, items, 2, X6, 2, items, X6, Y16))
    cosine, sine = unit(np.arange(SLABS)[:, None] * np.arange(Y16)[None, :], SLABS)
    for item in range(items):
        for x in range(X6):
            table[:, item, 0, x, 0, item, x] = cosine
            table[:, item, 0, x, 1, item, x] = -sine
            table[:, item, 1, x, 0, item, x] = sine
            table[:, item, 1, x, 1, item, x] = cosine
    return bf16(table.reshape(SLABS * items * 2 * X6, 2 * items * X6 * Y16))


@functools.cache
def x_table(items):
    table = np.zeros((2, items, N, SLABS, items, 2, X6))
    cosine, sine = unit(np.arange(N)[:, None] * np.arange(N)[None, :], N)
    cosine = (cosine * 0.5 / math.sqrt(N)).reshape(N, SLABS, X6)
    sine = (sine * 0.5 / math.sqrt(N)).reshape(N, SLABS, X6)
    for item in range(items):
        table[0, item, :, :, item, 0] = cosine
        table[0, item, :, :, item, 1] = -sine
        table[1, item, :, :, item, 0] = sine
        table[1, item, :, :, item, 1] = cosine
    return bf16(table.reshape(2 * items * N, SLABS * items * 2 * X6))


@functools.cache
def pair_table():
    valence, conduction = [], []
    for band in range(16):
        z, yl = divmod(band, 2)
        for half in range(2):
            for slot in SLOTS:
                valence.append(z * 2 + (yl ^ half))
                conduction.append((z - slot) % 8 * 2 + yl)
    return np.array(valence), np.array(conduction)


@functools.cache
def column_tables():
    tables = np.zeros((2, 128, 4, 2, NBLOCK))
    m = np.arange(NBLOCK)
    tables[0, 32 + m, :, 0, m] = 1.0
    tables[0, 64 + m, :, 1, m] = -1.0
    tables[1, 64 + m, :, 0, m] = 1.0
    tables[1, 32 + m, :, 1, m] = 1.0
    return bf16(tables.reshape(2, 128, 128))


VMEM = pl.BlockSpec(memory_space=pltpu.VMEM)
HBM = pl.BlockSpec(memory_space=pltpu.HBM)
ANY = pl.BlockSpec(memory_space=pl.ANY)
SLAB_CUTS = 4


def in_hbm(x):
    return pltpu.with_memory_space_constraint(x, pltpu.HBM)


PLANES_FLOPS = (30_000_000, 30_000_000, 30_000_000, 30_000_000)


def plane_kernel(*refs, items, first, through, chained, marked):
    refs = list(refs)
    take = lambda count: [refs.pop(0) for _ in range(count)]
    v0_ref, v1_ref = take(2)
    waves_c = take(items)
    lane_ref, twiddle_ref, row_ref = take(3)
    marks = take(marked)
    kept = take(through)
    take(chained)
    (out_ref,) = take(1)
    kept_out = take(through)
    low_ref, slab_ref, slab_sems, keep_sems = refs
    moves = [
        pltpu.make_async_copy(source, target, keep_sems.at[i])
        for i, (source, target) in enumerate(zip(kept, kept_out))
    ]
    for move in moves:
        move.start()
    rows = X6 * Y16
    twiddle_c = twiddle_ref[0][None]
    twiddle_s = twiddle_ref[1][None]
    for index, c_ref in enumerate(waves_c):
        wave_c = c_ref[...]
        pairs = jnp.concatenate([v0_ref[...] * wave_c, v1_ref[...] * wave_c], axis=0)
        moved = jnp.dot(pairs, lane_ref[...], preferred_element_type=F32)
        real = moved[:rows, :WIDE] - moved[rows:, WIDE:]
        imag = moved[:rows, WIDE:] + moved[rows:, :WIDE]
        real = real.reshape(X6, Y16, WIDE)
        imag = imag.reshape(X6, Y16, WIDE)
        turned_r = real * twiddle_c - imag * twiddle_s
        turned_i = real * twiddle_s + imag * twiddle_c
        low_ref[index * rows : (index + 1) * rows, :] = turned_r.reshape(rows, WIDE).astype(BF16)
        index += items
        low_ref[index * rows : (index + 1) * rows, :] = turned_i.reshape(rows, WIDE).astype(BF16)
    count = SLABS // SLAB_CUTS
    size = items * 2 * X6
    for part in range(SLAB_CUTS):
        slabs = slice(part * count, (part + 1) * count)
        planes = jnp.dot(
            row_ref[part * count * size : (part + 1) * count * size, :],
            low_ref[...],
            preferred_element_type=F32,
        ).reshape(count, size, WIDE)
        slab_ref[slabs] = planes.astype(BF16)
        if marks:
            tail = planes[:, :8, SPARE:] + marks[0][...][None]
            slab_ref[slabs, :8, SPARE:] = tail.astype(BF16)
        window = pl.ds(part * count, count)
        moves.append(
            pltpu.make_async_copy(
                slab_ref.at[window],
                out_ref.at[window, pl.ds(first, size)],
                slab_sems.at[part],
            )
        )
        moves[-1].start()
    for move in moves:
        move.wait()


def planes_of(group, v, c, marks=(), through=(), after=(), buffer=()):
    slots = GROUPS[group]
    items = len(slots)
    first = group % 2 * items * 2 * X6
    inputs = (
        *v,
        *(c[slot] for slot in slots),
        lane_table(),
        twiddle_table(),
        row_table(items),
        *marks,
        *through,
        *after,
        *buffer,
    )
    outside = len(through) + len(after) + len(buffer)
    return pl.pallas_call(
        functools.partial(
            plane_kernel,
            items=items,
            first=first,
            through=len(through),
            chained=len(after) + len(buffer),
            marked=len(marks),
        ),
        out_shape=[
            pltpu.HBM((SLABS, ROWS, WIDE), BF16),
            *(pltpu.HBM(x.shape, x.dtype) for x in through),
        ],
        in_specs=[VMEM] * (len(inputs) - outside)
        + [ANY] * (len(through) + len(after))
        + [HBM] * len(buffer),
        out_specs=[HBM] * (1 + len(through)),
        input_output_aliases={len(inputs) - 1: 0} if buffer else {},
        scratch_shapes=[
            pltpu.VMEM((2 * items * X6 * Y16, WIDE), BF16),
            pltpu.VMEM((SLABS, items * 2 * X6, WIDE), BF16),
            pltpu.SemaphoreType.DMA((SLAB_CUTS,)),
            pltpu.SemaphoreType.DMA((max(len(through), 1),)),
        ],
        compiler_params=pltpu.CompilerParams(vmem_limit_bytes=16 << 20),
        cost_estimate=pl.CostEstimate(
            flops=PLANES_FLOPS[group] * items, bytes_accessed=100_000, transcendentals=0
        ),
        name="planes",
    )(*inputs)


def pick(density_ref, flat_ref, kx_ref, store):
    rows = density_ref.shape[0]

    def body(step, carry):
        lanes = pl.ds(pl.multiple_of(step * TILE, TILE), TILE)
        spot = lax.broadcasted_iota(jnp.int32, (WIDE, TILE), 0)
        chosen = jnp.where(spot == flat_ref[:, lanes], 1.0, 0.0).astype(BF16)
        values = jnp.dot(density_ref[...], chosen, preferred_element_type=F32)
        kx = lax.broadcasted_iota(jnp.int32, (N, TILE), 0) == kx_ref[:, lanes]
        values = jnp.where(kx[None], values.reshape(rows // N, N, TILE), 0.0)
        store(lanes, values.sum(axis=1))
        return carry

    lax.fori_loop(0, G_DEV // TILE, body, 0, unroll=True)


def transform_x(chunk, t_ref, x_refs, low):
    first, place = 0, 0
    for items, x_ref in zip(X_GROUPS[chunk], x_refs):
        size = items * 2 * X6
        planes = t_ref[:, first : first + size, :]
        if size % 16:
            planes = planes.astype(F32)
        planes = planes.reshape(SLABS * size, WIDE).astype(BF16)
        rows = 2 * items * N
        low[place : place + rows, :] = jnp.dot(
            x_ref[...], planes, preferred_element_type=F32
        ).astype(BF16)
        first += size
        place += rows


def first_kernel(
    t_ref, x_ref, own_ref, own_kx_ref, far_ref, far_kx_ref, own_out, far_out, low
):
    transform_x(0, t_ref, (x_ref,) * len(X_GROUPS[0]), low)

    def store_far(lanes, values):
        far_out[:, lanes] = values.astype(BF16)

    def store_own(lanes, values):
        own_out[:, lanes] = values

    pick(low, far_ref, far_kx_ref, store_far)
    pick(low, own_ref, own_kx_ref, store_own)


def second_far_kernel(
    t_ref, x_ref, far_ref, far_kx_ref, first_ref, far_out, low, block_out
):
    transform_x(1, t_ref, (x_ref,) * len(X_GROUPS[1]), low)
    rows = first_ref.shape[0]
    far_out[:rows, :] = first_ref[...]

    def store_far(lanes, values):
        far_out[rows:, lanes] = values.astype(BF16)

    pick(low, far_ref, far_kx_ref, store_far)
    spare = t_ref[:, :16, SPARE:].astype(F32).sum(axis=0)
    spare = spare + pltpu.roll(spare, 128 - NBLOCK, 1)
    block_out[...] = spare


def second_own_kernel(low, own_ref, own_kx_ref, own_out):
    def store_own(lanes, values):
        own_out[:, lanes] = values

    pick(low, own_ref, own_kx_ref, store_own)


FIRST, SECOND = (2 * sum(chunk) for chunk in X_GROUPS)


def first_points(planes, own, far):
    return pl.pallas_call(
        first_kernel,
        out_shape=(
            jax.ShapeDtypeStruct((FIRST, G_DEV), F32),
            jax.ShapeDtypeStruct((FIRST, G_DEV), BF16),
        ),
        scratch_shapes=[pltpu.VMEM((FIRST * N, WIDE), BF16)],
        compiler_params=pltpu.CompilerParams(vmem_limit_bytes=16 << 20),
        cost_estimate=pl.CostEstimate(
            flops=100_000_000, bytes_accessed=100_000, transcendentals=0
        ),
        name="first_points",
    )(planes, x_table(X_GROUPS[0][0]), *own, *far)


def second_far_points(planes, far, first):
    return pl.pallas_call(
        second_far_kernel,
        out_shape=(
            jax.ShapeDtypeStruct((FIRST + SECOND, G_DEV), BF16),
            jax.ShapeDtypeStruct((SECOND * N, WIDE), BF16),
            jax.ShapeDtypeStruct((16, 128), F32),
        ),
        compiler_params=pltpu.CompilerParams(vmem_limit_bytes=16 << 20),
        cost_estimate=pl.CostEstimate(
            flops=100_000_000, bytes_accessed=100_000, transcendentals=0
        ),
        name="second_far_points",
    )(planes, x_table(X_GROUPS[1][0]), *far, first)


def second_own_points(low, own):
    return pl.pallas_call(
        second_own_kernel,
        out_shape=jax.ShapeDtypeStruct((SECOND, G_DEV), F32),
        compiler_params=pltpu.CompilerParams(vmem_limit_bytes=16 << 20),
        cost_estimate=pl.CostEstimate(
            flops=2_400_000_000, bytes_accessed=1_300_000, transcendentals=0
        ),
        name="second_own_points",
    )(low, *own)


def split_kernel(own0_ref, own1_ref, far_ref, block_ref, out_ref):
    parts = [[], [], [], []]
    first, place = 0, 0
    for own_ref, chunk in zip((own0_ref, own1_ref), X_GROUPS):
        first = 0
        for size in chunk:
            own_r = own_ref[first : first + size, :]
            own_i = own_ref[first + size : first + 2 * size, :]
            far_r = far_ref[place : place + size, :].astype(F32)
            far_i = far_ref[place + size : place + 2 * size, :].astype(F32)
            parts[0].append(own_r + far_r)
            parts[1].append(own_i + far_i)
            parts[2].append(own_i - far_i)
            parts[3].append(far_r - own_r)
            first += 2 * size
            place += 2 * size
    pairs = jnp.concatenate(sum(parts, []), axis=0).astype(BF16)
    block = block_ref[...].astype(BF16)
    for band in range(16):
        out_ref[band, :32, :] = pairs[:, band * 128 : (band + 1) * 128]
        out_ref[band, 32:, :] = block


def split_pairs(own0, own1, far, block):
    return pl.pallas_call(
        split_kernel,
        out_shape=jax.ShapeDtypeStruct((16, 48, 128), BF16),
        compiler_params=pltpu.CompilerParams(vmem_limit_bytes=8 << 20),
        cost_estimate=pl.CostEstimate(
            flops=1_000_000, bytes_accessed=500_000, transcendentals=0
        ),
        name="split",
    )(own0, own1, far, block)


def phase_cosine(phase):
    turns = jnp.floor((phase + 0.5) * (1.0 / N))
    rest = phase - N * turns
    angle = (N // 4 - jnp.minimum(rest, N - rest)) * (2.0 * math.pi / N)
    square = angle * angle
    series = -1.0 / 39916800.0
    for factor in (1.0 / 362880.0, -1.0 / 5040.0, 1.0 / 120.0, -1.0 / 6.0, 1.0):
        series = series * square + factor
    return angle * series


def block_kernel(*refs):
    waves_hbm, refs = refs[: 2 + len(SLOTS)], refs[2 + len(SLOTS) :]
    info_ref, marks_hbm, _, out_hbm, *refs = refs
    waves_ref, product_ref, marks_ref, tail_ref, sums_ref, wave_sems, sems = refs
    waves_in = [
        pltpu.make_async_copy(wave, waves_ref.at[i], wave_sems.at[i])
        for i, wave in enumerate(waves_hbm)
    ]
    place = marks_hbm.at[:, pl.ds(0, 8), pl.ds(SPARE, 128)]
    marks_in = pltpu.make_async_copy(place, marks_ref, sems.at[1])
    marks_in.start()
    for move in waves_in:
        move.start()
    tail = (slice(None), pl.ds(0, 16), pl.ds(SPARE, 128))
    fetch = pltpu.make_async_copy(out_hbm.at[tail], tail_ref, sems.at[0])
    fetch.start()
    info = info_ref[...]
    marks_in.wait()
    marks = marks_ref[...].astype(F32).sum(axis=0)
    used = info[3:4] != 0.0
    cell = jnp.where(used, 256.0 * marks[0:1] + marks[1:2], 0.0)
    block_x = jnp.floor((cell + 0.5) * (1.0 / 576.0))
    cell = cell - 576.0 * block_x
    block_y = jnp.floor((cell + 0.5) * (1.0 / N))
    block_z = cell - N * block_y
    block_y = block_y + info[0:1]
    lane = lax.broadcasted_iota(jnp.int32, (Y6 * N, 128), 0).astype(F32)
    y6 = jnp.floor((lane + 0.5) * (1.0 / N))
    lanes = phase_cosine(16.0 * y6 * block_y + (lane - N * y6) * block_z + info[1:2]).astype(BF16)
    rows = X6 * Y16
    row = lax.broadcasted_iota(jnp.int32, (rows, 128), 0).astype(F32)
    x = jnp.floor((row + 0.5) * (1.0 / Y16))
    turned = phase_cosine((x + info[4:5]) * block_x + (row - Y16 * x) * block_y + info[2:3])
    turned = turned * info[3:4]
    for move in waves_in:
        move.wait()
    for half in range(2):
        for item, slot in enumerate(SLOTS):
            index = half * len(SLOTS) + item
            product_ref[index * rows : (index + 1) * rows, :] = (
                waves_ref[half] * waves_ref[2 + slot]
            )
    sums = jnp.dot(product_ref[...], lanes, preferred_element_type=F32)
    sums_ref[...] = (sums.reshape(2 * ITEMS, rows, 128) * turned[None]).sum(axis=1)
    sums = sums_ref[...]
    sums = sums + pltpu.roll(sums, 128 - NBLOCK, 1)
    high = sums.astype(BF16).astype(F32)
    rest = pltpu.roll(sums - high, NBLOCK, 1)
    spot = lax.broadcasted_iota(jnp.int32, sums.shape, 1)
    sums = jnp.where(spot // NBLOCK % 2 == 0, high, rest)
    fetch.wait()
    tails = tail_ref[...].astype(F32)
    tail_ref[...] = jnp.where((spot >= 32) & (spot < 96), sums, tails).astype(BF16)
    store = pltpu.make_async_copy(tail_ref, out_hbm.at[tail], sems.at[2])
    store.start()
    store.wait()


def with_block_sums(v, c, info, arrived, planes):
    waves = [in_hbm(wave) for wave in (*v, *c)]
    inputs = (*waves, info, arrived, planes)
    return pl.pallas_call(
        block_kernel,
        out_shape=pltpu.HBM(planes.shape, planes.dtype),
        in_specs=[HBM] * len(waves) + [VMEM, ANY, HBM],
        out_specs=HBM,
        input_output_aliases={len(inputs) - 1: 0},
        scratch_shapes=[
            pltpu.VMEM((len(waves), X6 * Y16, Y6 * N), BF16),
            pltpu.VMEM((2 * ITEMS * X6 * Y16, Y6 * N), BF16),
            pltpu.VMEM((SLABS, 8, 128), BF16),
            pltpu.VMEM((SLABS, 16, 128), BF16),
            pltpu.VMEM((2 * ITEMS, 128), F32),
            pltpu.SemaphoreType.DMA((len(waves),)),
            pltpu.SemaphoreType.DMA((3,)),
        ],
        compiler_params=pltpu.CompilerParams(vmem_limit_bytes=10 << 20),
        cost_estimate=pl.CostEstimate(
            flops=10_000_000, bytes_accessed=100_000, transcendentals=0
        ),
        name="block",
    )(*inputs)


def sum_kernel(pairs_ref, weight_ref, column_ref, out_ref):
    pairs = 16 * 16
    block = pairs_ref[:, 32:, :].reshape(pairs, 128)
    total = None
    for part in range(2):
        left = pairs_ref[:, 16 * part : 16 * (part + 1), :].reshape(pairs, 128)
        columns = jnp.dot(block, column_ref[part], preferred_element_type=F32)
        right = (columns * weight_ref[...]).astype(BF16)
        term = lax.dot_general(
            left, right, (((0,), (0,)), ((), ())), preferred_element_type=F32
        )
        total = term if total is None else total + term
    out_ref[...] = total


def wave_rows(wave):
    return wave.reshape(X6, Y6, Y16, N).transpose(0, 2, 1, 3).reshape(X6 * Y16, Y6 * N)


def per_device(
    valence_wave,
    conduction_wave,
    valence_index,
    occupied_energy,
    conduction_energy,
    frequency,
    gvec_cell,
    block_cell,
):
    col = lax.axis_index(COL)
    wave_v = wave_rows(valence_wave)
    wave_c = wave_rows(conduction_wave)
    ahead = [(i, (i + 1) % 8) for i in range(8)]
    behind = [(i, (i + 7) % 8) for i in range(8)]
    v = [wave_v, lax.ppermute(wave_v, "yl", [(0, 1), (1, 0)])]
    c = [wave_c] + [None] * 7
    for slot in (1, 2, 3, 4):
        c[slot] = lax.ppermute(c[slot - 1], "z", ahead)
        if slot < 4:
            c[8 - slot] = lax.ppermute(c[(9 - slot) % 8], "z", behind)

    mirror_of = [(k, SLABS - 1 - k) for k in range(SLABS)]
    far_cell = lax.ppermute(gvec_cell, COL, mirror_of).reshape(16, 128)
    spots = jnp.arange(128, dtype=jnp.int32)
    cell = jnp.where((spots % NBLOCK == col) & (spots >= 32), block_cell[0], 0)
    marks = jnp.concatenate([jnp.stack([cell // 256, cell % 256]), jnp.zeros((6, 128), jnp.int32)])
    (planes0,) = planes_of(0, v, c, marks=(marks.astype(F32),))
    planes0, far_cell = planes_of(1, v, c, through=(far_cell,), buffer=(planes0,))
    sent0 = lax.all_to_all(planes0, COL, 0, 0, tiled=True)
    (planes1,) = planes_of(2, v, c)
    (planes1,) = planes_of(3, v, c, buffer=(planes1,))

    group = np.arange(128) // NBLOCK - 2
    used = (group >= 0) & (group < 4)
    info = np.zeros((8, 128), np.float32)
    info[0] = np.arange(128) % NBLOCK * 6
    info[1] = np.where(group % 2 == 1, N // 4, 0)
    info[2] = np.where(group == 1, 3 * N // 4, np.where(group == 2, N // 4, 0))
    info[3] = np.where(used, 1.0 / (N * math.sqrt(N)), 0.0)
    info = info + jnp.where(np.arange(8)[:, None] == 4, (X6 * col).astype(F32), 0.0)
    planes1 = with_block_sums(v, c, info, sent0, planes1)
    sent1 = lax.all_to_all(planes1, COL, 0, 0, tiled=True)

    far_cell = far_cell.reshape(G_DEV)
    far_x, far_y, far_z = far_cell // 576, far_cell // N % 6, far_cell % N
    own = ((gvec_cell % 576)[None], (gvec_cell // 576)[None])
    far = (((6 - far_y) * N + (N - far_z) % N)[None], ((N - far_x) % N)[None])

    pair_v, pair_c = pair_table()
    occupied = jnp.arange(occupied_energy.shape[0], dtype=jnp.int32)
    valence_energy = jnp.sum(
        jnp.where(valence_index[:, None] == occupied[None, :], occupied_energy[None, :], 0.0),
        axis=1,
    )
    count_v, count_c = valence_index.shape[0], conduction_energy.shape[0]
    energy_v = jnp.sum(
        jnp.where(pair_v[:, None] == np.arange(count_v)[None], valence_energy[None], 0.0), axis=1
    )
    energy_c = jnp.sum(
        jnp.where(pair_c[:, None] == np.arange(count_c)[None], conduction_energy[None], 0.0),
        axis=1,
    )
    gap = (energy_c - energy_v)[:, None]
    omega = jnp.repeat(frequency, 2 * NBLOCK)[None]
    weight = -4.0 * gap / (gap * gap + omega * omega) * (1.0 / math.sqrt(count_v * count_c))

    own0, far0 = first_points(sent0, own, far)
    mirrored, low, columns = second_far_points(sent1, far, far0)
    mirrored = lax.ppermute(mirrored, COL, mirror_of)
    own1 = second_own_points(low, own)
    pairs = split_pairs(own0, own1, mirrored, columns)
    pairs = lax.all_to_all(pairs, BAND, 0, 0, tiled=True)
    return pl.pallas_call(
        sum_kernel,
        out_shape=jax.ShapeDtypeStruct((128, 128), F32),
        compiler_params=pltpu.CompilerParams(vmem_limit_bytes=4 << 20),
        name="pair_sum",
    )(pairs, weight, column_tables())


def solution(mesh):
    fine = Mesh(
        mesh.devices.reshape(8, 2, 4, 2, 2), ("z", "yl", "x", "yh", "co")
    )
    return jax.shard_map(
        per_device,
        mesh=fine,
        in_specs=(
            P(BAND, COL, None),
            P(BAND, COL, None),
            P(),
            P(),
            P(),
            P(),
            P(COL),
            P(COL),
        ),
        out_specs=P(COL + BAND, None),
        check_vma=False,
    )
```

```python
import functools
import math

import jax
import jax.numpy as jnp
import ml_dtypes
import numpy as np
from jax import lax
from jax.experimental import pallas as pl
from jax.experimental.pallas import tpu as pltpu
from jax.sharding import Mesh
from jax.sharding import PartitionSpec as P

BF16 = jnp.bfloat16
F32 = jnp.float32

N = 96
SLABS = 16
X6 = 6
Y6 = 6
Y16 = 16
K7 = 7
FLAT = K7 * N
WIDE = 768
GROUPS = ((0, 1), (7, 2), (6, 3), (5, 4))
SLOTS = [slot for group in GROUPS for slot in group]
ITEMS = len(SLOTS)
SPARE = 640
G_DEV = 2048
NBLOCK = 16
TILE = 512
ROWS = 48
X_GROUPS = ((2, 2), (2, 2))

BAND = ("z", "yl")
COL = ("x", "yh", "co")


def unit(phase, period):
    angle = 2.0 * np.pi * (np.asarray(phase) % period) / period
    return np.cos(angle), -np.sin(angle)


def bf16(table):
    return np.asarray(table, np.float32).astype(ml_dtypes.bfloat16)


@functools.cache
def lane_table():
    y6, z = np.divmod(np.arange(Y6 * N), N)
    k7, kz = np.divmod(np.arange(FLAT), N)
    phase = 16 * y6[:, None] * k7[None, :] + z[:, None] * kz[None, :]
    cosine, sine = unit(phase, N)
    table = np.zeros((Y6 * N, 2 * WIDE))
    table[:, :FLAT] = cosine
    table[:, WIDE : WIDE + FLAT] = sine
    return bf16(table)


@functools.cache
def twiddle_table():
    k7 = np.arange(FLAT) // N
    cosine, sine = unit(np.arange(Y16)[:, None] * k7[None, :], N)
    table = np.zeros((2, Y16, WIDE), np.float32)
    table[0, :, :FLAT] = cosine / N
    table[1, :, :FLAT] = sine / N
    return table


@functools.cache
def row_table(items):
    table = np.zeros((SLABS, items, 2, X6, 2, items, X6, Y16))
    cosine, sine = unit(np.arange(SLABS)[:, None] * np.arange(Y16)[None, :], SLABS)
    for item in range(items):
        for x in range(X6):
            table[:, item, 0, x, 0, item, x] = cosine
            table[:, item, 0, x, 1, item, x] = -sine
            table[:, item, 1, x, 0, item, x] = sine
            table[:, item, 1, x, 1, item, x] = cosine
    return bf16(table.reshape(SLABS * items * 2 * X6, 2 * items * X6 * Y16))


@functools.cache
def x_table(items):
    table = np.zeros((2, items, N, SLABS, items, 2, X6))
    cosine, sine = unit(np.arange(N)[:, None] * np.arange(N)[None, :], N)
    cosine = (cosine * 0.5 / math.sqrt(N)).reshape(N, SLABS, X6)
    sine = (sine * 0.5 / math.sqrt(N)).reshape(N, SLABS, X6)
    for item in range(items):
        table[0, item, :, :, item, 0] = cosine
        table[0, item, :, :, item, 1] = -sine
        table[1, item, :, :, item, 0] = sine
        table[1, item, :, :, item, 1] = cosine
    return bf16(table.reshape(2 * items * N, SLABS * items * 2 * X6))


@functools.cache
def pair_table():
    valence, conduction = [], []
    for band in range(16):
        z, yl = divmod(band, 2)
        for half in range(2):
            for slot in SLOTS:
                valence.append(z * 2 + (yl ^ half))
                conduction.append((z - slot) % 8 * 2 + yl)
    return np.array(valence), np.array(conduction)


@functools.cache
def column_tables():
    tables = np.zeros((2, 128, 4, 2, NBLOCK))
    m = np.arange(NBLOCK)
    tables[0, 32 + m, :, 0, m] = 1.0
    tables[0, 64 + m, :, 1, m] = -1.0
    tables[1, 64 + m, :, 0, m] = 1.0
    tables[1, 32 + m, :, 1, m] = 1.0
    return bf16(tables.reshape(2, 128, 128))


VMEM = pl.BlockSpec(memory_space=pltpu.VMEM)
HBM = pl.BlockSpec(memory_space=pltpu.HBM)
ANY = pl.BlockSpec(memory_space=pl.ANY)
SLAB_CUTS = 4


def in_hbm(x):
    return pltpu.with_memory_space_constraint(x, pltpu.HBM)


PLANES_FLOPS = (30_000_000, 30_000_000, 30_000_000, 30_000_000)


def plane_kernel(*refs, items, first, through, chained, marked, passing):
    refs = list(refs)
    take = lambda count: [refs.pop(0) for _ in range(count)]
    v0_ref, v1_ref = take(2)
    waves_c = take(items)
    lane_ref, twiddle_ref, row_ref = take(3)
    marks = take(marked)
    kept = waves_c if passing else take(through)
    take(chained)
    (out_ref,) = take(1)
    kept_out = take(len(kept))
    low_ref, slab_ref, slab_sems, keep_sems = refs
    moves = [
        pltpu.make_async_copy(source, target, keep_sems.at[i])
        for i, (source, target) in enumerate(zip(kept, kept_out))
    ]
    for move in moves:
        move.start()
    rows = X6 * Y16
    twiddle_c = twiddle_ref[0][None]
    twiddle_s = twiddle_ref[1][None]
    for index, c_ref in enumerate(waves_c):
        wave_c = c_ref[...]
        pairs = jnp.concatenate([v0_ref[...] * wave_c, v1_ref[...] * wave_c], axis=0)
        moved = jnp.dot(pairs, lane_ref[...], preferred_element_type=F32)
        real = moved[:rows, :WIDE] - moved[rows:, WIDE:]
        imag = moved[:rows, WIDE:] + moved[rows:, :WIDE]
        real = real.reshape(X6, Y16, WIDE)
        imag = imag.reshape(X6, Y16, WIDE)
        turned_r = real * twiddle_c - imag * twiddle_s
        turned_i = real * twiddle_s + imag * twiddle_c
        low_ref[index * rows : (index + 1) * rows, :] = turned_r.reshape(rows, WIDE).astype(BF16)
        index += items
        low_ref[index * rows : (index + 1) * rows, :] = turned_i.reshape(rows, WIDE).astype(BF16)
    count = SLABS // SLAB_CUTS
    size = items * 2 * X6
    for part in range(SLAB_CUTS):
        slabs = slice(part * count, (part + 1) * count)
        planes = jnp.dot(
            row_ref[part * count * size : (part + 1) * count * size, :],
            low_ref[...],
            preferred_element_type=F32,
        ).reshape(count, size, WIDE)
        slab_ref[slabs] = planes.astype(BF16)
        if marks:
            tail = planes[:, :8, SPARE:] + marks[0][...][None]
            slab_ref[slabs, :8, SPARE:] = tail.astype(BF16)
        window = pl.ds(part * count, count)
        moves.append(
            pltpu.make_async_copy(
                slab_ref.at[window],
                out_ref.at[window, pl.ds(first, size)],
                slab_sems.at[part],
            )
        )
        moves[-1].start()
    for move in moves:
        move.wait()


def planes_of(group, v, c, marks=(), through=(), after=(), buffer=(), passing=False):
    slots = GROUPS[group]
    items = len(slots)
    outputs = [c[slot] for slot in slots] if passing else through
    first = group % 2 * items * 2 * X6
    inputs = (
        *v,
        *(c[slot] for slot in slots),
        lane_table(),
        twiddle_table(),
        row_table(items),
        *marks,
        *through,
        *after,
        *buffer,
    )
    outside = len(through) + len(after) + len(buffer)
    return pl.pallas_call(
        functools.partial(
            plane_kernel,
            items=items,
            first=first,
            through=len(through),
            chained=len(after) + len(buffer),
            marked=len(marks),
            passing=passing,
        ),
        out_shape=[
            pltpu.HBM((SLABS, ROWS, WIDE), BF16),
            *(pltpu.HBM(x.shape, x.dtype) for x in outputs),
        ],
        in_specs=[VMEM] * (len(inputs) - outside)
        + [ANY] * (len(through) + len(after))
        + [HBM] * len(buffer),
        out_specs=[HBM] * (1 + len(outputs)),
        input_output_aliases={len(inputs) - 1: 0} if buffer else {},
        scratch_shapes=[
            pltpu.VMEM((2 * items * X6 * Y16, WIDE), BF16),
            pltpu.VMEM((SLABS, items * 2 * X6, WIDE), BF16),
            pltpu.SemaphoreType.DMA((SLAB_CUTS,)),
            pltpu.SemaphoreType.DMA((max(len(outputs), 1),)),
        ],
        compiler_params=pltpu.CompilerParams(vmem_limit_bytes=16 << 20),
        cost_estimate=pl.CostEstimate(
            flops=PLANES_FLOPS[group] * items, bytes_accessed=100_000, transcendentals=0
        ),
        name="planes",
    )(*inputs)


def pick(density_ref, flat_ref, kx_ref, store):
    rows = density_ref.shape[0]

    def body(step, carry):
        lanes = pl.ds(pl.multiple_of(step * TILE, TILE), TILE)
        spot = lax.broadcasted_iota(jnp.int32, (WIDE, TILE), 0)
        chosen = jnp.where(spot == flat_ref[:, lanes], 1.0, 0.0).astype(BF16)
        values = jnp.dot(density_ref[...], chosen, preferred_element_type=F32)
        kx = lax.broadcasted_iota(jnp.int32, (N, TILE), 0) == kx_ref[:, lanes]
        values = jnp.where(kx[None], values.reshape(rows // N, N, TILE), 0.0)
        store(lanes, values.sum(axis=1))
        return carry

    lax.fori_loop(0, G_DEV // TILE, body, 0, unroll=True)


def transform_x(chunk, t_ref, x_refs, low):
    first, place = 0, 0
    for items, x_ref in zip(X_GROUPS[chunk], x_refs):
        size = items * 2 * X6
        planes = t_ref[:, first : first + size, :]
        if size % 16:
            planes = planes.astype(F32)
        planes = planes.reshape(SLABS * size, WIDE).astype(BF16)
        rows = 2 * items * N
        low[place : place + rows, :] = jnp.dot(
            x_ref[...], planes, preferred_element_type=F32
        ).astype(BF16)
        first += size
        place += rows


def first_kernel(
    t_ref, x_ref, own_ref, own_kx_ref, far_ref, far_kx_ref, own_out, far_out, low
):
    transform_x(0, t_ref, (x_ref,) * len(X_GROUPS[0]), low)

    def store_far(lanes, values):
        far_out[:, lanes] = values.astype(BF16)

    def store_own(lanes, values):
        own_out[:, lanes] = values

    pick(low, far_ref, far_kx_ref, store_far)
    pick(low, own_ref, own_kx_ref, store_own)


def second_far_kernel(
    t_ref, x_ref, far_ref, far_kx_ref, first_ref, far_out, low, block_out
):
    transform_x(1, t_ref, (x_ref,) * len(X_GROUPS[1]), low)
    rows = first_ref.shape[0]
    far_out[:rows, :] = first_ref[...]

    def store_far(lanes, values):
        far_out[rows:, lanes] = values.astype(BF16)

    pick(low, far_ref, far_kx_ref, store_far)
    spare = t_ref[:, :16, SPARE:].astype(F32).sum(axis=0)
    spare = spare + pltpu.roll(spare, 128 - NBLOCK, 1)
    block_out[...] = spare


def second_own_kernel(low, own_ref, own_kx_ref, own_out):
    def store_own(lanes, values):
        own_out[:, lanes] = values

    pick(low, own_ref, own_kx_ref, store_own)


FIRST, SECOND = (2 * sum(chunk) for chunk in X_GROUPS)


def first_points(planes, own, far):
    return pl.pallas_call(
        first_kernel,
        out_shape=(
            jax.ShapeDtypeStruct((FIRST, G_DEV), F32),
            jax.ShapeDtypeStruct((FIRST, G_DEV), BF16),
        ),
        scratch_shapes=[pltpu.VMEM((FIRST * N, WIDE), BF16)],
        compiler_params=pltpu.CompilerParams(vmem_limit_bytes=16 << 20),
        cost_estimate=pl.CostEstimate(
            flops=100_000_000, bytes_accessed=100_000, transcendentals=0
        ),
        name="first_points",
    )(planes, x_table(X_GROUPS[0][0]), *own, *far)


def second_far_points(planes, far, first):
    return pl.pallas_call(
        second_far_kernel,
        out_shape=(
            jax.ShapeDtypeStruct((FIRST + SECOND, G_DEV), BF16),
            jax.ShapeDtypeStruct((SECOND * N, WIDE), BF16),
            jax.ShapeDtypeStruct((16, 128), F32),
        ),
        compiler_params=pltpu.CompilerParams(vmem_limit_bytes=16 << 20),
        cost_estimate=pl.CostEstimate(
            flops=100_000_000, bytes_accessed=100_000, transcendentals=0
        ),
        name="second_far_points",
    )(planes, x_table(X_GROUPS[1][0]), *far, first)


def second_own_points(low, own):
    return pl.pallas_call(
        second_own_kernel,
        out_shape=jax.ShapeDtypeStruct((SECOND, G_DEV), F32),
        compiler_params=pltpu.CompilerParams(vmem_limit_bytes=16 << 20),
        cost_estimate=pl.CostEstimate(
            flops=2_400_000_000, bytes_accessed=1_300_000, transcendentals=0
        ),
        name="second_own_points",
    )(low, *own)


def split_kernel(own0_ref, own1_ref, far_ref, block_ref, out_ref):
    parts = [[], [], [], []]
    first, place = 0, 0
    for own_ref, chunk in zip((own0_ref, own1_ref), X_GROUPS):
        first = 0
        for size in chunk:
            own_r = own_ref[first : first + size, :]
            own_i = own_ref[first + size : first + 2 * size, :]
            far_r = far_ref[place : place + size, :].astype(F32)
            far_i = far_ref[place + size : place + 2 * size, :].astype(F32)
            parts[0].append(own_r + far_r)
            parts[1].append(own_i + far_i)
            parts[2].append(own_i - far_i)
            parts[3].append(far_r - own_r)
            first += 2 * size
            place += 2 * size
    pairs = jnp.concatenate(sum(parts, []), axis=0).astype(BF16)
    block = block_ref[...].astype(BF16)
    for band in range(16):
        out_ref[band, :32, :] = pairs[:, band * 128 : (band + 1) * 128]
        out_ref[band, 32:, :] = block


def split_pairs(own0, own1, far, block):
    return pl.pallas_call(
        split_kernel,
        out_shape=jax.ShapeDtypeStruct((16, 48, 128), BF16),
        compiler_params=pltpu.CompilerParams(vmem_limit_bytes=8 << 20),
        cost_estimate=pl.CostEstimate(
            flops=1_000_000, bytes_accessed=500_000, transcendentals=0
        ),
        name="split",
    )(own0, own1, far, block)


def phase_cosine(phase):
    turns = jnp.floor((phase + 0.5) * (1.0 / N))
    rest = phase - N * turns
    angle = (N // 4 - jnp.minimum(rest, N - rest)) * (2.0 * math.pi / N)
    square = angle * angle
    series = -1.0 / 39916800.0
    for factor in (1.0 / 362880.0, -1.0 / 5040.0, 1.0 / 120.0, -1.0 / 6.0, 1.0):
        series = series * square + factor
    return angle * series


def block_kernel(*refs):
    waves_hbm, refs = refs[: 2 + len(SLOTS)], refs[2 + len(SLOTS) :]
    info_ref, marks_hbm, _, out_hbm, *refs = refs
    waves_ref, product_ref, marks_ref, tail_ref, sums_ref, wave_sems, sems = refs
    waves_in = [
        pltpu.make_async_copy(wave, waves_ref.at[i], wave_sems.at[i])
        for i, wave in enumerate(waves_hbm)
    ]
    place = marks_hbm.at[:, pl.ds(0, 8), pl.ds(SPARE, 128)]
    marks_in = pltpu.make_async_copy(place, marks_ref, sems.at[1])
    marks_in.start()
    for move in waves_in:
        move.start()
    tail = (slice(None), pl.ds(0, 16), pl.ds(SPARE, 128))
    fetch = pltpu.make_async_copy(out_hbm.at[tail], tail_ref, sems.at[0])
    fetch.start()
    info = info_ref[...]
    marks_in.wait()
    marks = marks_ref[...].astype(F32).sum(axis=0)
    used = info[3:4] != 0.0
    cell = jnp.where(used, 256.0 * marks[0:1] + marks[1:2], 0.0)
    block_x = jnp.floor((cell + 0.5) * (1.0 / 576.0))
    cell = cell - 576.0 * block_x
    block_y = jnp.floor((cell + 0.5) * (1.0 / N))
    block_z = cell - N * block_y
    block_y = block_y + info[0:1]
    lane = lax.broadcasted_iota(jnp.int32, (Y6 * N, 128), 0).astype(F32)
    y6 = jnp.floor((lane + 0.5) * (1.0 / N))
    lanes = phase_cosine(16.0 * y6 * block_y + (lane - N * y6) * block_z + info[1:2]).astype(BF16)
    rows = X6 * Y16
    row = lax.broadcasted_iota(jnp.int32, (rows, 128), 0).astype(F32)
    x = jnp.floor((row + 0.5) * (1.0 / Y16))
    turned = phase_cosine((x + info[4:5]) * block_x + (row - Y16 * x) * block_y + info[2:3])
    turned = turned * info[3:4]
    for move in waves_in:
        move.wait()
    for half in range(2):
        for item, slot in enumerate(SLOTS):
            index = half * len(SLOTS) + item
            product_ref[index * rows : (index + 1) * rows, :] = (
                waves_ref[half] * waves_ref[2 + slot]
            )
    sums = jnp.dot(product_ref[...], lanes, preferred_element_type=F32)
    sums_ref[...] = (sums.reshape(2 * ITEMS, rows, 128) * turned[None]).sum(axis=1)
    sums = sums_ref[...]
    sums = sums + pltpu.roll(sums, 128 - NBLOCK, 1)
    high = sums.astype(BF16).astype(F32)
    rest = pltpu.roll(sums - high, NBLOCK, 1)
    spot = lax.broadcasted_iota(jnp.int32, sums.shape, 1)
    sums = jnp.where(spot // NBLOCK % 2 == 0, high, rest)
    fetch.wait()
    tails = tail_ref[...].astype(F32)
    tail_ref[...] = jnp.where((spot >= 32) & (spot < 96), sums, tails).astype(BF16)
    store = pltpu.make_async_copy(tail_ref, out_hbm.at[tail], sems.at[2])
    store.start()
    store.wait()


def with_block_sums(v, c, info, arrived, planes):
    waves = [in_hbm(wave) for wave in (*v, *c)]
    inputs = (*waves, info, arrived, planes)
    return pl.pallas_call(
        block_kernel,
        out_shape=pltpu.HBM(planes.shape, planes.dtype),
        in_specs=[HBM] * len(waves) + [VMEM, ANY, HBM],
        out_specs=HBM,
        input_output_aliases={len(inputs) - 1: 0},
        scratch_shapes=[
            pltpu.VMEM((len(waves), X6 * Y16, Y6 * N), BF16),
            pltpu.VMEM((2 * ITEMS * X6 * Y16, Y6 * N), BF16),
            pltpu.VMEM((SLABS, 8, 128), BF16),
            pltpu.VMEM((SLABS, 16, 128), BF16),
            pltpu.VMEM((2 * ITEMS, 128), F32),
            pltpu.SemaphoreType.DMA((len(waves),)),
            pltpu.SemaphoreType.DMA((3,)),
        ],
        compiler_params=pltpu.CompilerParams(vmem_limit_bytes=10 << 20),
        cost_estimate=pl.CostEstimate(
            flops=10_000_000, bytes_accessed=100_000, transcendentals=0
        ),
        name="block",
    )(*inputs)


def sum_kernel(pairs_ref, weight_ref, column_ref, out_ref):
    pairs = 16 * 16
    block = pairs_ref[:, 32:, :].reshape(pairs, 128)
    total = None
    for part in range(2):
        left = pairs_ref[:, 16 * part : 16 * (part + 1), :].reshape(pairs, 128)
        columns = jnp.dot(block, column_ref[part], preferred_element_type=F32)
        right = (columns * weight_ref[...]).astype(BF16)
        term = lax.dot_general(
            left, right, (((0,), (0,)), ((), ())), preferred_element_type=F32
        )
        total = term if total is None else total + term
    out_ref[...] = total


def wave_rows(wave):
    return wave.reshape(X6, Y6, Y16, N).transpose(0, 2, 1, 3).reshape(X6 * Y16, Y6 * N)


def per_device(
    valence_wave,
    conduction_wave,
    valence_index,
    occupied_energy,
    conduction_energy,
    frequency,
    gvec_cell,
    block_cell,
):
    col = lax.axis_index(COL)
    wave_v = wave_rows(valence_wave)
    wave_c = wave_rows(conduction_wave)
    ahead = [(i, (i + 1) % 8) for i in range(8)]
    behind = [(i, (i + 7) % 8) for i in range(8)]
    v = [wave_v, lax.ppermute(wave_v, "yl", [(0, 1), (1, 0)])]
    c = [wave_c] + [None] * 7
    for slot in (1, 2, 3, 4):
        c[slot] = lax.ppermute(c[slot - 1], "z", ahead)
        if slot < 4:
            c[8 - slot] = lax.ppermute(c[(9 - slot) % 8], "z", behind)

    mirror_of = [(k, SLABS - 1 - k) for k in range(SLABS)]
    far_cell = lax.ppermute(gvec_cell, COL, mirror_of).reshape(16, 128)
    spots = jnp.arange(128, dtype=jnp.int32)
    cell = jnp.where((spots % NBLOCK == col) & (spots >= 32), block_cell[0], 0)
    marks = jnp.concatenate([jnp.stack([cell // 256, cell % 256]), jnp.zeros((6, 128), jnp.int32)])
    (planes0,) = planes_of(0, v, c, marks=(marks.astype(F32),))
    planes0, far_cell = planes_of(1, v, c, through=(far_cell,), buffer=(planes0,))
    sent0 = lax.all_to_all(planes0, COL, 0, 0, tiled=True)
    (planes1,) = planes_of(2, v, c)
    last = GROUPS[3]
    planes1, *passed = planes_of(3, v, c, buffer=(planes1,), passing=True)
    for slot, wave in zip(last, passed):
        c[slot] = wave

    group = np.arange(128) // NBLOCK - 2
    used = (group >= 0) & (group < 4)
    info = np.zeros((8, 128), np.float32)
    info[0] = np.arange(128) % NBLOCK * 6
    info[1] = np.where(group % 2 == 1, N // 4, 0)
    info[2] = np.where(group == 1, 3 * N // 4, np.where(group == 2, N // 4, 0))
    info[3] = np.where(used, 1.0 / (N * math.sqrt(N)), 0.0)
    info = info + jnp.where(np.arange(8)[:, None] == 4, (X6 * col).astype(F32), 0.0)
    planes1 = with_block_sums(v, c, info, sent0, planes1)
    sent1 = lax.all_to_all(planes1, COL, 0, 0, tiled=True)

    far_cell = far_cell.reshape(G_DEV)
    far_x, far_y, far_z = far_cell // 576, far_cell // N % 6, far_cell % N
    own = ((gvec_cell % 576)[None], (gvec_cell // 576)[None])
    far = (((6 - far_y) * N + (N - far_z) % N)[None], ((N - far_x) % N)[None])

    pair_v, pair_c = pair_table()
    occupied = jnp.arange(occupied_energy.shape[0], dtype=jnp.int32)
    valence_energy = jnp.sum(
        jnp.where(valence_index[:, None] == occupied[None, :], occupied_energy[None, :], 0.0),
        axis=1,
    )
    count_v, count_c = valence_index.shape[0], conduction_energy.shape[0]
    energy_v = jnp.sum(
        jnp.where(pair_v[:, None] == np.arange(count_v)[None], valence_energy[None], 0.0), axis=1
    )
    energy_c = jnp.sum(
        jnp.where(pair_c[:, None] == np.arange(count_c)[None], conduction_energy[None], 0.0),
        axis=1,
    )
    gap = (energy_c - energy_v)[:, None]
    omega = jnp.repeat(frequency, 2 * NBLOCK)[None]
    weight = -4.0 * gap / (gap * gap + omega * omega) * (1.0 / math.sqrt(count_v * count_c))

    own0, far0 = first_points(sent0, own, far)
    mirrored, low, columns = second_far_points(sent1, far, far0)
    mirrored = lax.ppermute(mirrored, COL, mirror_of)
    own1 = second_own_points(low, own)
    pairs = split_pairs(own0, own1, mirrored, columns)
    pairs = lax.all_to_all(pairs, BAND, 0, 0, tiled=True)
    return pl.pallas_call(
        sum_kernel,
        out_shape=jax.ShapeDtypeStruct((128, 128), F32),
        compiler_params=pltpu.CompilerParams(vmem_limit_bytes=4 << 20),
        name="pair_sum",
    )(pairs, weight, column_tables())


def solution(mesh):
    fine = Mesh(
        mesh.devices.reshape(8, 2, 4, 2, 2), ("z", "yl", "x", "yh", "co")
    )
    return jax.shard_map(
        per_device,
        mesh=fine,
        in_specs=(
            P(BAND, COL, None),
            P(BAND, COL, None),
            P(),
            P(),
            P(),
            P(),
            P(COL),
            P(COL),
        ),
        out_specs=P(COL + BAND, None),
        check_vma=False,
    )
```

```python
import functools
import math

import jax
import jax.numpy as jnp
import ml_dtypes
import numpy as np
from jax import lax
from jax.experimental import pallas as pl
from jax.experimental.pallas import tpu as pltpu
from jax.sharding import Mesh
from jax.sharding import PartitionSpec as P

BF16 = jnp.bfloat16
F32 = jnp.float32

N = 96
SLABS = 16
X6 = 6
Y6 = 6
Y16 = 16
K7 = 7
FLAT = K7 * N
WIDE = 768
GROUPS = ((0, 1), (7, 2), (6, 3), (5, 4))
SLOTS = [slot for group in GROUPS for slot in group]
ITEMS = len(SLOTS)
SPARE = 640
G_DEV = 2048
NBLOCK = 16
TILE = 512
ROWS = 48
X_GROUPS = ((2, 2), (2, 2))

BAND = ("z", "yl")
COL = ("x", "yh", "co")


def unit(phase, period):
    angle = 2.0 * np.pi * (np.asarray(phase) % period) / period
    return np.cos(angle), -np.sin(angle)


def bf16(table):
    return np.asarray(table, np.float32).astype(ml_dtypes.bfloat16)


@functools.cache
def lane_table():
    y6, z = np.divmod(np.arange(Y6 * N), N)
    k7, kz = np.divmod(np.arange(FLAT), N)
    phase = 16 * y6[:, None] * k7[None, :] + z[:, None] * kz[None, :]
    cosine, sine = unit(phase, N)
    table = np.zeros((Y6 * N, 2 * WIDE))
    table[:, :FLAT] = cosine
    table[:, WIDE : WIDE + FLAT] = sine
    return bf16(table)


@functools.cache
def twiddle_table():
    k7 = np.arange(FLAT) // N
    cosine, sine = unit(np.arange(Y16)[:, None] * k7[None, :], N)
    table = np.zeros((2, Y16, WIDE), np.float32)
    table[0, :, :FLAT] = cosine / N
    table[1, :, :FLAT] = sine / N
    return table


@functools.cache
def row_table(items):
    table = np.zeros((SLABS, items, 2, X6, 2, items, X6, Y16))
    cosine, sine = unit(np.arange(SLABS)[:, None] * np.arange(Y16)[None, :], SLABS)
    for item in range(items):
        for x in range(X6):
            table[:, item, 0, x, 0, item, x] = cosine
            table[:, item, 0, x, 1, item, x] = -sine
            table[:, item, 1, x, 0, item, x] = sine
            table[:, item, 1, x, 1, item, x] = cosine
    return bf16(table.reshape(SLABS * items * 2 * X6, 2 * items * X6 * Y16))


@functools.cache
def x_table(items):
    table = np.zeros((2, items, N, SLABS, items, 2, X6))
    cosine, sine = unit(np.arange(N)[:, None] * np.arange(N)[None, :], N)
    cosine = (cosine * 0.5 / math.sqrt(N)).reshape(N, SLABS, X6)
    sine = (sine * 0.5 / math.sqrt(N)).reshape(N, SLABS, X6)
    for item in range(items):
        table[0, item, :, :, item, 0] = cosine
        table[0, item, :, :, item, 1] = -sine
        table[1, item, :, :, item, 0] = sine
        table[1, item, :, :, item, 1] = cosine
    return bf16(table.reshape(2 * items * N, SLABS * items * 2 * X6))


@functools.cache
def pair_table():
    valence, conduction = [], []
    for band in range(16):
        z, yl = divmod(band, 2)
        for half in range(2):
            for slot in SLOTS:
                valence.append(z * 2 + (yl ^ half))
                conduction.append((z - slot) % 8 * 2 + yl)
    return np.array(valence), np.array(conduction)


@functools.cache
def column_tables():
    tables = np.zeros((2, 128, 4, 2, NBLOCK))
    m = np.arange(NBLOCK)
    tables[0, 32 + m, :, 0, m] = 1.0
    tables[0, 64 + m, :, 1, m] = -1.0
    tables[1, 64 + m, :, 0, m] = 1.0
    tables[1, 32 + m, :, 1, m] = 1.0
    return bf16(tables.reshape(2, 128, 128))


VMEM = pl.BlockSpec(memory_space=pltpu.VMEM)
HBM = pl.BlockSpec(memory_space=pltpu.HBM)
ANY = pl.BlockSpec(memory_space=pl.ANY)
SLAB_CUTS = 4


def in_hbm(x):
    return pltpu.with_memory_space_constraint(x, pltpu.HBM)


PLANES_FLOPS = (30_000_000, 30_000_000, 30_000_000, 30_000_000)


def plane_kernel(*refs, items, first, through, chained, marked, passing):
    refs = list(refs)
    take = lambda count: [refs.pop(0) for _ in range(count)]
    v0_ref, v1_ref = take(2)
    waves_c = take(items)
    lane_ref, twiddle_ref, row_ref = take(3)
    marks = take(marked)
    kept = waves_c if passing else take(through)
    take(chained)
    (out_ref,) = take(1)
    kept_out = take(len(kept))
    low_ref, slab_ref, slab_sems, keep_sems = refs
    moves = [
        pltpu.make_async_copy(source, target, keep_sems.at[i])
        for i, (source, target) in enumerate(zip(kept, kept_out))
    ]
    for move in moves:
        move.start()
    rows = X6 * Y16
    twiddle_c = twiddle_ref[0][None]
    twiddle_s = twiddle_ref[1][None]
    for index, c_ref in enumerate(waves_c):
        wave_c = c_ref[...]
        pairs = jnp.concatenate([v0_ref[...] * wave_c, v1_ref[...] * wave_c], axis=0)
        moved = jnp.dot(pairs, lane_ref[...], preferred_element_type=F32)
        real = moved[:rows, :WIDE] - moved[rows:, WIDE:]
        imag = moved[:rows, WIDE:] + moved[rows:, :WIDE]
        real = real.reshape(X6, Y16, WIDE)
        imag = imag.reshape(X6, Y16, WIDE)
        turned_r = real * twiddle_c - imag * twiddle_s
        turned_i = real * twiddle_s + imag * twiddle_c
        low_ref[index * rows : (index + 1) * rows, :] = turned_r.reshape(rows, WIDE).astype(BF16)
        index += items
        low_ref[index * rows : (index + 1) * rows, :] = turned_i.reshape(rows, WIDE).astype(BF16)
    count = SLABS // SLAB_CUTS
    size = items * 2 * X6
    for part in range(SLAB_CUTS):
        slabs = slice(part * count, (part + 1) * count)
        planes = jnp.dot(
            row_ref[part * count * size : (part + 1) * count * size, :],
            low_ref[...],
            preferred_element_type=F32,
        ).reshape(count, size, WIDE)
        slab_ref[slabs] = planes.astype(BF16)
        if marks:
            tail = planes[:, :8, SPARE:] + marks[0][...][None]
            slab_ref[slabs, :8, SPARE:] = tail.astype(BF16)
        window = pl.ds(part * count, count)
        moves.append(
            pltpu.make_async_copy(
                slab_ref.at[window],
                out_ref.at[window, pl.ds(first, size)],
                slab_sems.at[part],
            )
        )
        moves[-1].start()
    for move in moves:
        move.wait()


def planes_of(group, v, c, marks=(), through=(), after=(), buffer=(), passing=False):
    slots = GROUPS[group]
    items = len(slots)
    outputs = [c[slot] for slot in slots] if passing else through
    first = group % 2 * items * 2 * X6
    inputs = (
        *v,
        *(c[slot] for slot in slots),
        lane_table(),
        twiddle_table(),
        row_table(items),
        *marks,
        *through,
        *after,
        *buffer,
    )
    outside = len(through) + len(after) + len(buffer)
    return pl.pallas_call(
        functools.partial(
            plane_kernel,
            items=items,
            first=first,
            through=len(through),
            chained=len(after) + len(buffer),
            marked=len(marks),
            passing=passing,
        ),
        out_shape=[
            pltpu.HBM((SLABS, ROWS, WIDE), BF16),
            *(pltpu.HBM(x.shape, x.dtype) for x in outputs),
        ],
        in_specs=[VMEM] * (len(inputs) - outside)
        + [ANY] * (len(through) + len(after))
        + [HBM] * len(buffer),
        out_specs=[HBM] * (1 + len(outputs)),
        input_output_aliases={len(inputs) - 1: 0} if buffer else {},
        scratch_shapes=[
            pltpu.VMEM((2 * items * X6 * Y16, WIDE), BF16),
            pltpu.VMEM((SLABS, items * 2 * X6, WIDE), BF16),
            pltpu.SemaphoreType.DMA((SLAB_CUTS,)),
            pltpu.SemaphoreType.DMA((max(len(outputs), 1),)),
        ],
        compiler_params=pltpu.CompilerParams(vmem_limit_bytes=16 << 20),
        cost_estimate=pl.CostEstimate(
            flops=PLANES_FLOPS[group] * items, bytes_accessed=100_000, transcendentals=0
        ),
        name="planes",
    )(*inputs)


def marks_kernel(cell_ref, out_ref):
    cell = cell_ref[...].astype(F32)
    high = jnp.floor((cell + 0.5) * (1.0 / 256.0))
    row = lax.broadcasted_iota(jnp.int32, (8, 128), 0)
    out_ref[...] = jnp.where(row == 0, high, jnp.where(row == 1, cell - 256.0 * high, 0.0))


def block_marks(cell):
    return pl.pallas_call(
        marks_kernel,
        out_shape=jax.ShapeDtypeStruct((8, 128), F32),
        compiler_params=pltpu.CompilerParams(vmem_limit_bytes=1 << 20),
        cost_estimate=pl.CostEstimate(
            flops=MARKS_FLOPS, bytes_accessed=10_000, transcendentals=0
        ),
        name="marks",
    )(cell[None])


MARKS_FLOPS = 150_000_000


def pick(density_ref, flat_ref, kx_ref, store):
    rows = density_ref.shape[0]

    def body(step, carry):
        lanes = pl.ds(pl.multiple_of(step * TILE, TILE), TILE)
        spot = lax.broadcasted_iota(jnp.int32, (WIDE, TILE), 0)
        chosen = jnp.where(spot == flat_ref[:, lanes], 1.0, 0.0).astype(BF16)
        values = jnp.dot(density_ref[...], chosen, preferred_element_type=F32)
        kx = lax.broadcasted_iota(jnp.int32, (N, TILE), 0) == kx_ref[:, lanes]
        values = jnp.where(kx[None], values.reshape(rows // N, N, TILE), 0.0)
        store(lanes, values.sum(axis=1))
        return carry

    lax.fori_loop(0, G_DEV // TILE, body, 0, unroll=True)


def transform_x(chunk, t_ref, x_refs, low):
    first, place = 0, 0
    for items, x_ref in zip(X_GROUPS[chunk], x_refs):
        size = items * 2 * X6
        planes = t_ref[:, first : first + size, :]
        if size % 16:
            planes = planes.astype(F32)
        planes = planes.reshape(SLABS * size, WIDE).astype(BF16)
        rows = 2 * items * N
        low[place : place + rows, :] = jnp.dot(
            x_ref[...], planes, preferred_element_type=F32
        ).astype(BF16)
        first += size
        place += rows


def first_kernel(
    t_ref, x_ref, own_ref, own_kx_ref, far_ref, far_kx_ref, own_out, far_out, low
):
    transform_x(0, t_ref, (x_ref,) * len(X_GROUPS[0]), low)

    def store_far(lanes, values):
        far_out[:, lanes] = values.astype(BF16)

    def store_own(lanes, values):
        own_out[:, lanes] = values

    pick(low, far_ref, far_kx_ref, store_far)
    pick(low, own_ref, own_kx_ref, store_own)


def second_far_kernel(
    t_ref, x_ref, far_ref, far_kx_ref, first_ref, far_out, low, block_out
):
    transform_x(1, t_ref, (x_ref,) * len(X_GROUPS[1]), low)
    rows = first_ref.shape[0]
    far_out[:rows, :] = first_ref[...]

    def store_far(lanes, values):
        far_out[rows:, lanes] = values.astype(BF16)

    pick(low, far_ref, far_kx_ref, store_far)
    spare = t_ref[:, :16, SPARE:].astype(F32).sum(axis=0)
    spare = spare + pltpu.roll(spare, 128 - NBLOCK, 1)
    block_out[...] = spare


def second_own_kernel(low, own_ref, own_kx_ref, own_out):
    def store_own(lanes, values):
        own_out[:, lanes] = values

    pick(low, own_ref, own_kx_ref, store_own)


FIRST, SECOND = (2 * sum(chunk) for chunk in X_GROUPS)


def first_points(planes, own, far):
    return pl.pallas_call(
        first_kernel,
        out_shape=(
            jax.ShapeDtypeStruct((FIRST, G_DEV), F32),
            jax.ShapeDtypeStruct((FIRST, G_DEV), BF16),
        ),
        scratch_shapes=[pltpu.VMEM((FIRST * N, WIDE), BF16)],
        compiler_params=pltpu.CompilerParams(vmem_limit_bytes=16 << 20),
        cost_estimate=pl.CostEstimate(
            flops=100_000_000, bytes_accessed=100_000, transcendentals=0
        ),
        name="first_points",
    )(planes, x_table(X_GROUPS[0][0]), *own, *far)


def second_far_points(planes, far, first):
    return pl.pallas_call(
        second_far_kernel,
        out_shape=(
            jax.ShapeDtypeStruct((FIRST + SECOND, G_DEV), BF16),
            jax.ShapeDtypeStruct((SECOND * N, WIDE), BF16),
            jax.ShapeDtypeStruct((16, 128), F32),
        ),
        compiler_params=pltpu.CompilerParams(vmem_limit_bytes=16 << 20),
        cost_estimate=pl.CostEstimate(
            flops=100_000_000, bytes_accessed=100_000, transcendentals=0
        ),
        name="second_far_points",
    )(planes, x_table(X_GROUPS[1][0]), *far, first)


def second_own_points(low, own):
    return pl.pallas_call(
        second_own_kernel,
        out_shape=jax.ShapeDtypeStruct((SECOND, G_DEV), F32),
        compiler_params=pltpu.CompilerParams(vmem_limit_bytes=16 << 20),
        cost_estimate=pl.CostEstimate(
            flops=2_400_000_000, bytes_accessed=1_300_000, transcendentals=0
        ),
        name="second_own_points",
    )(low, *own)


def split_kernel(own0_ref, own1_ref, far_ref, block_ref, out_ref):
    parts = [[], [], [], []]
    first, place = 0, 0
    for own_ref, chunk in zip((own0_ref, own1_ref), X_GROUPS):
        first = 0
        for size in chunk:
            own_r = own_ref[first : first + size, :]
            own_i = own_ref[first + size : first + 2 * size, :]
            far_r = far_ref[place : place + size, :].astype(F32)
            far_i = far_ref[place + size : place + 2 * size, :].astype(F32)
            parts[0].append(own_r + far_r)
            parts[1].append(own_i + far_i)
            parts[2].append(own_i - far_i)
            parts[3].append(far_r - own_r)
            first += 2 * size
            place += 2 * size
    pairs = jnp.concatenate(sum(parts, []), axis=0).astype(BF16)
    block = block_ref[...].astype(BF16)
    for band in range(16):
        out_ref[band, :32, :] = pairs[:, band * 128 : (band + 1) * 128]
        out_ref[band, 32:, :] = block


def split_pairs(own0, own1, far, block):
    return pl.pallas_call(
        split_kernel,
        out_shape=jax.ShapeDtypeStruct((16, 48, 128), BF16),
        compiler_params=pltpu.CompilerParams(vmem_limit_bytes=8 << 20),
        cost_estimate=pl.CostEstimate(
            flops=1_000_000, bytes_accessed=500_000, transcendentals=0
        ),
        name="split",
    )(own0, own1, far, block)


def phase_cosine(phase):
    turns = jnp.floor((phase + 0.5) * (1.0 / N))
    rest = phase - N * turns
    angle = (N // 4 - jnp.minimum(rest, N - rest)) * (2.0 * math.pi / N)
    square = angle * angle
    series = -1.0 / 39916800.0
    for factor in (1.0 / 362880.0, -1.0 / 5040.0, 1.0 / 120.0, -1.0 / 6.0, 1.0):
        series = series * square + factor
    return angle * series


def block_kernel(*refs):
    waves_hbm, refs = refs[: 2 + len(SLOTS)], refs[2 + len(SLOTS) :]
    info_ref, marks_hbm, _, out_hbm, *refs = refs
    waves_ref, product_ref, marks_ref, tail_ref, sums_ref, wave_sems, sems = refs
    waves_in = [
        pltpu.make_async_copy(wave, waves_ref.at[i], wave_sems.at[i])
        for i, wave in enumerate(waves_hbm)
    ]
    place = marks_hbm.at[:, pl.ds(0, 8), pl.ds(SPARE, 128)]
    marks_in = pltpu.make_async_copy(place, marks_ref, sems.at[1])
    marks_in.start()
    for move in waves_in:
        move.start()
    tail = (slice(None), pl.ds(0, 16), pl.ds(SPARE, 128))
    fetch = pltpu.make_async_copy(out_hbm.at[tail], tail_ref, sems.at[0])
    fetch.start()
    info = info_ref[...]
    marks_in.wait()
    marks = marks_ref[...].astype(F32).sum(axis=0)
    used = info[3:4] != 0.0
    cell = jnp.where(used, 256.0 * marks[0:1] + marks[1:2], 0.0)
    block_x = jnp.floor((cell + 0.5) * (1.0 / 576.0))
    cell = cell - 576.0 * block_x
    block_y = jnp.floor((cell + 0.5) * (1.0 / N))
    block_z = cell - N * block_y
    block_y = block_y + info[0:1]
    lane = lax.broadcasted_iota(jnp.int32, (Y6 * N, 128), 0).astype(F32)
    y6 = jnp.floor((lane + 0.5) * (1.0 / N))
    lanes = phase_cosine(16.0 * y6 * block_y + (lane - N * y6) * block_z + info[1:2]).astype(BF16)
    rows = X6 * Y16
    row = lax.broadcasted_iota(jnp.int32, (rows, 128), 0).astype(F32)
    x = jnp.floor((row + 0.5) * (1.0 / Y16))
    turned = phase_cosine((x + info[4:5]) * block_x + (row - Y16 * x) * block_y + info[2:3])
    turned = turned * info[3:4]
    for move in waves_in:
        move.wait()
    for half in range(2):
        for item, slot in enumerate(SLOTS):
            index = half * len(SLOTS) + item
            product_ref[index * rows : (index + 1) * rows, :] = (
                waves_ref[half] * waves_ref[2 + slot]
            )
    sums = jnp.dot(product_ref[...], lanes, preferred_element_type=F32)
    sums_ref[...] = (sums.reshape(2 * ITEMS, rows, 128) * turned[None]).sum(axis=1)
    sums = sums_ref[...]
    sums = sums + pltpu.roll(sums, 128 - NBLOCK, 1)
    high = sums.astype(BF16).astype(F32)
    rest = pltpu.roll(sums - high, NBLOCK, 1)
    spot = lax.broadcasted_iota(jnp.int32, sums.shape, 1)
    sums = jnp.where(spot // NBLOCK % 2 == 0, high, rest)
    fetch.wait()
    tails = tail_ref[...].astype(F32)
    tail_ref[...] = jnp.where((spot >= 32) & (spot < 96), sums, tails).astype(BF16)
    store = pltpu.make_async_copy(tail_ref, out_hbm.at[tail], sems.at[2])
    store.start()
    store.wait()


def with_block_sums(v, c, info, arrived, planes):
    waves = [in_hbm(wave) for wave in (*v, *c)]
    inputs = (*waves, info, arrived, planes)
    return pl.pallas_call(
        block_kernel,
        out_shape=pltpu.HBM(planes.shape, planes.dtype),
        in_specs=[HBM] * len(waves) + [VMEM, ANY, HBM],
        out_specs=HBM,
        input_output_aliases={len(inputs) - 1: 0},
        scratch_shapes=[
            pltpu.VMEM((len(waves), X6 * Y16, Y6 * N), BF16),
            pltpu.VMEM((2 * ITEMS * X6 * Y16, Y6 * N), BF16),
            pltpu.VMEM((SLABS, 8, 128), BF16),
            pltpu.VMEM((SLABS, 16, 128), BF16),
            pltpu.VMEM((2 * ITEMS, 128), F32),
            pltpu.SemaphoreType.DMA((len(waves),)),
            pltpu.SemaphoreType.DMA((3,)),
        ],
        compiler_params=pltpu.CompilerParams(vmem_limit_bytes=10 << 20),
        cost_estimate=pl.CostEstimate(
            flops=10_000_000, bytes_accessed=100_000, transcendentals=0
        ),
        name="block",
    )(*inputs)


def sum_kernel(pairs_ref, weight_ref, column_ref, out_ref):
    pairs = 16 * 16
    block = pairs_ref[:, 32:, :].reshape(pairs, 128)
    total = None
    for part in range(2):
        left = pairs_ref[:, 16 * part : 16 * (part + 1), :].reshape(pairs, 128)
        columns = jnp.dot(block, column_ref[part], preferred_element_type=F32)
        right = (columns * weight_ref[...]).astype(BF16)
        term = lax.dot_general(
            left, right, (((0,), (0,)), ((), ())), preferred_element_type=F32
        )
        total = term if total is None else total + term
    out_ref[...] = total


def wave_rows(wave):
    return wave.reshape(X6, Y6, Y16, N).transpose(0, 2, 1, 3).reshape(X6 * Y16, Y6 * N)


def per_device(
    valence_wave,
    conduction_wave,
    valence_index,
    occupied_energy,
    conduction_energy,
    frequency,
    gvec_cell,
    block_cell,
):
    col = lax.axis_index(COL)
    wave_v = wave_rows(valence_wave)
    wave_c = wave_rows(conduction_wave)
    ahead = [(i, (i + 1) % 8) for i in range(8)]
    behind = [(i, (i + 7) % 8) for i in range(8)]
    v = [wave_v, lax.ppermute(wave_v, "yl", [(0, 1), (1, 0)])]
    c = [wave_c] + [None] * 7
    for slot in (1, 2, 3, 4):
        c[slot] = lax.ppermute(c[slot - 1], "z", ahead)
        if slot < 4:
            c[8 - slot] = lax.ppermute(c[(9 - slot) % 8], "z", behind)

    mirror_of = [(k, SLABS - 1 - k) for k in range(SLABS)]
    far_cell = lax.ppermute(gvec_cell, COL, mirror_of).reshape(16, 128)
    spots = jnp.arange(128, dtype=jnp.int32)
    marks = block_marks(jnp.where((spots % NBLOCK == col) & (spots >= 32), block_cell[0], 0))
    (planes0,) = planes_of(0, v, c, marks=(marks,))
    planes0, far_cell = planes_of(1, v, c, through=(far_cell,), buffer=(planes0,))
    sent0 = lax.all_to_all(planes0, COL, 0, 0, tiled=True)
    (planes1,) = planes_of(2, v, c)
    last = GROUPS[3]
    planes1, *passed = planes_of(3, v, c, buffer=(planes1,), passing=True)
    for slot, wave in zip(last, passed):
        c[slot] = wave

    group = np.arange(128) // NBLOCK - 2
    used = (group >= 0) & (group < 4)
    info = np.zeros((8, 128), np.float32)
    info[0] = np.arange(128) % NBLOCK * 6
    info[1] = np.where(group % 2 == 1, N // 4, 0)
    info[2] = np.where(group == 1, 3 * N // 4, np.where(group == 2, N // 4, 0))
    info[3] = np.where(used, 1.0 / (N * math.sqrt(N)), 0.0)
    info = info + jnp.where(np.arange(8)[:, None] == 4, (X6 * col).astype(F32), 0.0)
    planes1 = with_block_sums(v, c, info, sent0, planes1)
    sent1 = lax.all_to_all(planes1, COL, 0, 0, tiled=True)

    far_cell = far_cell.reshape(G_DEV)
    far_x, far_y, far_z = far_cell // 576, far_cell // N % 6, far_cell % N
    own = ((gvec_cell % 576)[None], (gvec_cell // 576)[None])
    far = (((6 - far_y) * N + (N - far_z) % N)[None], ((N - far_x) % N)[None])

    pair_v, pair_c = pair_table()
    occupied = jnp.arange(occupied_energy.shape[0], dtype=jnp.int32)
    valence_energy = jnp.sum(
        jnp.where(valence_index[:, None] == occupied[None, :], occupied_energy[None, :], 0.0),
        axis=1,
    )
    count_v, count_c = valence_index.shape[0], conduction_energy.shape[0]
    energy_v = jnp.sum(
        jnp.where(pair_v[:, None] == np.arange(count_v)[None], valence_energy[None], 0.0), axis=1
    )
    energy_c = jnp.sum(
        jnp.where(pair_c[:, None] == np.arange(count_c)[None], conduction_energy[None], 0.0),
        axis=1,
    )
    gap = (energy_c - energy_v)[:, None]
    omega = jnp.repeat(frequency, 2 * NBLOCK)[None]
    weight = -4.0 * gap / (gap * gap + omega * omega) * (1.0 / math.sqrt(count_v * count_c))

    own0, far0 = first_points(sent0, own, far)
    mirrored, low, columns = second_far_points(sent1, far, far0)
    mirrored = lax.ppermute(mirrored, COL, mirror_of)
    own1 = second_own_points(low, own)
    pairs = split_pairs(own0, own1, mirrored, columns)
    pairs = lax.all_to_all(pairs, BAND, 0, 0, tiled=True)
    return pl.pallas_call(
        sum_kernel,
        out_shape=jax.ShapeDtypeStruct((128, 128), F32),
        compiler_params=pltpu.CompilerParams(vmem_limit_bytes=4 << 20),
        name="pair_sum",
    )(pairs, weight, column_tables())


def solution(mesh):
    fine = Mesh(
        mesh.devices.reshape(8, 2, 4, 2, 2), ("z", "yl", "x", "yh", "co")
    )
    return jax.shard_map(
        per_device,
        mesh=fine,
        in_specs=(
            P(BAND, COL, None),
            P(BAND, COL, None),
            P(),
            P(),
            P(),
            P(),
            P(COL),
            P(COL),
        ),
        out_specs=P(COL + BAND, None),
        check_vma=False,
    )
```

```python
import functools
import math

import jax
import jax.numpy as jnp
import ml_dtypes
import numpy as np
from jax import lax
from jax.experimental import pallas as pl
from jax.experimental.pallas import tpu as pltpu
from jax.sharding import Mesh
from jax.sharding import PartitionSpec as P

BF16 = jnp.bfloat16
F32 = jnp.float32

N = 96
SLABS = 16
X6 = 6
Y6 = 6
Y16 = 16
K7 = 7
FLAT = K7 * N
WIDE = 768
GROUPS = ((0, 1), (7, 2), (6, 3), (5, 4))
SLOTS = [slot for group in GROUPS for slot in group]
ITEMS = len(SLOTS)
SPARE = 640
G_DEV = 2048
NBLOCK = 16
TILE = 1024
ROWS = 48
X_GROUPS = ((2, 2), (2, 2))

BAND = ("z", "yl")
COL = ("x", "yh", "co")


def unit(phase, period):
    angle = 2.0 * np.pi * (np.asarray(phase) % period) / period
    return np.cos(angle), -np.sin(angle)


def bf16(table):
    return np.asarray(table, np.float32).astype(ml_dtypes.bfloat16)


@functools.cache
def lane_table():
    y6, z = np.divmod(np.arange(Y6 * N), N)
    k7, kz = np.divmod(np.arange(FLAT), N)
    phase = 16 * y6[:, None] * k7[None, :] + z[:, None] * kz[None, :]
    cosine, sine = unit(phase, N)
    table = np.zeros((Y6 * N, 2 * WIDE))
    table[:, :FLAT] = cosine
    table[:, WIDE : WIDE + FLAT] = sine
    return bf16(table)


@functools.cache
def twiddle_table():
    k7 = np.arange(FLAT) // N
    cosine, sine = unit(np.arange(Y16)[:, None] * k7[None, :], N)
    table = np.zeros((2, Y16, WIDE), np.float32)
    table[0, :, :FLAT] = cosine / N
    table[1, :, :FLAT] = sine / N
    return table


@functools.cache
def row_table(items):
    table = np.zeros((SLABS, items, 2, X6, 2, items, X6, Y16))
    cosine, sine = unit(np.arange(SLABS)[:, None] * np.arange(Y16)[None, :], SLABS)
    for item in range(items):
        for x in range(X6):
            table[:, item, 0, x, 0, item, x] = cosine
            table[:, item, 0, x, 1, item, x] = -sine
            table[:, item, 1, x, 0, item, x] = sine
            table[:, item, 1, x, 1, item, x] = cosine
    return bf16(table.reshape(SLABS * items * 2 * X6, 2 * items * X6 * Y16))


@functools.cache
def x_table(items):
    table = np.zeros((2, items, N, SLABS, items, 2, X6))
    cosine, sine = unit(np.arange(N)[:, None] * np.arange(N)[None, :], N)
    cosine = (cosine * 0.5 / math.sqrt(N)).reshape(N, SLABS, X6)
    sine = (sine * 0.5 / math.sqrt(N)).reshape(N, SLABS, X6)
    for item in range(items):
        table[0, item, :, :, item, 0] = cosine
        table[0, item, :, :, item, 1] = -sine
        table[1, item, :, :, item, 0] = sine
        table[1, item, :, :, item, 1] = cosine
    return bf16(table.reshape(2 * items * N, SLABS * items * 2 * X6))


@functools.cache
def pair_table():
    valence, conduction = [], []
    for band in range(16):
        z, yl = divmod(band, 2)
        for half in range(2):
            for slot in SLOTS:
                valence.append(z * 2 + (yl ^ half))
                conduction.append((z - slot) % 8 * 2 + yl)
    return np.array(valence), np.array(conduction)


@functools.cache
def column_tables():
    tables = np.zeros((2, 128, 4, 2, NBLOCK))
    m = np.arange(NBLOCK)
    tables[0, 32 + m, :, 0, m] = 1.0
    tables[0, 64 + m, :, 1, m] = -1.0
    tables[1, 64 + m, :, 0, m] = 1.0
    tables[1, 32 + m, :, 1, m] = 1.0
    return bf16(tables.reshape(2, 128, 128))


VMEM = pl.BlockSpec(memory_space=pltpu.VMEM)
HBM = pl.BlockSpec(memory_space=pltpu.HBM)
ANY = pl.BlockSpec(memory_space=pl.ANY)
SLAB_CUTS = 4


def in_hbm(x):
    return pltpu.with_memory_space_constraint(x, pltpu.HBM)


PLANES_FLOPS = (30_000_000, 30_000_000, 30_000_000, 30_000_000)


def plane_kernel(*refs, items, first, through, chained, marked, passing):
    refs = list(refs)
    take = lambda count: [refs.pop(0) for _ in range(count)]
    v0_ref, v1_ref = take(2)
    waves_c = take(items)
    lane_ref, twiddle_ref, row_ref = take(3)
    marks = take(marked)
    kept = waves_c if passing else take(through)
    take(chained)
    (out_ref,) = take(1)
    kept_out = take(len(kept))
    low_ref, slab_ref, slab_sems, keep_sems = refs
    moves = [
        pltpu.make_async_copy(source, target, keep_sems.at[i])
        for i, (source, target) in enumerate(zip(kept, kept_out))
    ]
    for move in moves:
        move.start()
    rows = X6 * Y16
    twiddle_c = twiddle_ref[0][None]
    twiddle_s = twiddle_ref[1][None]
    for index, c_ref in enumerate(waves_c):
        wave_c = c_ref[...]
        pairs = jnp.concatenate([v0_ref[...] * wave_c, v1_ref[...] * wave_c], axis=0)
        moved = jnp.dot(pairs, lane_ref[...], preferred_element_type=F32)
        real = moved[:rows, :WIDE] - moved[rows:, WIDE:]
        imag = moved[:rows, WIDE:] + moved[rows:, :WIDE]
        real = real.reshape(X6, Y16, WIDE)
        imag = imag.reshape(X6, Y16, WIDE)
        turned_r = real * twiddle_c - imag * twiddle_s
        turned_i = real * twiddle_s + imag * twiddle_c
        low_ref[index * rows : (index + 1) * rows, :] = turned_r.reshape(rows, WIDE).astype(BF16)
        index += items
        low_ref[index * rows : (index + 1) * rows, :] = turned_i.reshape(rows, WIDE).astype(BF16)
    count = SLABS // SLAB_CUTS
    size = items * 2 * X6
    for part in range(SLAB_CUTS):
        slabs = slice(part * count, (part + 1) * count)
        planes = jnp.dot(
            row_ref[part * count * size : (part + 1) * count * size, :],
            low_ref[...],
            preferred_element_type=F32,
        ).reshape(count, size, WIDE)
        slab_ref[slabs] = planes.astype(BF16)
        if marks:
            tail = planes[:, :8, SPARE:] + marks[0][...][None]
            slab_ref[slabs, :8, SPARE:] = tail.astype(BF16)
        window = pl.ds(part * count, count)
        moves.append(
            pltpu.make_async_copy(
                slab_ref.at[window],
                out_ref.at[window, pl.ds(first, size)],
                slab_sems.at[part],
            )
        )
        moves[-1].start()
    for move in moves:
        move.wait()


def planes_of(group, v, c, marks=(), through=(), after=(), buffer=(), passing=False):
    slots = GROUPS[group]
    items = len(slots)
    outputs = [c[slot] for slot in slots] if passing else through
    first = group % 2 * items * 2 * X6
    inputs = (
        *v,
        *(c[slot] for slot in slots),
        lane_table(),
        twiddle_table(),
        row_table(items),
        *marks,
        *through,
        *after,
        *buffer,
    )
    outside = len(through) + len(after) + len(buffer)
    return pl.pallas_call(
        functools.partial(
            plane_kernel,
            items=items,
            first=first,
            through=len(through),
            chained=len(after) + len(buffer),
            marked=len(marks),
            passing=passing,
        ),
        out_shape=[
            pltpu.HBM((SLABS, ROWS, WIDE), BF16),
            *(pltpu.HBM(x.shape, x.dtype) for x in outputs),
        ],
        in_specs=[VMEM] * (len(inputs) - outside)
        + [ANY] * (len(through) + len(after))
        + [HBM] * len(buffer),
        out_specs=[HBM] * (1 + len(outputs)),
        input_output_aliases={len(inputs) - 1: 0} if buffer else {},
        scratch_shapes=[
            pltpu.VMEM((2 * items * X6 * Y16, WIDE), BF16),
            pltpu.VMEM((SLABS, items * 2 * X6, WIDE), BF16),
            pltpu.SemaphoreType.DMA((SLAB_CUTS,)),
            pltpu.SemaphoreType.DMA((max(len(outputs), 1),)),
        ],
        compiler_params=pltpu.CompilerParams(vmem_limit_bytes=16 << 20),
        cost_estimate=pl.CostEstimate(
            flops=PLANES_FLOPS[group] * items, bytes_accessed=100_000, transcendentals=0
        ),
        name="planes",
    )(*inputs)


def marks_kernel(cell_ref, out_ref):
    cell = cell_ref[...].astype(F32)
    high = jnp.floor((cell + 0.5) * (1.0 / 256.0))
    row = lax.broadcasted_iota(jnp.int32, (8, 128), 0)
    out_ref[...] = jnp.where(row == 0, high, jnp.where(row == 1, cell - 256.0 * high, 0.0))


def block_marks(cell):
    return pl.pallas_call(
        marks_kernel,
        out_shape=jax.ShapeDtypeStruct((8, 128), F32),
        compiler_params=pltpu.CompilerParams(vmem_limit_bytes=1 << 20),
        cost_estimate=pl.CostEstimate(
            flops=MARKS_FLOPS, bytes_accessed=10_000, transcendentals=0
        ),
        name="marks",
    )(cell[None])


MARKS_FLOPS = 150_000_000


def pick(density_ref, flat_ref, kx_ref, store):
    rows = density_ref.shape[0]

    def body(step, carry):
        lanes = pl.ds(pl.multiple_of(step * TILE, TILE), TILE)
        spot = lax.broadcasted_iota(jnp.int32, (WIDE, TILE), 0)
        chosen = jnp.where(spot == flat_ref[:, lanes], 1.0, 0.0).astype(BF16)
        values = jnp.dot(density_ref[...], chosen, preferred_element_type=F32)
        kx = lax.broadcasted_iota(jnp.int32, (N, TILE), 0) == kx_ref[:, lanes]
        values = jnp.where(kx[None], values.reshape(rows // N, N, TILE), 0.0)
        store(lanes, values.sum(axis=1))
        return carry

    lax.fori_loop(0, G_DEV // TILE, body, 0, unroll=True)


def transform_x(chunk, t_ref, x_refs, low):
    first, place = 0, 0
    for items, x_ref in zip(X_GROUPS[chunk], x_refs):
        size = items * 2 * X6
        planes = t_ref[:, first : first + size, :]
        if size % 16:
            planes = planes.astype(F32)
        planes = planes.reshape(SLABS * size, WIDE).astype(BF16)
        rows = 2 * items * N
        low[place : place + rows, :] = jnp.dot(
            x_ref[...], planes, preferred_element_type=F32
        ).astype(BF16)
        first += size
        place += rows


def first_kernel(
    t_ref, x_ref, own_ref, own_kx_ref, far_ref, far_kx_ref, own_out, far_out, low
):
    transform_x(0, t_ref, (x_ref,) * len(X_GROUPS[0]), low)

    def store_far(lanes, values):
        far_out[:, lanes] = values.astype(BF16)

    def store_own(lanes, values):
        own_out[:, lanes] = values

    pick(low, far_ref, far_kx_ref, store_far)
    pick(low, own_ref, own_kx_ref, store_own)


def second_far_kernel(
    t_ref, x_ref, far_ref, far_kx_ref, first_ref, far_out, low, block_out
):
    transform_x(1, t_ref, (x_ref,) * len(X_GROUPS[1]), low)
    rows = first_ref.shape[0]
    far_out[:rows, :] = first_ref[...]

    def store_far(lanes, values):
        far_out[rows:, lanes] = values.astype(BF16)

    pick(low, far_ref, far_kx_ref, store_far)
    spare = t_ref[:, :16, SPARE:].astype(F32).sum(axis=0)
    spare = spare + pltpu.roll(spare, 128 - NBLOCK, 1)
    block_out[...] = spare


def second_own_kernel(low, own_ref, own_kx_ref, own_out):
    def store_own(lanes, values):
        own_out[:, lanes] = values

    pick(low, own_ref, own_kx_ref, store_own)


FIRST, SECOND = (2 * sum(chunk) for chunk in X_GROUPS)


def first_points(planes, own, far):
    return pl.pallas_call(
        first_kernel,
        out_shape=(
            jax.ShapeDtypeStruct((FIRST, G_DEV), F32),
            jax.ShapeDtypeStruct((FIRST, G_DEV), BF16),
        ),
        scratch_shapes=[pltpu.VMEM((FIRST * N, WIDE), BF16)],
        compiler_params=pltpu.CompilerParams(vmem_limit_bytes=16 << 20),
        cost_estimate=pl.CostEstimate(
            flops=100_000_000, bytes_accessed=100_000, transcendentals=0
        ),
        name="first_points",
    )(planes, x_table(X_GROUPS[0][0]), *own, *far)


def second_far_points(planes, far, first):
    return pl.pallas_call(
        second_far_kernel,
        out_shape=(
            jax.ShapeDtypeStruct((FIRST + SECOND, G_DEV), BF16),
            jax.ShapeDtypeStruct((SECOND * N, WIDE), BF16),
            jax.ShapeDtypeStruct((16, 128), F32),
        ),
        compiler_params=pltpu.CompilerParams(vmem_limit_bytes=16 << 20),
        cost_estimate=pl.CostEstimate(
            flops=100_000_000, bytes_accessed=100_000, transcendentals=0
        ),
        name="second_far_points",
    )(planes, x_table(X_GROUPS[1][0]), *far, first)


def second_own_points(low, own):
    return pl.pallas_call(
        second_own_kernel,
        out_shape=jax.ShapeDtypeStruct((SECOND, G_DEV), F32),
        compiler_params=pltpu.CompilerParams(vmem_limit_bytes=16 << 20),
        cost_estimate=pl.CostEstimate(
            flops=2_400_000_000, bytes_accessed=1_300_000, transcendentals=0
        ),
        name="second_own_points",
    )(low, *own)


def split_kernel(own0_ref, own1_ref, far_ref, block_ref, out_ref):
    parts = [[], [], [], []]
    first, place = 0, 0
    for own_ref, chunk in zip((own0_ref, own1_ref), X_GROUPS):
        first = 0
        for size in chunk:
            own_r = own_ref[first : first + size, :]
            own_i = own_ref[first + size : first + 2 * size, :]
            far_r = far_ref[place : place + size, :].astype(F32)
            far_i = far_ref[place + size : place + 2 * size, :].astype(F32)
            parts[0].append(own_r + far_r)
            parts[1].append(own_i + far_i)
            parts[2].append(own_i - far_i)
            parts[3].append(far_r - own_r)
            first += 2 * size
            place += 2 * size
    pairs = jnp.concatenate(sum(parts, []), axis=0).astype(BF16)
    block = block_ref[...].astype(BF16)
    for band in range(16):
        out_ref[band, :32, :] = pairs[:, band * 128 : (band + 1) * 128]
        out_ref[band, 32:, :] = block


def split_pairs(own0, own1, far, block):
    return pl.pallas_call(
        split_kernel,
        out_shape=jax.ShapeDtypeStruct((16, 48, 128), BF16),
        compiler_params=pltpu.CompilerParams(vmem_limit_bytes=8 << 20),
        cost_estimate=pl.CostEstimate(
            flops=1_000_000, bytes_accessed=500_000, transcendentals=0
        ),
        name="split",
    )(own0, own1, far, block)


def phase_cosine(phase):
    turns = jnp.floor((phase + 0.5) * (1.0 / N))
    rest = phase - N * turns
    angle = (N // 4 - jnp.minimum(rest, N - rest)) * (2.0 * math.pi / N)
    square = angle * angle
    series = -1.0 / 39916800.0
    for factor in (1.0 / 362880.0, -1.0 / 5040.0, 1.0 / 120.0, -1.0 / 6.0, 1.0):
        series = series * square + factor
    return angle * series


def block_kernel(*refs):
    waves_hbm, refs = refs[: 2 + len(SLOTS)], refs[2 + len(SLOTS) :]
    info_ref, marks_hbm, _, out_hbm, *refs = refs
    waves_ref, product_ref, marks_ref, tail_ref, sums_ref, wave_sems, sems = refs
    waves_in = [
        pltpu.make_async_copy(wave, waves_ref.at[i], wave_sems.at[i])
        for i, wave in enumerate(waves_hbm)
    ]
    place = marks_hbm.at[:, pl.ds(0, 8), pl.ds(SPARE, 128)]
    marks_in = pltpu.make_async_copy(place, marks_ref, sems.at[1])
    marks_in.start()
    for move in waves_in:
        move.start()
    tail = (slice(None), pl.ds(0, 16), pl.ds(SPARE, 128))
    fetch = pltpu.make_async_copy(out_hbm.at[tail], tail_ref, sems.at[0])
    fetch.start()
    info = info_ref[...]
    marks_in.wait()
    marks = marks_ref[...].astype(F32).sum(axis=0)
    used = info[3:4] != 0.0
    cell = jnp.where(used, 256.0 * marks[0:1] + marks[1:2], 0.0)
    block_x = jnp.floor((cell + 0.5) * (1.0 / 576.0))
    cell = cell - 576.0 * block_x
    block_y = jnp.floor((cell + 0.5) * (1.0 / N))
    block_z = cell - N * block_y
    block_y = block_y + info[0:1]
    lane = lax.broadcasted_iota(jnp.int32, (Y6 * N, 128), 0).astype(F32)
    y6 = jnp.floor((lane + 0.5) * (1.0 / N))
    lanes = phase_cosine(16.0 * y6 * block_y + (lane - N * y6) * block_z + info[1:2]).astype(BF16)
    rows = X6 * Y16
    row = lax.broadcasted_iota(jnp.int32, (rows, 128), 0).astype(F32)
    x = jnp.floor((row + 0.5) * (1.0 / Y16))
    turned = phase_cosine((x + info[4:5]) * block_x + (row - Y16 * x) * block_y + info[2:3])
    turned = turned * info[3:4]
    for move in waves_in:
        move.wait()
    for half in range(2):
        for item, slot in enumerate(SLOTS):
            index = half * len(SLOTS) + item
            product_ref[index * rows : (index + 1) * rows, :] = (
                waves_ref[half] * waves_ref[2 + slot]
            )
    sums = jnp.dot(product_ref[...], lanes, preferred_element_type=F32)
    sums_ref[...] = (sums.reshape(2 * ITEMS, rows, 128) * turned[None]).sum(axis=1)
    sums = sums_ref[...]
    sums = sums + pltpu.roll(sums, 128 - NBLOCK, 1)
    high = sums.astype(BF16).astype(F32)
    rest = pltpu.roll(sums - high, NBLOCK, 1)
    spot = lax.broadcasted_iota(jnp.int32, sums.shape, 1)
    sums = jnp.where(spot // NBLOCK % 2 == 0, high, rest)
    fetch.wait()
    tails = tail_ref[...].astype(F32)
    tail_ref[...] = jnp.where((spot >= 32) & (spot < 96), sums, tails).astype(BF16)
    store = pltpu.make_async_copy(tail_ref, out_hbm.at[tail], sems.at[2])
    store.start()
    store.wait()


def with_block_sums(v, c, info, arrived, planes):
    waves = [in_hbm(wave) for wave in (*v, *c)]
    inputs = (*waves, info, arrived, planes)
    return pl.pallas_call(
        block_kernel,
        out_shape=pltpu.HBM(planes.shape, planes.dtype),
        in_specs=[HBM] * len(waves) + [VMEM, ANY, HBM],
        out_specs=HBM,
        input_output_aliases={len(inputs) - 1: 0},
        scratch_shapes=[
            pltpu.VMEM((len(waves), X6 * Y16, Y6 * N), BF16),
            pltpu.VMEM((2 * ITEMS * X6 * Y16, Y6 * N), BF16),
            pltpu.VMEM((SLABS, 8, 128), BF16),
            pltpu.VMEM((SLABS, 16, 128), BF16),
            pltpu.VMEM((2 * ITEMS, 128), F32),
            pltpu.SemaphoreType.DMA((len(waves),)),
            pltpu.SemaphoreType.DMA((3,)),
        ],
        compiler_params=pltpu.CompilerParams(vmem_limit_bytes=10 << 20),
        cost_estimate=pl.CostEstimate(
            flops=10_000_000, bytes_accessed=100_000, transcendentals=0
        ),
        name="block",
    )(*inputs)


def sum_kernel(pairs_ref, weight_ref, column_ref, out_ref):
    pairs = 16 * 16
    block = pairs_ref[:, 32:, :].reshape(pairs, 128)
    total = None
    for part in range(2):
        left = pairs_ref[:, 16 * part : 16 * (part + 1), :].reshape(pairs, 128)
        columns = jnp.dot(block, column_ref[part], preferred_element_type=F32)
        right = (columns * weight_ref[...]).astype(BF16)
        term = lax.dot_general(
            left, right, (((0,), (0,)), ((), ())), preferred_element_type=F32
        )
        total = term if total is None else total + term
    out_ref[...] = total


def wave_rows(wave):
    return wave.reshape(X6, Y6, Y16, N).transpose(0, 2, 1, 3).reshape(X6 * Y16, Y6 * N)


def per_device(
    valence_wave,
    conduction_wave,
    valence_index,
    occupied_energy,
    conduction_energy,
    frequency,
    gvec_cell,
    block_cell,
):
    col = lax.axis_index(COL)
    wave_v = wave_rows(valence_wave)
    wave_c = wave_rows(conduction_wave)
    ahead = [(i, (i + 1) % 8) for i in range(8)]
    behind = [(i, (i + 7) % 8) for i in range(8)]
    v = [wave_v, lax.ppermute(wave_v, "yl", [(0, 1), (1, 0)])]
    c = [wave_c] + [None] * 7
    for slot in (1, 2, 3, 4):
        c[slot] = lax.ppermute(c[slot - 1], "z", ahead)
        if slot < 4:
            c[8 - slot] = lax.ppermute(c[(9 - slot) % 8], "z", behind)

    mirror_of = [(k, SLABS - 1 - k) for k in range(SLABS)]
    far_cell = lax.ppermute(gvec_cell, COL, mirror_of).reshape(16, 128)
    spots = jnp.arange(128, dtype=jnp.int32)
    marks = block_marks(jnp.where((spots % NBLOCK == col) & (spots >= 32), block_cell[0], 0))
    (planes0,) = planes_of(0, v, c, marks=(marks,))
    planes0, far_cell = planes_of(1, v, c, through=(far_cell,), buffer=(planes0,))
    sent0 = lax.all_to_all(planes0, COL, 0, 0, tiled=True)
    (planes1,) = planes_of(2, v, c)
    last = GROUPS[3]
    planes1, *passed = planes_of(3, v, c, buffer=(planes1,), passing=True)
    for slot, wave in zip(last, passed):
        c[slot] = wave

    group = np.arange(128) // NBLOCK - 2
    used = (group >= 0) & (group < 4)
    info = np.zeros((8, 128), np.float32)
    info[0] = np.arange(128) % NBLOCK * 6
    info[1] = np.where(group % 2 == 1, N // 4, 0)
    info[2] = np.where(group == 1, 3 * N // 4, np.where(group == 2, N // 4, 0))
    info[3] = np.where(used, 1.0 / (N * math.sqrt(N)), 0.0)
    info = info + jnp.where(np.arange(8)[:, None] == 4, (X6 * col).astype(F32), 0.0)
    planes1 = with_block_sums(v, c, info, sent0, planes1)
    sent1 = lax.all_to_all(planes1, COL, 0, 0, tiled=True)

    far_cell = far_cell.reshape(G_DEV)
    far_x, far_y, far_z = far_cell // 576, far_cell // N % 6, far_cell % N
    own = ((gvec_cell % 576)[None], (gvec_cell // 576)[None])
    far = (((6 - far_y) * N + (N - far_z) % N)[None], ((N - far_x) % N)[None])

    pair_v, pair_c = pair_table()
    occupied = jnp.arange(occupied_energy.shape[0], dtype=jnp.int32)
    valence_energy = jnp.sum(
        jnp.where(valence_index[:, None] == occupied[None, :], occupied_energy[None, :], 0.0),
        axis=1,
    )
    count_v, count_c = valence_index.shape[0], conduction_energy.shape[0]
    energy_v = jnp.sum(
        jnp.where(pair_v[:, None] == np.arange(count_v)[None], valence_energy[None], 0.0), axis=1
    )
    energy_c = jnp.sum(
        jnp.where(pair_c[:, None] == np.arange(count_c)[None], conduction_energy[None], 0.0),
        axis=1,
    )
    gap = (energy_c - energy_v)[:, None]
    omega = jnp.repeat(frequency, 2 * NBLOCK)[None]
    weight = -4.0 * gap / (gap * gap + omega * omega) * (1.0 / math.sqrt(count_v * count_c))

    own0, far0 = first_points(sent0, own, far)
    mirrored, low, columns = second_far_points(sent1, far, far0)
    mirrored = lax.ppermute(mirrored, COL, mirror_of)
    own1 = second_own_points(low, own)
    pairs = split_pairs(own0, own1, mirrored, columns)
    pairs = lax.all_to_all(pairs, BAND, 0, 0, tiled=True)
    return pl.pallas_call(
        sum_kernel,
        out_shape=jax.ShapeDtypeStruct((128, 128), F32),
        compiler_params=pltpu.CompilerParams(vmem_limit_bytes=4 << 20),
        name="pair_sum",
    )(pairs, weight, column_tables())


def solution(mesh):
    fine = Mesh(
        mesh.devices.reshape(8, 2, 4, 2, 2), ("z", "yl", "x", "yh", "co")
    )
    return jax.shard_map(
        per_device,
        mesh=fine,
        in_specs=(
            P(BAND, COL, None),
            P(BAND, COL, None),
            P(),
            P(),
            P(),
            P(),
            P(COL),
            P(COL),
        ),
        out_specs=P(COL + BAND, None),
        check_vma=False,
    )
```

```python
import functools
import math

import jax
import jax.numpy as jnp
import ml_dtypes
import numpy as np
from jax import lax
from jax.experimental import pallas as pl
from jax.experimental.pallas import tpu as pltpu
from jax.sharding import Mesh
from jax.sharding import PartitionSpec as P

BF16 = jnp.bfloat16
F32 = jnp.float32

N = 96
SLABS = 16
X6 = 6
Y6 = 6
Y16 = 16
K7 = 7
FLAT = K7 * N
WIDE = 768
GROUPS = ((0, 1), (7, 2), (6, 3), (5, 4))
SLOTS = [slot for group in GROUPS for slot in group]
ITEMS = len(SLOTS)
SPARE = 640
G_DEV = 2048
NBLOCK = 16
TILE = 512
ROWS = 48
X_GROUPS = ((2, 2), (2, 2))

BAND = ("z", "yl")
COL = ("x", "yh", "co")


def unit(phase, period):
    angle = 2.0 * np.pi * (np.asarray(phase) % period) / period
    return np.cos(angle), -np.sin(angle)


def bf16(table):
    return np.asarray(table, np.float32).astype(ml_dtypes.bfloat16)


@functools.cache
def lane_table():
    y6, z = np.divmod(np.arange(Y6 * N), N)
    k7, kz = np.divmod(np.arange(FLAT), N)
    phase = 16 * y6[:, None] * k7[None, :] + z[:, None] * kz[None, :]
    cosine, sine = unit(phase, N)
    table = np.zeros((Y6 * N, 2 * WIDE))
    table[:, :FLAT] = cosine
    table[:, WIDE : WIDE + FLAT] = sine
    return bf16(table)


@functools.cache
def twiddle_table():
    k7 = np.arange(FLAT) // N
    cosine, sine = unit(np.arange(Y16)[:, None] * k7[None, :], N)
    table = np.zeros((2, Y16, WIDE), np.float32)
    table[0, :, :FLAT] = cosine / N
    table[1, :, :FLAT] = sine / N
    return table


@functools.cache
def row_table(items):
    table = np.zeros((SLABS, items, 2, X6, 2, items, X6, Y16))
    cosine, sine = unit(np.arange(SLABS)[:, None] * np.arange(Y16)[None, :], SLABS)
    for item in range(items):
        for x in range(X6):
            table[:, item, 0, x, 0, item, x] = cosine
            table[:, item, 0, x, 1, item, x] = -sine
            table[:, item, 1, x, 0, item, x] = sine
            table[:, item, 1, x, 1, item, x] = cosine
    return bf16(table.reshape(SLABS * items * 2 * X6, 2 * items * X6 * Y16))


@functools.cache
def x_table(items):
    table = np.zeros((2, items, N, SLABS, items, 2, X6))
    cosine, sine = unit(np.arange(N)[:, None] * np.arange(N)[None, :], N)
    cosine = (cosine * 0.5 / math.sqrt(N)).reshape(N, SLABS, X6)
    sine = (sine * 0.5 / math.sqrt(N)).reshape(N, SLABS, X6)
    for item in range(items):
        table[0, item, :, :, item, 0] = cosine
        table[0, item, :, :, item, 1] = -sine
        table[1, item, :, :, item, 0] = sine
        table[1, item, :, :, item, 1] = cosine
    return bf16(table.reshape(2 * items * N, SLABS * items * 2 * X6))


@functools.cache
def pair_table():
    valence, conduction = [], []
    for band in range(16):
        z, yl = divmod(band, 2)
        for half in range(2):
            for slot in SLOTS:
                valence.append(z * 2 + (yl ^ half))
                conduction.append((z - slot) % 8 * 2 + yl)
    return np.array(valence), np.array(conduction)


@functools.cache
def column_tables():
    tables = np.zeros((2, 128, 4, 2, NBLOCK))
    m = np.arange(NBLOCK)
    tables[0, 32 + m, :, 0, m] = 1.0
    tables[0, 64 + m, :, 1, m] = -1.0
    tables[1, 64 + m, :, 0, m] = 1.0
    tables[1, 32 + m, :, 1, m] = 1.0
    return bf16(tables.reshape(2, 128, 128))


VMEM = pl.BlockSpec(memory_space=pltpu.VMEM)
HBM = pl.BlockSpec(memory_space=pltpu.HBM)
ANY = pl.BlockSpec(memory_space=pl.ANY)
SLAB_CUTS = 2


def in_hbm(x):
    return pltpu.with_memory_space_constraint(x, pltpu.HBM)


PLANES_FLOPS = (30_000_000, 30_000_000, 30_000_000, 30_000_000)


def plane_kernel(*refs, items, first, through, chained, marked, passing):
    refs = list(refs)
    take = lambda count: [refs.pop(0) for _ in range(count)]
    v0_ref, v1_ref = take(2)
    waves_c = take(items)
    lane_ref, twiddle_ref, row_ref = take(3)
    marks = take(marked)
    kept = waves_c if passing else take(through)
    take(chained)
    (out_ref,) = take(1)
    kept_out = take(len(kept))
    low_ref, slab_ref, slab_sems, keep_sems = refs
    moves = [
        pltpu.make_async_copy(source, target, keep_sems.at[i])
        for i, (source, target) in enumerate(zip(kept, kept_out))
    ]
    for move in moves:
        move.start()
    rows = X6 * Y16
    twiddle_c = twiddle_ref[0][None]
    twiddle_s = twiddle_ref[1][None]
    for index, c_ref in enumerate(waves_c):
        wave_c = c_ref[...]
        pairs = jnp.concatenate([v0_ref[...] * wave_c, v1_ref[...] * wave_c], axis=0)
        moved = jnp.dot(pairs, lane_ref[...], preferred_element_type=F32)
        real = moved[:rows, :WIDE] - moved[rows:, WIDE:]
        imag = moved[:rows, WIDE:] + moved[rows:, :WIDE]
        real = real.reshape(X6, Y16, WIDE)
        imag = imag.reshape(X6, Y16, WIDE)
        turned_r = real * twiddle_c - imag * twiddle_s
        turned_i = real * twiddle_s + imag * twiddle_c
        low_ref[index * rows : (index + 1) * rows, :] = turned_r.reshape(rows, WIDE).astype(BF16)
        index += items
        low_ref[index * rows : (index + 1) * rows, :] = turned_i.reshape(rows, WIDE).astype(BF16)
    count = SLABS // SLAB_CUTS
    size = items * 2 * X6
    for part in range(SLAB_CUTS):
        slabs = slice(part * count, (part + 1) * count)
        planes = jnp.dot(
            row_ref[part * count * size : (part + 1) * count * size, :],
            low_ref[...],
            preferred_element_type=F32,
        ).reshape(count, size, WIDE)
        slab_ref[slabs] = planes.astype(BF16)
        if marks:
            tail = planes[:, :8, SPARE:] + marks[0][...][None]
            slab_ref[slabs, :8, SPARE:] = tail.astype(BF16)
        window = pl.ds(part * count, count)
        moves.append(
            pltpu.make_async_copy(
                slab_ref.at[window],
                out_ref.at[window, pl.ds(first, size)],
                slab_sems.at[part],
            )
        )
        moves[-1].start()
    for move in moves:
        move.wait()


def planes_of(group, v, c, marks=(), through=(), after=(), buffer=(), passing=False):
    slots = GROUPS[group]
    items = len(slots)
    outputs = [c[slot] for slot in slots] if passing else through
    first = group % 2 * items * 2 * X6
    inputs = (
        *v,
        *(c[slot] for slot in slots),
        lane_table(),
        twiddle_table(),
        row_table(items),
        *marks,
        *through,
        *after,
        *buffer,
    )
    outside = len(through) + len(after) + len(buffer)
    return pl.pallas_call(
        functools.partial(
            plane_kernel,
            items=items,
            first=first,
            through=len(through),
            chained=len(after) + len(buffer),
            marked=len(marks),
            passing=passing,
        ),
        out_shape=[
            pltpu.HBM((SLABS, ROWS, WIDE), BF16),
            *(pltpu.HBM(x.shape, x.dtype) for x in outputs),
        ],
        in_specs=[VMEM] * (len(inputs) - outside)
        + [ANY] * (len(through) + len(after))
        + [HBM] * len(buffer),
        out_specs=[HBM] * (1 + len(outputs)),
        input_output_aliases={len(inputs) - 1: 0} if buffer else {},
        scratch_shapes=[
            pltpu.VMEM((2 * items * X6 * Y16, WIDE), BF16),
            pltpu.VMEM((SLABS, items * 2 * X6, WIDE), BF16),
            pltpu.SemaphoreType.DMA((SLAB_CUTS,)),
            pltpu.SemaphoreType.DMA((max(len(outputs), 1),)),
        ],
        compiler_params=pltpu.CompilerParams(vmem_limit_bytes=16 << 20),
        cost_estimate=pl.CostEstimate(
            flops=PLANES_FLOPS[group] * items, bytes_accessed=100_000, transcendentals=0
        ),
        name="planes",
    )(*inputs)


def marks_kernel(cell_ref, out_ref):
    cell = cell_ref[...].astype(F32)
    high = jnp.floor((cell + 0.5) * (1.0 / 256.0))
    row = lax.broadcasted_iota(jnp.int32, (8, 128), 0)
    out_ref[...] = jnp.where(row == 0, high, jnp.where(row == 1, cell - 256.0 * high, 0.0))


def block_marks(cell):
    return pl.pallas_call(
        marks_kernel,
        out_shape=jax.ShapeDtypeStruct((8, 128), F32),
        compiler_params=pltpu.CompilerParams(vmem_limit_bytes=1 << 20),
        cost_estimate=pl.CostEstimate(
            flops=MARKS_FLOPS, bytes_accessed=10_000, transcendentals=0
        ),
        name="marks",
    )(cell[None])


MARKS_FLOPS = 150_000_000


def pick(density_ref, flat_ref, kx_ref, store):
    rows = density_ref.shape[0]

    def body(step, carry):
        lanes = pl.ds(pl.multiple_of(step * TILE, TILE), TILE)
        spot = lax.broadcasted_iota(jnp.int32, (WIDE, TILE), 0)
        chosen = jnp.where(spot == flat_ref[:, lanes], 1.0, 0.0).astype(BF16)
        values = jnp.dot(density_ref[...], chosen, preferred_element_type=F32)
        kx = lax.broadcasted_iota(jnp.int32, (N, TILE), 0) == kx_ref[:, lanes]
        values = jnp.where(kx[None], values.reshape(rows // N, N, TILE), 0.0)
        store(lanes, values.sum(axis=1))
        return carry

    lax.fori_loop(0, G_DEV // TILE, body, 0, unroll=True)


def transform_x(chunk, t_ref, x_refs, low):
    first, place = 0, 0
    for items, x_ref in zip(X_GROUPS[chunk], x_refs):
        size = items * 2 * X6
        planes = t_ref[:, first : first + size, :]
        if size % 16:
            planes = planes.astype(F32)
        planes = planes.reshape(SLABS * size, WIDE).astype(BF16)
        rows = 2 * items * N
        low[place : place + rows, :] = jnp.dot(
            x_ref[...], planes, preferred_element_type=F32
        ).astype(BF16)
        first += size
        place += rows


def first_kernel(
    t_ref, x_ref, own_ref, own_kx_ref, far_ref, far_kx_ref, own_out, far_out, low
):
    transform_x(0, t_ref, (x_ref,) * len(X_GROUPS[0]), low)

    def store_far(lanes, values):
        far_out[:, lanes] = values.astype(BF16)

    def store_own(lanes, values):
        own_out[:, lanes] = values

    pick(low, far_ref, far_kx_ref, store_far)
    pick(low, own_ref, own_kx_ref, store_own)


def second_far_kernel(
    t_ref, x_ref, far_ref, far_kx_ref, first_ref, far_out, low, block_out
):
    transform_x(1, t_ref, (x_ref,) * len(X_GROUPS[1]), low)
    rows = first_ref.shape[0]
    far_out[:rows, :] = first_ref[...]

    def store_far(lanes, values):
        far_out[rows:, lanes] = values.astype(BF16)

    pick(low, far_ref, far_kx_ref, store_far)
    spare = t_ref[:, :16, SPARE:].astype(F32).sum(axis=0)
    spare = spare + pltpu.roll(spare, 128 - NBLOCK, 1)
    block_out[...] = spare


def second_own_kernel(low, own_ref, own_kx_ref, own_out):
    def store_own(lanes, values):
        own_out[:, lanes] = values

    pick(low, own_ref, own_kx_ref, store_own)


FIRST, SECOND = (2 * sum(chunk) for chunk in X_GROUPS)


def first_points(planes, own, far):
    return pl.pallas_call(
        first_kernel,
        out_shape=(
            jax.ShapeDtypeStruct((FIRST, G_DEV), F32),
            jax.ShapeDtypeStruct((FIRST, G_DEV), BF16),
        ),
        scratch_shapes=[pltpu.VMEM((FIRST * N, WIDE), BF16)],
        compiler_params=pltpu.CompilerParams(vmem_limit_bytes=16 << 20),
        cost_estimate=pl.CostEstimate(
            flops=100_000_000, bytes_accessed=100_000, transcendentals=0
        ),
        name="first_points",
    )(planes, x_table(X_GROUPS[0][0]), *own, *far)


def second_far_points(planes, far, first):
    return pl.pallas_call(
        second_far_kernel,
        out_shape=(
            jax.ShapeDtypeStruct((FIRST + SECOND, G_DEV), BF16),
            jax.ShapeDtypeStruct((SECOND * N, WIDE), BF16),
            jax.ShapeDtypeStruct((16, 128), F32),
        ),
        compiler_params=pltpu.CompilerParams(vmem_limit_bytes=16 << 20),
        cost_estimate=pl.CostEstimate(
            flops=100_000_000, bytes_accessed=100_000, transcendentals=0
        ),
        name="second_far_points",
    )(planes, x_table(X_GROUPS[1][0]), *far, first)


def second_own_points(low, own):
    return pl.pallas_call(
        second_own_kernel,
        out_shape=jax.ShapeDtypeStruct((SECOND, G_DEV), F32),
        compiler_params=pltpu.CompilerParams(vmem_limit_bytes=16 << 20),
        cost_estimate=pl.CostEstimate(
            flops=2_400_000_000, bytes_accessed=1_300_000, transcendentals=0
        ),
        name="second_own_points",
    )(low, *own)


def split_kernel(own0_ref, own1_ref, far_ref, block_ref, out_ref):
    parts = [[], [], [], []]
    first, place = 0, 0
    for own_ref, chunk in zip((own0_ref, own1_ref), X_GROUPS):
        first = 0
        for size in chunk:
            own_r = own_ref[first : first + size, :]
            own_i = own_ref[first + size : first + 2 * size, :]
            far_r = far_ref[place : place + size, :].astype(F32)
            far_i = far_ref[place + size : place + 2 * size, :].astype(F32)
            parts[0].append(own_r + far_r)
            parts[1].append(own_i + far_i)
            parts[2].append(own_i - far_i)
            parts[3].append(far_r - own_r)
            first += 2 * size
            place += 2 * size
    pairs = jnp.concatenate(sum(parts, []), axis=0).astype(BF16)
    block = block_ref[...].astype(BF16)
    for band in range(16):
        out_ref[band, :32, :] = pairs[:, band * 128 : (band + 1) * 128]
        out_ref[band, 32:, :] = block


def split_pairs(own0, own1, far, block):
    return pl.pallas_call(
        split_kernel,
        out_shape=jax.ShapeDtypeStruct((16, 48, 128), BF16),
        compiler_params=pltpu.CompilerParams(vmem_limit_bytes=8 << 20),
        cost_estimate=pl.CostEstimate(
            flops=1_000_000, bytes_accessed=500_000, transcendentals=0
        ),
        name="split",
    )(own0, own1, far, block)


def phase_cosine(phase):
    turns = jnp.floor((phase + 0.5) * (1.0 / N))
    rest = phase - N * turns
    angle = (N // 4 - jnp.minimum(rest, N - rest)) * (2.0 * math.pi / N)
    square = angle * angle
    series = -1.0 / 39916800.0
    for factor in (1.0 / 362880.0, -1.0 / 5040.0, 1.0 / 120.0, -1.0 / 6.0, 1.0):
        series = series * square + factor
    return angle * series


def block_kernel(*refs):
    waves_hbm, refs = refs[: 2 + len(SLOTS)], refs[2 + len(SLOTS) :]
    info_ref, marks_hbm, _, out_hbm, *refs = refs
    waves_ref, product_ref, marks_ref, tail_ref, sums_ref, wave_sems, sems = refs
    waves_in = [
        pltpu.make_async_copy(wave, waves_ref.at[i], wave_sems.at[i])
        for i, wave in enumerate(waves_hbm)
    ]
    place = marks_hbm.at[:, pl.ds(0, 8), pl.ds(SPARE, 128)]
    marks_in = pltpu.make_async_copy(place, marks_ref, sems.at[1])
    marks_in.start()
    for move in waves_in:
        move.start()
    tail = (slice(None), pl.ds(0, 16), pl.ds(SPARE, 128))
    fetch = pltpu.make_async_copy(out_hbm.at[tail], tail_ref, sems.at[0])
    fetch.start()
    info = info_ref[...]
    marks_in.wait()
    marks = marks_ref[...].astype(F32).sum(axis=0)
    used = info[3:4] != 0.0
    cell = jnp.where(used, 256.0 * marks[0:1] + marks[1:2], 0.0)
    block_x = jnp.floor((cell + 0.5) * (1.0 / 576.0))
    cell = cell - 576.0 * block_x
    block_y = jnp.floor((cell + 0.5) * (1.0 / N))
    block_z = cell - N * block_y
    block_y = block_y + info[0:1]
    lane = lax.broadcasted_iota(jnp.int32, (Y6 * N, 128), 0).astype(F32)
    y6 = jnp.floor((lane + 0.5) * (1.0 / N))
    lanes = phase_cosine(16.0 * y6 * block_y + (lane - N * y6) * block_z + info[1:2]).astype(BF16)
    rows = X6 * Y16
    row = lax.broadcasted_iota(jnp.int32, (rows, 128), 0).astype(F32)
    x = jnp.floor((row + 0.5) * (1.0 / Y16))
    turned = phase_cosine((x + info[4:5]) * block_x + (row - Y16 * x) * block_y + info[2:3])
    turned = turned * info[3:4]
    for move in waves_in:
        move.wait()
    for half in range(2):
        for item, slot in enumerate(SLOTS):
            index = half * len(SLOTS) + item
            product_ref[index * rows : (index + 1) * rows, :] = (
                waves_ref[half] * waves_ref[2 + slot]
            )
    sums = jnp.dot(product_ref[...], lanes, preferred_element_type=F32)
    sums_ref[...] = (sums.reshape(2 * ITEMS, rows, 128) * turned[None]).sum(axis=1)
    sums = sums_ref[...]
    sums = sums + pltpu.roll(sums, 128 - NBLOCK, 1)
    high = sums.astype(BF16).astype(F32)
    rest = pltpu.roll(sums - high, NBLOCK, 1)
    spot = lax.broadcasted_iota(jnp.int32, sums.shape, 1)
    sums = jnp.where(spot // NBLOCK % 2 == 0, high, rest)
    fetch.wait()
    tails = tail_ref[...].astype(F32)
    tail_ref[...] = jnp.where((spot >= 32) & (spot < 96), sums, tails).astype(BF16)
    store = pltpu.make_async_copy(tail_ref, out_hbm.at[tail], sems.at[2])
    store.start()
    store.wait()


def with_block_sums(v, c, info, arrived, planes):
    waves = [in_hbm(wave) for wave in (*v, *c)]
    inputs = (*waves, info, arrived, planes)
    return pl.pallas_call(
        block_kernel,
        out_shape=pltpu.HBM(planes.shape, planes.dtype),
        in_specs=[HBM] * len(waves) + [VMEM, ANY, HBM],
        out_specs=HBM,
        input_output_aliases={len(inputs) - 1: 0},
        scratch_shapes=[
            pltpu.VMEM((len(waves), X6 * Y16, Y6 * N), BF16),
            pltpu.VMEM((2 * ITEMS * X6 * Y16, Y6 * N), BF16),
            pltpu.VMEM((SLABS, 8, 128), BF16),
            pltpu.VMEM((SLABS, 16, 128), BF16),
            pltpu.VMEM((2 * ITEMS, 128), F32),
            pltpu.SemaphoreType.DMA((len(waves),)),
            pltpu.SemaphoreType.DMA((3,)),
        ],
        compiler_params=pltpu.CompilerParams(vmem_limit_bytes=10 << 20),
        cost_estimate=pl.CostEstimate(
            flops=10_000_000, bytes_accessed=100_000, transcendentals=0
        ),
        name="block",
    )(*inputs)


def sum_kernel(pairs_ref, weight_ref, column_ref, out_ref):
    pairs = 16 * 16
    block = pairs_ref[:, 32:, :].reshape(pairs, 128)
    total = None
    for part in range(2):
        left = pairs_ref[:, 16 * part : 16 * (part + 1), :].reshape(pairs, 128)
        columns = jnp.dot(block, column_ref[part], preferred_element_type=F32)
        right = (columns * weight_ref[...]).astype(BF16)
        term = lax.dot_general(
            left, right, (((0,), (0,)), ((), ())), preferred_element_type=F32
        )
        total = term if total is None else total + term
    out_ref[...] = total


def wave_rows(wave):
    return wave.reshape(X6, Y6, Y16, N).transpose(0, 2, 1, 3).reshape(X6 * Y16, Y6 * N)


def per_device(
    valence_wave,
    conduction_wave,
    valence_index,
    occupied_energy,
    conduction_energy,
    frequency,
    gvec_cell,
    block_cell,
):
    col = lax.axis_index(COL)
    wave_v = wave_rows(valence_wave)
    wave_c = wave_rows(conduction_wave)
    ahead = [(i, (i + 1) % 8) for i in range(8)]
    behind = [(i, (i + 7) % 8) for i in range(8)]
    v = [wave_v, lax.ppermute(wave_v, "yl", [(0, 1), (1, 0)])]
    c = [wave_c] + [None] * 7
    for slot in (1, 2, 3, 4):
        c[slot] = lax.ppermute(c[slot - 1], "z", ahead)
        if slot < 4:
            c[8 - slot] = lax.ppermute(c[(9 - slot) % 8], "z", behind)

    mirror_of = [(k, SLABS - 1 - k) for k in range(SLABS)]
    far_cell = lax.ppermute(gvec_cell, COL, mirror_of).reshape(16, 128)
    spots = jnp.arange(128, dtype=jnp.int32)
    marks = block_marks(jnp.where((spots % NBLOCK == col) & (spots >= 32), block_cell[0], 0))
    (planes0,) = planes_of(0, v, c, marks=(marks,))
    planes0, far_cell = planes_of(1, v, c, through=(far_cell,), buffer=(planes0,))
    sent0 = lax.all_to_all(planes0, COL, 0, 0, tiled=True)
    (planes1,) = planes_of(2, v, c)
    last = GROUPS[3]
    planes1, *passed = planes_of(3, v, c, buffer=(planes1,), passing=True)
    for slot, wave in zip(last, passed):
        c[slot] = wave

    group = np.arange(128) // NBLOCK - 2
    used = (group >= 0) & (group < 4)
    info = np.zeros((8, 128), np.float32)
    info[0] = np.arange(128) % NBLOCK * 6
    info[1] = np.where(group % 2 == 1, N // 4, 0)
    info[2] = np.where(group == 1, 3 * N // 4, np.where(group == 2, N // 4, 0))
    info[3] = np.where(used, 1.0 / (N * math.sqrt(N)), 0.0)
    info = info + jnp.where(np.arange(8)[:, None] == 4, (X6 * col).astype(F32), 0.0)
    planes1 = with_block_sums(v, c, info, sent0, planes1)
    sent1 = lax.all_to_all(planes1, COL, 0, 0, tiled=True)

    far_cell = far_cell.reshape(G_DEV)
    far_x, far_y, far_z = far_cell // 576, far_cell // N % 6, far_cell % N
    own = ((gvec_cell % 576)[None], (gvec_cell // 576)[None])
    far = (((6 - far_y) * N + (N - far_z) % N)[None], ((N - far_x) % N)[None])

    pair_v, pair_c = pair_table()
    occupied = jnp.arange(occupied_energy.shape[0], dtype=jnp.int32)
    valence_energy = jnp.sum(
        jnp.where(valence_index[:, None] == occupied[None, :], occupied_energy[None, :], 0.0),
        axis=1,
    )
    count_v, count_c = valence_index.shape[0], conduction_energy.shape[0]
    energy_v = jnp.sum(
        jnp.where(pair_v[:, None] == np.arange(count_v)[None], valence_energy[None], 0.0), axis=1
    )
    energy_c = jnp.sum(
        jnp.where(pair_c[:, None] == np.arange(count_c)[None], conduction_energy[None], 0.0),
        axis=1,
    )
    gap = (energy_c - energy_v)[:, None]
    omega = jnp.repeat(frequency, 2 * NBLOCK)[None]
    weight = -4.0 * gap / (gap * gap + omega * omega) * (1.0 / math.sqrt(count_v * count_c))

    own0, far0 = first_points(sent0, own, far)
    mirrored, low, columns = second_far_points(sent1, far, far0)
    mirrored = lax.ppermute(mirrored, COL, mirror_of)
    own1 = second_own_points(low, own)
    pairs = split_pairs(own0, own1, mirrored, columns)
    pairs = lax.all_to_all(pairs, BAND, 0, 0, tiled=True)
    return pl.pallas_call(
        sum_kernel,
        out_shape=jax.ShapeDtypeStruct((128, 128), F32),
        compiler_params=pltpu.CompilerParams(vmem_limit_bytes=4 << 20),
        name="pair_sum",
    )(pairs, weight, column_tables())


def solution(mesh):
    fine = Mesh(
        mesh.devices.reshape(8, 2, 4, 2, 2), ("z", "yl", "x", "yh", "co")
    )
    return jax.shard_map(
        per_device,
        mesh=fine,
        in_specs=(
            P(BAND, COL, None),
            P(BAND, COL, None),
            P(),
            P(),
            P(),
            P(),
            P(COL),
            P(COL),
        ),
        out_specs=P(COL + BAND, None),
        check_vma=False,
    )
```
